32 devices in a mesh: table: 8 (over z, y), batch: 4 (over x, core).
Axes of the slice: x: 2, y: 2, z: 4, core: 2. Of those that a mesh axis runs over, the one named last changes fastest.
Arguments:
- tokens: bfloat16 [96, 512, 768], P(('table', 'batch')), may hold values from -6 to 6
- row_blocks: int32 [96], P(('table', 'batch')), may hold values from 8 to 64, as said below
- block_fill: int32 [96, 64], P(('table', 'batch')), may hold values from 4 to 8
- row_table: int32 [96], P('table'), may hold values from 0 to 3
- class_count: int32 [32], P(('table', 'batch')), may hold values from 2 to 128, as said below
- merge_w: bfloat16 [768, 768], P(('table', 'batch')), may hold values from -0.21875 to 0.21875
- qkv_w: bfloat16 [768, 2304], P(('table', 'batch')), may hold values from -0.21875 to 0.21875
- query_bias: bfloat16 [768], P(('table', 'batch')), may hold values from -3 to 3
- value_bias: bfloat16 [768], P(('table', 'batch')), may hold values from -3 to 3
- out_w: bfloat16 [768, 768], P(('table', 'batch')), may hold values from -2.5 to 2.5
- out_bias: bfloat16 [768], P(('table', 'batch')), may hold values from -3 to 3
- gain_one: bfloat16 [768], P(('table', 'batch')), may hold values from 0.5 to 1.5
- shift_one: bfloat16 [768], P(('table', 'batch')), may hold values from -3 to 3
- up_w: bfloat16 [768, 3072], P(('table', 'batch')), may hold values from -0.21875 to 0.21875
- up_bias: bfloat16 [3072], P(('table', 'batch')), may hold values from -3 to 3
- down_w: bfloat16 [3072, 768], P(('table', 'batch')), may hold values from -0.109375 to 0.109375
- down_bias: bfloat16 [768], P(('table', 'batch')), may hold values from -3 to 3
- gain_two: bfloat16 [768], P(('table', 'batch')), may hold values from 0.5 to 1.5
- shift_two: bfloat16 [768], P(('table', 'batch')), may hold values from -3 to 3
- head_w: bfloat16 [32, 768, 128], P(('table', 'batch')), may hold values from -0.21875 to 0.21875
- cotangent: bfloat16 [96, 512, 768], P(('table', 'batch')), may hold values from -6 to 6
- logit_cotangent: float32 [96, 128], P(('table', 'batch')), may hold values from -6 to 6
Outputs:
- layer_out: bfloat16 [96, 512, 768], P(('table', 'batch'))
- logits: float32 [96, 128], P(('table', 'batch'))
- grad_input: bfloat16 [96, 512, 768], P(('table', 'batch'))
- grad_merge_w: float32 [768, 768], P(('table', 'batch'))
- grad_qkv_w: float32 [768, 2304], P(('table', 'batch'))
- grad_query_bias: float32 [768], P(('table', 'batch'))
- grad_value_bias: float32 [768], P(('table', 'batch'))
- grad_out_w: float32 [768, 768], P(('table', 'batch'))
- grad_out_bias: float32 [768], P(('table', 'batch'))
- grad_gain_one: float32 [768], P(('table', 'batch'))
- grad_shift_one: float32 [768], P(('table', 'batch'))
- grad_up_w: float32 [768, 3072], P(('table', 'batch'))
- grad_up_bias: float32 [3072], P(('table', 'batch'))
- grad_down_w: float32 [3072, 768], P(('table', 'batch'))
- grad_down_bias: float32 [768], P(('table', 'batch'))
- grad_gain_two: float32 [768], P(('table', 'batch'))
- grad_shift_two: float32 [768], P(('table', 'batch'))
- grad_head_w: float32 [32, 768, 128], P(('table', 'batch'))
- root_squares: float32 [5], replicated
The draws below stay inside these ranges and needn't reach their ends.
Inputs may be any that keep to these rules, and one draw needn't show every extreme that they name: A row's live positions lie in its first row_blocks word groups; some row has 64 and some 8. Head of a row is its table group's index times the batch axis's size plus row_table. `class_count`: some table has 128 classes and some 2.
All inputs are finite; a program needn't handle non-finite values.
Results may differ from the reference program's by a relative error of at most 0.018.
The reference program's roundings to bfloat16 on the way count: a program that leaves them out, or rounds other values in their place, can miss the bound.
Values may be sent and summed in bfloat16 or wider, within the bound.
A program may use at most 256 MiB of HBM per device.

```python
import jax
import jax.numpy as jnp
from jax import lax

D = 768
HEADS = 12
FF = 3072
HEAD_DIM = 64
BLOCK = 8
L = 512
BLOCKS = 64
MIN_BLOCKS = 8
ROWS_DEV = 3
CLASSES = 128
ROWS = 96
TABLES = 32
N_TABLE = 8
N_BATCH = 4


def draw_row_blocks(key, part):
    drawn = jax.random.randint(key, (ROWS,), MIN_BLOCKS, BLOCKS + 1)
    drawn = drawn.at[0].set(BLOCKS)
    return drawn.at[1].set(MIN_BLOCKS).astype(jnp.int32)


def draw_class_count(key, part):
    drawn = jax.random.randint(key, (TABLES,), 2, CLASSES + 1)
    drawn = drawn.at[0].set(CLASSES)
    return drawn.at[1].set(2).astype(jnp.int32)


def touch_ends(array, stream_key, least, top_value):
    longest = array.shape.index(max(array.shape))
    spots = []
    for shift in (0, 1):
        where = [jax.random.randint(jax.random.fold_in(stream_key, axis), (), 0, length) for axis, length in enumerate(array.shape)]
        where[longest] = (where[longest] + shift) % array.shape[longest]
        spots.append(tuple(where))
    return array.at[spots[0]].set(least).at[spots[1]].set(top_value)


def level_of(stream_key, shape, pieces, low, largest):
    def one(dim, shards_of):
        heights = jax.random.uniform(jax.random.fold_in(jax.random.fold_in(stream_key, 6), dim), (shards_of,), jnp.float32, low / len(pieces), largest / len(pieces))
        return jnp.repeat(jnp.exp(heights), shape[dim] // shards_of).reshape((-1,) + (1,) * (len(shape) - dim - 1))

    loudness = one(*pieces[0])
    for cut in pieces[1:]:
        loudness = loudness * one(*cut)
    return loudness


def normal_values(key, extent, deviation, limit, pieces=(), kind=jnp.bfloat16):
    entries = deviation * jax.random.normal(key, extent, jnp.float32)
    if pieces:
        entries = entries * level_of(key, extent, pieces, -0.22, 0.18)
    return jnp.clip(entries, -limit, limit).astype(kind)


def setup_inputs(seed: int = 0) -> dict:
    arg_keys = jax.random.split(jax.random.key(seed), 23)
    return {
        "tokens": normal_values(arg_keys[0], (ROWS, L, D), 1.0, 6.0, ((0, 32),)),
        "row_blocks": draw_row_blocks(jax.random.fold_in(arg_keys[22], 71), 0),
        "block_fill": touch_ends(jax.random.randint(arg_keys[2], (ROWS, BLOCKS), 4, BLOCK + 1), jax.random.fold_in(arg_keys[2], 1), 4, BLOCK).astype(jnp.int32),
        "row_table": touch_ends(jax.random.randint(arg_keys[3], (ROWS,), 0, N_BATCH), jax.random.fold_in(arg_keys[3], 1), 0, N_BATCH - 1).astype(jnp.int32),
        "class_count": draw_class_count(jax.random.fold_in(arg_keys[22], 71), 0),
        "merge_w": normal_values(arg_keys[5], (D, D), D ** -0.5, 0.21875, ((0, 32),)),
        "qkv_w": normal_values(arg_keys[6], (D, 3 * D), D ** -0.5, 0.21875, ((0, 32),)),
        "query_bias": normal_values(arg_keys[7], (D,), 0.3, 3.0, ((0, 32),)),
        "value_bias": normal_values(arg_keys[8], (D,), 0.3, 3.0, ((0, 32),)),
        "out_w": normal_values(arg_keys[9], (D, D), (D * 4 // L) ** -0.5, 2.5, ((0, 32),)),
        "out_bias": normal_values(arg_keys[10], (D,), 0.3, 3.0, ((0, 32),)),
        "gain_one": jnp.clip(1.0 + 0.1 * jax.random.normal(arg_keys[11], (D,), jnp.float32), 0.5, 1.5).astype(jnp.bfloat16),
        "shift_one": normal_values(arg_keys[12], (D,), 0.3, 3.0, ((0, 32),)),
        "up_w": normal_values(arg_keys[13], (D, FF), D ** -0.5, 0.21875, ((0, 32),)),
        "up_bias": normal_values(arg_keys[14], (FF,), 0.3, 3.0, ((0, 32),)),
        "down_w": normal_values(arg_keys[15], (FF, D), FF ** -0.5, 0.109375, ((0, 32),)),
        "down_bias": normal_values(arg_keys[16], (D,), 0.3, 3.0, ((0, 32),)),
        "gain_two": jnp.clip(1.0 + 0.1 * jax.random.normal(arg_keys[17], (D,), jnp.float32), 0.5, 1.5).astype(jnp.bfloat16),
        "shift_two": normal_values(arg_keys[18], (D,), 0.3, 3.0, ((0, 32),)),
        "head_w": normal_values(arg_keys[19], (TABLES, D, CLASSES), D ** -0.5, 0.21875, ((0, 32),)),
        "cotangent": normal_values(arg_keys[20], (ROWS, L, D), 1.0, 6.0, ((0, 32),)),
        "logit_cotangent": normal_values(arg_keys[21], (ROWS, CLASSES), 1.0, 6.0, ((0, 32),), jnp.float32),
    }


@jax.custom_vjp
def low(v):
    return lax.optimization_barrier(v.astype(jnp.bfloat16)).astype(jnp.float32)

@jax.custom_vjp
def low_back(v):
    return v

def low_keep(v):
    return (low(v), None)

def low_pass(kept, grad):
    return (grad,)

def back_keep(v):
    return (v, None)

def back_low(kept, grad):
    return (low(grad),)
low.defvjp(low_keep, low_pass)
low_back.defvjp(back_keep, back_low)
PRECISE = lax.Precision.HIGHEST
NORM_EPS = 1e-05
MASKED = -1000000000.0

def valid_tokens(row_blocks, block_fill):
    position = jnp.arange(L, dtype=jnp.int32)
    fill_tok = jnp.repeat(block_fill, BLOCK, axis=1)
    live_mask = ((position // BLOCK)[None, :] < row_blocks[:, None]) & ((position % BLOCK)[None, :] < fill_tok)
    return live_mask.astype(jnp.float32)

def matmul(left, right):
    return jnp.dot(left, right, precision=PRECISE, preferred_element_type=jnp.float32)

def layer_norm(hidden, norm_gain, norm_shift):
    average = lax.optimization_barrier(jnp.mean(hidden, axis=-1, keepdims=True))
    centered = hidden - average
    variance = lax.optimization_barrier(jnp.mean(centered * centered, axis=-1, keepdims=True))
    return centered * lax.rsqrt(variance + NORM_EPS) * norm_gain + norm_shift

def forward(weights, tokens, live_mask, head_rows, class_mask):
    merge_w, qkv_w, query_bias, value_bias, out_w, out_bias, gain_one, shift_one, up_w, up_bias, down_w, down_bias, gain_two, shift_two, head_w = weights
    count_rows = tokens.shape[0]
    tok_flat = tokens.reshape(-1, D)
    live_flat = live_mask.reshape(-1, 1)
    blocks_x = tokens.reshape(count_rows, BLOCKS, BLOCK, D)
    live_blk = live_mask.reshape(count_rows, BLOCKS, 1, BLOCK)
    merge_query = low(low_back(matmul(tok_flat, merge_w))).reshape(count_rows, BLOCKS, BLOCK, D)
    merge_scores = low_back(jnp.einsum('rbid,rbjd->rbij', merge_query, blocks_x, precision=PRECISE) * D ** (-0.5))
    merge_scores = jnp.where(live_blk > 0, merge_scores, MASKED)
    merge_probs = low(jax.nn.softmax(merge_scores, axis=-1))
    merged_out = low_back(jnp.einsum('rbij,rbjd->rbid', merge_probs, blocks_x, precision=PRECISE)).reshape(-1, D) * live_flat
    hidden_one = tok_flat + merged_out
    attn_in = low(hidden_one)
    qkv_bias = jnp.concatenate([query_bias, jnp.zeros((D,), jnp.float32), value_bias])
    packed_qkv = low(low_back(matmul(attn_in, qkv_w) + qkv_bias)).reshape(count_rows, L, 3, HEADS, HEAD_DIM)
    queries = packed_qkv[:, :, 0]
    keys_all = packed_qkv[:, :, 1]
    values = packed_qkv[:, :, 2]
    scores = low_back(jnp.einsum('rqhe,rkhe->rhqk', queries, keys_all, precision=PRECISE) * HEAD_DIM ** (-0.5))
    scores = jnp.where(live_mask[:, None, None, :] > 0, scores, MASKED)
    attn_probs = low(jax.nn.softmax(scores, axis=-1))
    context = low(low_back(jnp.einsum('rhqk,rkhe->rqhe', attn_probs, values, precision=PRECISE))).reshape(-1, D)
    attn_branch = low_back(matmul(context, out_w) + out_bias)
    norm_one = layer_norm(hidden_one + attn_branch, gain_one, shift_one)
    ffn_in = low(norm_one)
    up_pre = low_back(matmul(ffn_in, up_w) + up_bias)
    activated = low(jax.nn.gelu(up_pre, approximate=False))
    down_branch = low_back(matmul(activated, down_w) + down_bias)
    result = low(layer_norm(norm_one + down_branch, gain_two, shift_two) * live_flat)
    cls_rows = result.reshape(count_rows, L, D)[:, 0, :]
    logits = jnp.einsum('rd,rdc->rc', cls_rows, head_w[head_rows], precision=PRECISE) * class_mask
    square_sums = jnp.stack([jnp.sum(live_flat * field * field) for field in (tok_flat, merged_out, attn_branch, down_branch, result)])
    return ((result.reshape(count_rows, L, D), logits), (square_sums, jnp.sum(live_mask)))

def reference(tokens, row_blocks, block_fill, row_table, class_count, merge_w, qkv_w, query_bias, value_bias, out_w, out_bias, gain_one, shift_one, up_w, up_bias, down_w, down_bias, gain_two, shift_two, head_w, cotangent, logit_cotangent):
    weights = tuple((weight.astype(jnp.float32) for weight in (merge_w, qkv_w, query_bias, value_bias, out_w, out_bias, gain_one, shift_one, up_w, up_bias, down_w, down_bias, gain_two, shift_two, head_w)))
    steps_count = N_TABLE * N_BATCH
    live_all = valid_tokens(row_blocks, block_fill)
    row_index = jnp.arange(ROWS, dtype=jnp.int32)
    head_rows = row_index // (ROWS_DEV * N_BATCH) * N_BATCH + row_table
    class_mask = (jnp.arange(CLASSES, dtype=jnp.int32)[None, :] < class_count[head_rows][:, None]).astype(jnp.float32)
    spans = (tokens.astype(jnp.float32).reshape(steps_count, ROWS_DEV, L, D), live_all.reshape(steps_count, ROWS_DEV, L), head_rows.reshape(steps_count, ROWS_DEV), class_mask.reshape(steps_count, ROWS_DEV, CLASSES), cotangent.astype(jnp.float32).reshape(steps_count, ROWS_DEV, L, D), logit_cotangent.reshape(steps_count, ROWS_DEV, CLASSES))

    def step(carry, span):
        grads_acc, sums_acc, count_acc = carry
        tok_span, live_span, rows_span, mask_span, grad_span, dlog_span = span

        def run(all_weights, tok_in):
            return forward(all_weights, tok_in, live_span, rows_span, mask_span)
        outputs, pull_back, aux_out = jax.vjp(run, weights, tok_span, has_aux=True)
        grad_weights, grad_tok = pull_back((grad_span, dlog_span))
        grads_new = jax.tree.map(lambda running, adding: running + adding, grads_acc, grad_weights)
        return ((grads_new, sums_acc + aux_out[0], count_acc + aux_out[1]), (outputs[0], outputs[1], grad_tok))
    init = (jax.tree.map(jnp.zeros_like, weights), jnp.zeros((5,), jnp.float32), jnp.zeros((), jnp.float32))
    (grads, square_sums, live_count), (result, logits, grad_tok) = lax.scan(step, init, spans)
    root_squares = jnp.sqrt(square_sums / (live_count * D))
    return (result.reshape(ROWS, L, D).astype(jnp.bfloat16), logits.reshape(ROWS, CLASSES), grad_tok.reshape(ROWS, L, D).astype(jnp.bfloat16), grads[0], grads[1], grads[2], grads[3], grads[4], grads[5], grads[6], grads[7], grads[8], grads[9], grads[10], grads[11], grads[12], grads[13], grads[14], root_squares)
```

```python
import functools

import jax
import jax.numpy as jnp
from jax import lax
from jax.experimental import pallas as pl
from jax.experimental.pallas import tpu as pltpu
from jax.sharding import PartitionSpec as P

HEADS = 12
BLOCK = 8
NORM_EPS = 1e-05
MASKED = -1000000000.0
FAR = -3e38
PRECISE = lax.Precision.HIGHEST
TILE = 256
VMEM_BYTES = 64_000_000
BOTH = ("table", "batch")
F32 = jnp.float32
BF16 = jnp.bfloat16


def mm(left, right):
    return jnp.dot(left, right, preferred_element_type=F32)


def mm_t(left, right):
    return lax.dot_general(left, right, (((1,), (1,)), ((), ())), preferred_element_type=F32)


def t_mm(left, right):
    return lax.dot_general(left, right, (((0,), (0,)), ((), ())), preferred_element_type=F32)


def rowsum(values):
    return jnp.sum(values, axis=0, keepdims=True)


def norm_forward(hidden, gain, shift):
    average = jnp.mean(hidden, axis=-1, keepdims=True)
    centered = hidden - average
    variance = jnp.mean(centered * centered, axis=-1, keepdims=True)
    inv_std = lax.rsqrt(variance + NORM_EPS)
    standard = centered * inv_std
    return standard * gain + shift, standard, inv_std


def norm_backward(grad_norm, standard, inv_std, gain):
    scaled = grad_norm * gain
    return inv_std * (
        scaled
        - jnp.mean(scaled, axis=-1, keepdims=True)
        - standard * jnp.mean(scaled * standard, axis=-1, keepdims=True)
    )


def group_probs(query, tok, live_row, scale):
    size = tok.shape[0]
    row = lax.broadcasted_iota(jnp.int32, (size, size), 0) // BLOCK
    col = lax.broadcasted_iota(jnp.int32, (size, size), 1) // BLOCK
    scores = jnp.where(live_row > 0, mm_t(query, tok) * scale, MASKED)
    scores = jnp.where(row == col, scores, FAR)
    terms = jnp.exp(scores - jnp.max(scores, axis=-1, keepdims=True))
    return terms / jnp.sum(terms, axis=-1, keepdims=True), row == col


def merge_kernel(tok, live_row, live_col, merge_w, qkv_w, qkv_bias, query_out, hidden_out, attn_out, packed_out, squares):
    step = pl.program_id(0)
    scale = tok.shape[1] ** -0.5
    x = tok[...]
    live = live_col[...]
    query = mm(x, merge_w[...]).astype(BF16)
    query_out[...] = query
    probs, _ = group_probs(query, x, live_row[0], scale)
    merged = mm(probs.astype(BF16), x) * live
    wide = x.astype(F32)
    hidden = wide + merged
    hidden_out[...] = hidden
    attn_in = hidden.astype(BF16)
    attn_out[...] = attn_in
    packed_out[...] = (mm(attn_in, qkv_w[...]) + qkv_bias[...]).astype(BF16)

    @pl.when(step == 0)
    def _():
        squares[...] = jnp.zeros_like(squares)

    squares[0:1, :] += rowsum(live * wide * wide)
    squares[1:2, :] += rowsum(merged * merged)


def lane_mask(values, low, high):
    lane = lax.broadcasted_iota(jnp.int32, values.shape, 1)
    return jnp.where((lane >= low) & (lane < high), values, jnp.zeros_like(values))


def attn_kernel(scale, q_ref, k_ref, v_ref, bias_ref, ctx_ref, lse_ref):
    seq, lanes = q_ref.shape[1:]
    head = lanes // 2
    q = q_ref[0] * jnp.asarray(scale, BF16)
    k = k_ref[0]
    v_t = v_ref[0].T
    bias = bias_ref[0]
    for c in range(seq // TILE):
        rows = slice(c * TILE, (c + 1) * TILE)
        parts = []
        for h in range(2):
            scores = mm_t(k, lane_mask(q[rows], h * head, (h + 1) * head)) + bias
            top = jnp.max(scores, axis=0, keepdims=True)
            terms = jnp.exp(scores - top)
            total = jnp.sum(terms, axis=0, keepdims=True)
            probs = (terms * (1.0 / total)).astype(BF16)
            lse_ref[0, 0, h : h + 1, rows] = top + jnp.log(total)
            parts.append(mm(v_t[h * head : (h + 1) * head], probs))
        ctx_ref[0, rows, :] = jnp.concatenate(parts, axis=0).T.astype(BF16)


def attn_back_kernel(scale, q_ref, k_ref, v_ref, bias_ref, lse_ref, grad_ref, dq_ref, dk_ref, dv_ref):
    seq, lanes = q_ref.shape[1:]
    head = lanes // 2
    q = q_ref[0] * jnp.asarray(scale, BF16)
    k = k_ref[0]
    v = v_ref[0]
    k_t = k.T
    bias = bias_ref[0]
    grad_k = jnp.zeros((seq, lanes), F32)
    grad_v = jnp.zeros((seq, lanes), F32)
    for c in range(seq // TILE):
        rows = slice(c * TILE, (c + 1) * TILE)
        parts = []
        for h in range(2):
            q_part = lane_mask(q[rows], h * head, (h + 1) * head)
            g_part = lane_mask(grad_ref[0, rows, :], h * head, (h + 1) * head)
            scores = mm_t(k, q_part) + bias
            probs = jnp.exp(scores - lse_ref[0, 0, h : h + 1, rows])
            grad_v += mm(probs.astype(BF16), g_part)
            grad_p = mm_t(v, g_part)
            grad_s = (probs * (grad_p - jnp.sum(probs * grad_p, axis=0, keepdims=True))).astype(BF16)
            grad_k += mm(grad_s, q_part)
            parts.append(mm(k_t[h * head : (h + 1) * head], grad_s))
        dq_ref[0, rows, :] = (jnp.concatenate(parts, axis=0).T * scale).astype(BF16)
    dk_ref[0] = grad_k.astype(BF16)
    dv_ref[0] = grad_v.astype(BF16)


def ffn_kernel(
    per_row,
    ctx,
    hidden,
    cot,
    cls_grad,
    live_col,
    out_w,
    up_w,
    down_w,
    vecs,
    layer_out,
    activated,
    grad_up,
    ffn_in_out,
    grad_down_out,
    grad_attn_out,
    grad_two_out,
    grad_ctx_out,
    sums,
    up_sums,
    slope,
):
    step = pl.program_id(0)
    width = hidden.shape[1]
    chunks = up_w.shape[1] // width

    @pl.when(step == 0)
    def _():
        sums[...] = jnp.zeros_like(sums)
        up_sums[...] = jnp.zeros_like(up_sums)

    live = live_col[...]
    out_bias, gain_one, shift_one, down_bias, gain_two, shift_two = (vecs[i : i + 1, :width] for i in range(6))
    branch = mm(ctx[...], out_w[...]) + out_bias
    norm_one, standard_one, inv_one = norm_forward(hidden[...] + branch, gain_one, shift_one)
    ffn_in = norm_one.astype(BF16)
    ffn_in_out[...] = ffn_in
    down = jnp.zeros_like(norm_one)
    for j in range(chunks):
        cols = slice(j * width, (j + 1) * width)
        pre = mm(ffn_in, up_w[:, cols]) + vecs[6:7, cols]
        cumulative = 0.5 * (1.0 + lax.erf(pre * 0.7071067811865476))
        act = (pre * cumulative).astype(BF16)
        slope[:, cols] = cumulative + pre * (jnp.exp(-0.5 * pre * pre) * 0.3989422804014327)
        activated[:, cols] = act
        down += mm(act, down_w[cols, :])
    down += down_bias
    normed, standard_two, inv_two = norm_forward(norm_one + down, gain_two, shift_two)
    result = (normed * live).astype(BF16)
    layer_out[...] = result
    wide = result.astype(F32)
    sums[5:6, :] += rowsum(live * branch * branch)
    sums[6:7, :] += rowsum(live * down * down)
    sums[7:8, :] += rowsum(wide * wide)
    first = (lax.broadcasted_iota(jnp.int32, (hidden.shape[0], 1), 0) == 0) & (step % per_row == 0)
    grad = live * (cot[...].astype(F32) + jnp.where(first, cls_grad[0], 0.0))
    sums[0:1, :] += rowsum(grad * standard_two)
    sums[1:2, :] += rowsum(grad)
    grad_three = norm_backward(grad, standard_two, inv_two, gain_two)
    grad_down = grad_three.astype(BF16)
    grad_down_out[...] = grad_down
    sums[2:3, :] += rowsum(grad_down.astype(F32))
    total = grad_three
    for j in range(chunks):
        cols = slice(j * width, (j + 1) * width)
        piece = (mm_t(grad_down, down_w[cols, :]) * slope[:, cols]).astype(BF16)
        grad_up[:, cols] = piece
        up_sums[0:1, cols] += rowsum(piece.astype(F32))
        total += mm_t(piece, up_w[:, cols])
    sums[3:4, :] += rowsum(total * standard_one)
    sums[4:5, :] += rowsum(total)
    grad_two = norm_backward(total, standard_one, inv_one, gain_one)
    grad_two_out[...] = grad_two
    grad_attn = grad_two.astype(BF16)
    grad_attn_out[...] = grad_attn
    sums[8:9, :] += rowsum(grad_attn.astype(F32))
    grad_ctx_out[...] = mm_t(grad_attn, out_w[...]).astype(BF16)


def input_kernel(
    dq, dk, dv, grad_two, tok, query, live_row, live_col, merge_w, qkv_w, grad_input, grad_query_out, packed_out, sums
):
    step = pl.program_id(0)
    width = tok.shape[1]
    scale = width**-0.5

    @pl.when(step == 0)
    def _():
        sums[...] = jnp.zeros_like(sums)

    x = tok[...]
    grad_q, grad_v = dq[...], dv[...]
    grad_one = grad_two[...]
    for i, piece in enumerate((grad_q, dk[...], grad_v)):
        cols = slice(i * width, (i + 1) * width)
        packed_out[:, cols] = piece
        grad_one += mm_t(piece, qkv_w[:, cols])
    sums[0:1, :] += rowsum(grad_q.astype(F32))
    sums[1:2, :] += rowsum(grad_v.astype(F32))
    grad_merged = (grad_one * live_col[...]).astype(BF16)
    mq = query[...]
    probs, same = group_probs(mq, x, live_row[0], scale)
    grad_probs = mm_t(grad_merged, x)
    grad_scores = probs * (grad_probs - jnp.sum(probs * grad_probs, axis=-1, keepdims=True))
    grad_scores = jnp.where(same & (live_row[0] > 0), grad_scores, 0.0)
    grad_query = (mm(grad_scores.astype(BF16), x) * scale).astype(BF16)
    grad_query_out[...] = grad_query
    blocks = mm(probs.T.astype(BF16), grad_merged) + mm(grad_scores.T.astype(BF16), mq) * scale
    blocks += mm_t(grad_query, merge_w[...])
    grad_input[...] = (grad_one + blocks).astype(BF16)


def params(**kw):
    return pltpu.CompilerParams(vmem_limit_bytes=VMEM_BYTES, **kw)


def fixed(shape):
    zeros = (0,) * len(shape)
    return pl.BlockSpec(shape, lambda *_: zeros, pipeline_mode=pl.Buffered(1))


def tiled(size, width):
    return pl.BlockSpec((size, width), lambda i: (i, 0))


def body(
    tokens,
    row_blocks,
    block_fill,
    row_table,
    class_count,
    merge_w,
    qkv_w,
    query_bias,
    value_bias,
    out_w,
    out_bias,
    gain_one,
    shift_one,
    up_w,
    up_bias,
    down_w,
    down_bias,
    gain_two,
    shift_two,
    head_w,
    cotangent,
    logit_cotangent,
):
    rows, seq, width = tokens.shape
    count = rows * seq
    ff = up_w.shape[1]
    head = width // HEADS
    per_row = seq // TILE
    tiles = count // TILE
    share = merge_w.shape[0]
    devices = width // share
    wide_ff = ff // width

    def cut(mat, n):
        return [mat[:, i * width : (i + 1) * width] for i in range(n)]

    vec_list = (out_bias, gain_one, shift_one, down_bias, gain_two, shift_two, query_bias, value_bias)
    vec_row = jnp.concatenate([*vec_list, up_bias])
    used = vec_row.shape[0]
    vec_row = jnp.pad(vec_row, (0, 8 * width - used)).reshape(8, width)
    mine = jnp.concatenate([merge_w, out_w, *cut(qkv_w, 3), *cut(up_w, wide_ff), down_w, vec_row], axis=0)
    gathered = lax.all_gather(mine, BOTH, axis=0)

    def unit(start, n):
        part = gathered[:, start : start + n * share]
        part = part.reshape(devices, n, share, width).transpose(0, 2, 1, 3)
        return part.reshape(width, n * width)

    merge_full = unit(0, 1)
    out_full = unit(share, 1)
    qkv_full = unit(2 * share, 3)
    up_full = unit(5 * share, wide_ff)
    base = (5 + wide_ff) * share
    down_full = gathered[:, base : base + wide_ff * share].reshape(ff, width)
    vec_rows = gathered[:, base + wide_ff * share].astype(F32)
    vectors = [vec_rows[:, i * share : (i + 1) * share].reshape(1, width) for i in range(8)]
    up_bias_full = vec_rows[:, 8 * share : 8 * share + wide_ff * share].reshape(1, ff)
    query_vec, value_vec = vectors[6], vectors[7]
    qkv_bias = jnp.concatenate([query_vec, jnp.zeros_like(query_vec), value_vec], axis=1)
    vecs = jnp.concatenate(
        [jnp.pad(jnp.concatenate(vectors[:6], axis=0), ((0, 0), (0, ff - width))), up_bias_full, jnp.zeros((1, ff), F32)],
        axis=0,
    )

    position = jnp.arange(seq, dtype=jnp.int32)
    fill_tok = jnp.repeat(block_fill, BLOCK, axis=1)
    live = ((position // BLOCK)[None, :] < row_blocks[:, None]) & ((position % BLOCK)[None, :] < fill_tok)
    live_mask = live.astype(F32)
    live_col = live_mask.reshape(count, 1)
    live_row = live_mask.reshape(tiles, 1, TILE)
    key_bias = jnp.where(live, 0.0, MASKED).astype(F32).reshape(rows, seq, 1)

    batch = lax.axis_size("batch")
    group_rows = rows * batch
    heads = lax.all_gather(head_w[0], "batch", axis=0)
    counts = lax.all_gather(class_count, "batch", axis=0, tiled=True)
    group_dlog_raw = lax.all_gather(logit_cotangent, "batch", axis=0, tiled=True)
    classes = head_w.shape[2]
    own = lax.axis_index("batch")
    my_table = lax.dynamic_slice(row_table, (own * rows,), (rows,))
    class_ids = jnp.arange(classes, dtype=jnp.int32)
    my_select = (my_table[:, None] == jnp.arange(batch, dtype=jnp.int32)[None, :]).astype(F32)
    my_class = (class_ids[None, :] < (my_select * counts[None, :].astype(F32)).sum(1, keepdims=True)).astype(F32)
    my_dlog = logit_cotangent * my_class
    picked = (my_select[:, :, None] * my_dlog[:, None, :]).transpose(1, 0, 2)
    cls_grad = jnp.sum(
        lax.dot_general(picked, heads.astype(F32), (((2,), (2,)), ((0,), (0,))), precision=PRECISE), axis=0
    )

    tok_flat = tokens.reshape(count, width)
    cot_flat = cotangent.reshape(count, width)
    merge_query, hidden, attn_in, packed, squares = pl.pallas_call(
        merge_kernel,
        grid=(tiles,),
        in_specs=[
            tiled(TILE, width),
            pl.BlockSpec((1, 1, TILE), lambda i: (i, 0, 0)),
            tiled(TILE, 1),
            fixed((width, width)),
            fixed((width, 3 * width)),
            fixed((1, 3 * width)),
        ],
        out_specs=[
            tiled(TILE, width),
            tiled(TILE, width),
            tiled(TILE, width),
            tiled(TILE, 3 * width),
            fixed((8, width)),
        ],
        out_shape=[
            jax.ShapeDtypeStruct((count, width), BF16),
            jax.ShapeDtypeStruct((count, width), F32),
            jax.ShapeDtypeStruct((count, width), BF16),
            jax.ShapeDtypeStruct((count, 3 * width), BF16),
            jax.ShapeDtypeStruct((8, width), F32),
        ],
        compiler_params=params(),
        name="merge_qkv",
    )(tok_flat, live_row, live_col, merge_full, qkv_full, qkv_bias)

    packed_rows = packed.reshape(rows, seq, 3 * width)
    pairs = HEADS // 2
    lanes = 2 * head

    def head_block(offset):
        return pl.BlockSpec((1, seq, lanes), lambda r, p: (r, 0, p + offset))

    bias_block = pl.BlockSpec((1, seq, 1), lambda r, p: (r, 0, 0))
    lse_block = pl.BlockSpec((1, 1, 2, seq), lambda r, p: (r, p, 0, 0))
    context, lse = pl.pallas_call(
        functools.partial(attn_kernel, head**-0.5),
        grid=(rows, pairs),
        in_specs=[head_block(0), head_block(pairs), head_block(2 * pairs), bias_block],
        out_specs=[head_block(0), lse_block],
        out_shape=[
            jax.ShapeDtypeStruct((rows, seq, width), BF16),
            jax.ShapeDtypeStruct((rows, pairs, 2, seq), F32),
        ],
        compiler_params=params(),
        name="attention",
    )(packed_rows, packed_rows, packed_rows, key_bias)

    context = context.reshape(count, width)
    (layer_out, activated, grad_up, ffn_in, grad_down, grad_attn, grad_two, grad_ctx, sums, up_sums) = pl.pallas_call(
        functools.partial(ffn_kernel, per_row),
        grid=(tiles,),
        in_specs=[
            tiled(TILE, width),
            tiled(TILE, width),
            tiled(TILE, width),
            pl.BlockSpec((1, 1, width), lambda i: (i // per_row, 0, 0)),
            tiled(TILE, 1),
            fixed((width, width)),
            fixed((width, ff)),
            fixed((ff, width)),
            fixed((8, ff)),
        ],
        out_specs=[
            tiled(TILE, width),
            tiled(TILE, ff),
            tiled(TILE, ff),
            tiled(TILE, width),
            tiled(TILE, width),
            tiled(TILE, width),
            tiled(TILE, width),
            tiled(TILE, width),
            fixed((16, width)),
            fixed((8, ff)),
        ],
        out_shape=[
            jax.ShapeDtypeStruct((count, width), BF16),
            jax.ShapeDtypeStruct((count, ff), BF16),
            jax.ShapeDtypeStruct((count, ff), BF16),
            jax.ShapeDtypeStruct((count, width), BF16),
            jax.ShapeDtypeStruct((count, width), BF16),
            jax.ShapeDtypeStruct((count, width), BF16),
            jax.ShapeDtypeStruct((count, width), F32),
            jax.ShapeDtypeStruct((count, width), BF16),
            jax.ShapeDtypeStruct((16, width), F32),
            jax.ShapeDtypeStruct((8, ff), F32),
        ],
        scratch_shapes=[pltpu.VMEM((TILE, ff), F32)],
        compiler_params=params(),
        name="ffn",
    )(context, hidden, cot_flat, cls_grad.reshape(rows, 1, width), live_col, out_full, up_full, down_full, vecs)

    grad_rows = grad_ctx.reshape(rows, seq, width)
    grad_q, grad_k, grad_v = pl.pallas_call(
        functools.partial(attn_back_kernel, head**-0.5),
        grid=(rows, pairs),
        in_specs=[head_block(0), head_block(pairs), head_block(2 * pairs), bias_block, lse_block, head_block(0)],
        out_specs=[head_block(0)] * 3,
        out_shape=[jax.ShapeDtypeStruct((rows, seq, width), BF16)] * 3,
        compiler_params=params(),
        name="attention_back",
    )(packed_rows, packed_rows, packed_rows, key_bias, lse, grad_rows)

    grad_input, grad_query, grad_packed, bias_sums = pl.pallas_call(
        input_kernel,
        grid=(tiles,),
        in_specs=[
            tiled(TILE, width),
            tiled(TILE, width),
            tiled(TILE, width),
            tiled(TILE, width),
            tiled(TILE, width),
            tiled(TILE, width),
            pl.BlockSpec((1, 1, TILE), lambda i: (i, 0, 0)),
            tiled(TILE, 1),
            fixed((width, width)),
            fixed((width, 3 * width)),
        ],
        out_specs=[tiled(TILE, width), tiled(TILE, width), tiled(TILE, 3 * width), fixed((8, width))],
        out_shape=[
            jax.ShapeDtypeStruct((count, width), BF16),
            jax.ShapeDtypeStruct((count, width), BF16),
            jax.ShapeDtypeStruct((count, 3 * width), BF16),
            jax.ShapeDtypeStruct((8, width), F32),
        ],
        compiler_params=params(),
        name="merge_back",
    )(
        grad_q.reshape(count, width),
        grad_k.reshape(count, width),
        grad_v.reshape(count, width),
        grad_two,
        tok_flat,
        merge_query,
        live_row,
        live_col,
        merge_full,
        qkv_full,
    )

    grad_merge_w = t_mm(tok_flat, grad_query).astype(BF16)
    grad_qkv_w = t_mm(attn_in, grad_packed).astype(BF16)
    grad_out_w = t_mm(context, grad_attn).astype(BF16)
    grad_up_w = t_mm(ffn_in, grad_up).astype(BF16)
    grad_down_w = t_mm(activated, grad_down).astype(BF16)

    def owners(mat, n):
        return mat.reshape(devices, share, n, width).transpose(0, 2, 1, 3).reshape(devices, n * share, width)

    vec_grads = (sums[8], sums[3], sums[4], sums[2], sums[0], sums[1], bias_sums[0], bias_sums[1])
    vec_block = jnp.concatenate(
        [v.reshape(devices, share) for v in vec_grads] + [up_sums[0].reshape(devices, wide_ff * share)], axis=1
    )
    vec_block = jnp.pad(vec_block, ((0, 0), (0, 8 * width - used))).astype(BF16).reshape(devices, 8, width)
    all_grads = jnp.concatenate(
        [
            owners(grad_merge_w, 1),
            owners(grad_out_w, 1),
            owners(grad_qkv_w, 3),
            owners(grad_up_w, wide_ff),
            grad_down_w.reshape(devices, wide_ff * share, width),
            vec_block,
        ],
        axis=1,
    )
    owned = lax.psum_scatter(all_grads, BOTH, scatter_dimension=0, tiled=True)[0].astype(F32)

    def joined(start, n):
        return jnp.concatenate([owned[start + i * share : start + (i + 1) * share] for i in range(n)], axis=1)

    own_vec = owned[base + wide_ff * share]
    own_vecs = [own_vec[i * share : (i + 1) * share] for i in range(8)]
    own_up_bias = own_vec[8 * share : 8 * share + wide_ff * share]

    layer_rows = layer_out.reshape(rows, seq, width)
    cls_rows = layer_rows[:, 0, :]
    my_logits = jnp.sum(
        my_select[:, :, None] * jnp.einsum("rd,kdc->rkc", cls_rows, heads, preferred_element_type=F32), axis=1
    )
    logits = my_logits * my_class
    group_cls = lax.all_gather(cls_rows, "batch", axis=0, tiled=True)
    owner_mask = (row_table == own).astype(F32)[:, None]
    class_live = (class_ids < class_count[0]).astype(F32)[None, :]
    group_dlog = group_dlog_raw * (owner_mask * class_live)
    grad_head = lax.dot_general(
        group_cls.astype(F32), group_dlog, (((0,), (0,)), ((), ())), precision=PRECISE, preferred_element_type=F32
    )[None]
    partial = jnp.stack(
        [
            jnp.sum(squares[0]),
            jnp.sum(squares[1]),
            jnp.sum(sums[5]),
            jnp.sum(sums[6]),
            jnp.sum(sums[7]),
            jnp.sum(live_mask),
        ]
    )
    totals = lax.psum(partial, BOTH)
    root_squares = jnp.sqrt(totals[:5] / (totals[5] * width))
    return (
        layer_rows,
        logits,
        grad_input.reshape(rows, seq, width),
        joined(0, 1),
        joined(2 * share, 3),
        own_vecs[6],
        own_vecs[7],
        joined(share, 1),
        own_vecs[0],
        own_vecs[1],
        own_vecs[2],
        joined(5 * share, wide_ff),
        own_up_bias,
        owned[base : base + wide_ff * share],
        own_vecs[3],
        own_vecs[4],
        own_vecs[5],
        grad_head,
        root_squares,
    )


def solution(mesh):
    three = P(BOTH, None, None)
    two = P(BOTH, None)
    one = P(BOTH)
    placed = (
        three, one, two, P("table"), one, two, two, one, one, two, one, one, one, two, one, two, one, one, one, three,
        three, two,
    )
    results = (
        three, two, three, two, two, one, one, two, one, one, one, two, one, two, one, one, one, three, P(),
    )
    return jax.shard_map(body, mesh=mesh, in_specs=placed, out_specs=results, check_vma=False)
```

```python
import functools

import jax
import jax.numpy as jnp
from jax import lax
from jax.experimental import pallas as pl
from jax.experimental.pallas import tpu as pltpu
from jax.sharding import PartitionSpec as P

HEADS = 12
BLOCK = 8
NORM_EPS = 1e-05
MASKED = -1000000000.0
FAR = -3e38
PRECISE = lax.Precision.HIGHEST
TILE = 256
VMEM_BYTES = 64_000_000
BOTH = ("table", "batch")
F32 = jnp.float32
BF16 = jnp.bfloat16


def mm(left, right):
    return jnp.dot(left, right, preferred_element_type=F32)


def mm_t(left, right):
    return lax.dot_general(left, right, (((1,), (1,)), ((), ())), preferred_element_type=F32)


def t_mm(left, right):
    return lax.dot_general(left, right, (((0,), (0,)), ((), ())), preferred_element_type=F32)


def rowsum(values):
    return jnp.sum(values, axis=0, keepdims=True)


def norm_forward(hidden, gain, shift):
    average = jnp.mean(hidden, axis=-1, keepdims=True)
    centered = hidden - average
    variance = jnp.mean(centered * centered, axis=-1, keepdims=True)
    inv_std = lax.rsqrt(variance + NORM_EPS)
    standard = centered * inv_std
    return standard * gain + shift, standard, inv_std


def norm_backward(grad_norm, standard, inv_std, gain):
    scaled = grad_norm * gain
    return inv_std * (
        scaled
        - jnp.mean(scaled, axis=-1, keepdims=True)
        - standard * jnp.mean(scaled * standard, axis=-1, keepdims=True)
    )


def group_probs(query, tok, live_row, scale):
    size = tok.shape[0]
    row = lax.broadcasted_iota(jnp.int32, (size, size), 0) // BLOCK
    col = lax.broadcasted_iota(jnp.int32, (size, size), 1) // BLOCK
    scores = jnp.where(live_row > 0, mm_t(query, tok) * scale, MASKED)
    scores = jnp.where(row == col, scores, FAR)
    terms = jnp.exp(scores - jnp.max(scores, axis=-1, keepdims=True))
    return terms / jnp.sum(terms, axis=-1, keepdims=True), row == col


def merge_kernel(tok, live_row, live_col, merge_w, qkv_w, qkv_bias, query_out, hidden_out, attn_out, packed_out, squares):
    step = pl.program_id(0)
    scale = tok.shape[1] ** -0.5
    x = tok[...]
    live = live_col[...]
    query = mm(x, merge_w[...]).astype(BF16)
    query_out[...] = query
    probs, _ = group_probs(query, x, live_row[0], scale)
    merged = mm(probs.astype(BF16), x) * live
    wide = x.astype(F32)
    hidden = wide + merged
    hidden_out[...] = hidden
    attn_in = hidden.astype(BF16)
    attn_out[...] = attn_in
    packed_out[...] = (mm(attn_in, qkv_w[...]) + qkv_bias[...]).astype(BF16)

    @pl.when(step == 0)
    def _():
        squares[...] = jnp.zeros_like(squares)

    squares[0:1, :] += rowsum(live * wide * wide)
    squares[1:2, :] += rowsum(merged * merged)


def lane_mask(values, low, high):
    lane = lax.broadcasted_iota(jnp.int32, values.shape, 1)
    return jnp.where((lane >= low) & (lane < high), values, jnp.zeros_like(values))


def attn_kernel(scale, q_ref, k_ref, v_ref, bias_ref, ctx_ref, lse_ref):
    seq, lanes = q_ref.shape[1:]
    head = lanes // 2
    q = q_ref[0] * jnp.asarray(scale, BF16)
    k = k_ref[0]
    v_t = v_ref[0].T
    bias = bias_ref[0]
    for c in range(seq // TILE):
        rows = slice(c * TILE, (c + 1) * TILE)
        parts = []
        for h in range(2):
            scores = mm_t(k, lane_mask(q[rows], h * head, (h + 1) * head)) + bias
            top = jnp.max(scores, axis=0, keepdims=True)
            terms = jnp.exp(scores - top)
            total = jnp.sum(terms, axis=0, keepdims=True)
            probs = (terms * (1.0 / total)).astype(BF16)
            lse_ref[0, 0, h : h + 1, rows] = top + jnp.log(total)
            parts.append(mm(v_t[h * head : (h + 1) * head], probs))
        ctx_ref[0, rows, :] = jnp.concatenate(parts, axis=0).T.astype(BF16)


def attn_back_kernel(scale, q_ref, k_ref, v_ref, bias_ref, lse_ref, grad_ref, dq_ref, dk_ref, dv_ref):
    seq, lanes = q_ref.shape[1:]
    head = lanes // 2
    q = q_ref[0] * jnp.asarray(scale, BF16)
    k = k_ref[0]
    v = v_ref[0]
    k_t = k.T
    bias = bias_ref[0]
    grad_k = jnp.zeros((seq, lanes), F32)
    grad_v = jnp.zeros((seq, lanes), F32)
    for c in range(seq // TILE):
        rows = slice(c * TILE, (c + 1) * TILE)
        parts = []
        for h in range(2):
            q_part = lane_mask(q[rows], h * head, (h + 1) * head)
            g_part = lane_mask(grad_ref[0, rows, :], h * head, (h + 1) * head)
            scores = mm_t(k, q_part) + bias
            probs = jnp.exp(scores - lse_ref[0, 0, h : h + 1, rows])
            grad_v += mm(probs.astype(BF16), g_part)
            grad_p = mm_t(v, g_part)
            grad_s = (probs * (grad_p - jnp.sum(probs * grad_p, axis=0, keepdims=True))).astype(BF16)
            grad_k += mm(grad_s, q_part)
            parts.append(mm(k_t[h * head : (h + 1) * head], grad_s))
        dq_ref[0, rows, :] = (jnp.concatenate(parts, axis=0).T * scale).astype(BF16)
    dk_ref[0] = grad_k.astype(BF16)
    dv_ref[0] = grad_v.astype(BF16)


def ffn_kernel(
    per_row,
    ctx,
    hidden,
    cot,
    cls_grad,
    live_col,
    out_w,
    up_w,
    down_w,
    vecs,
    layer_out,
    activated,
    grad_up,
    ffn_in_out,
    grad_down_out,
    grad_attn_out,
    grad_two_out,
    grad_ctx_out,
    sums,
    up_sums,
    slope,
):
    step = pl.program_id(0)
    width = hidden.shape[1]
    chunks = up_w.shape[1] // width

    @pl.when(step == 0)
    def _():
        sums[...] = jnp.zeros_like(sums)
        up_sums[...] = jnp.zeros_like(up_sums)

    live = live_col[...]
    out_bias, gain_one, shift_one, down_bias, gain_two, shift_two = (vecs[i : i + 1, :width] for i in range(6))
    branch = mm(ctx[...], out_w[...]) + out_bias
    norm_one, standard_one, inv_one = norm_forward(hidden[...] + branch, gain_one, shift_one)
    ffn_in = norm_one.astype(BF16)
    ffn_in_out[...] = ffn_in
    down = jnp.zeros_like(norm_one)
    for j in range(chunks):
        cols = slice(j * width, (j + 1) * width)
        pre = mm(ffn_in, up_w[:, cols]) + vecs[6:7, cols]
        cumulative = 0.5 * (1.0 + lax.erf(pre * 0.7071067811865476))
        act = (pre * cumulative).astype(BF16)
        slope[:, cols] = cumulative + pre * (jnp.exp(-0.5 * pre * pre) * 0.3989422804014327)
        activated[:, cols] = act
        down += mm(act, down_w[cols, :])
    down += down_bias
    normed, standard_two, inv_two = norm_forward(norm_one + down, gain_two, shift_two)
    result = (normed * live).astype(BF16)
    layer_out[...] = result
    wide = result.astype(F32)
    sums[5:6, :] += rowsum(live * branch * branch)
    sums[6:7, :] += rowsum(live * down * down)
    sums[7:8, :] += rowsum(wide * wide)
    first = (lax.broadcasted_iota(jnp.int32, (hidden.shape[0], 1), 0) == 0) & (step % per_row == 0)
    grad = live * (cot[...].astype(F32) + jnp.where(first, cls_grad[0], 0.0))
    sums[0:1, :] += rowsum(grad * standard_two)
    sums[1:2, :] += rowsum(grad)
    grad_three = norm_backward(grad, standard_two, inv_two, gain_two)
    grad_down = grad_three.astype(BF16)
    grad_down_out[...] = grad_down
    sums[2:3, :] += rowsum(grad_down.astype(F32))
    total = grad_three
    for j in range(chunks):
        cols = slice(j * width, (j + 1) * width)
        piece = (mm_t(grad_down, down_w[cols, :]) * slope[:, cols]).astype(BF16)
        grad_up[:, cols] = piece
        up_sums[0:1, cols] += rowsum(piece.astype(F32))
        total += mm_t(piece, up_w[:, cols])
    sums[3:4, :] += rowsum(total * standard_one)
    sums[4:5, :] += rowsum(total)
    grad_two = norm_backward(total, standard_one, inv_one, gain_one)
    grad_two_out[...] = grad_two
    grad_attn = grad_two.astype(BF16)
    grad_attn_out[...] = grad_attn
    sums[8:9, :] += rowsum(grad_attn.astype(F32))
    grad_ctx_out[...] = mm_t(grad_attn, out_w[...]).astype(BF16)


def input_kernel(
    dq, dk, dv, grad_two, tok, query, live_row, live_col, merge_w, qkv_w, grad_input, grad_query_out, packed_out, sums
):
    step = pl.program_id(0)
    width = tok.shape[1]
    scale = width**-0.5

    @pl.when(step == 0)
    def _():
        sums[...] = jnp.zeros_like(sums)

    x = tok[...]
    grad_q, grad_v = dq[...], dv[...]
    grad_one = grad_two[...]
    for i, piece in enumerate((grad_q, dk[...], grad_v)):
        cols = slice(i * width, (i + 1) * width)
        packed_out[:, cols] = piece
        grad_one += mm_t(piece, qkv_w[:, cols])
    sums[0:1, :] += rowsum(grad_q.astype(F32))
    sums[1:2, :] += rowsum(grad_v.astype(F32))
    grad_merged = (grad_one * live_col[...]).astype(BF16)
    mq = query[...]
    probs, same = group_probs(mq, x, live_row[0], scale)
    grad_probs = mm_t(grad_merged, x)
    grad_scores = probs * (grad_probs - jnp.sum(probs * grad_probs, axis=-1, keepdims=True))
    grad_scores = jnp.where(same & (live_row[0] > 0), grad_scores, 0.0)
    grad_query = (mm(grad_scores.astype(BF16), x) * scale).astype(BF16)
    grad_query_out[...] = grad_query
    blocks = mm(probs.T.astype(BF16), grad_merged) + mm(grad_scores.T.astype(BF16), mq) * scale
    blocks += mm_t(grad_query, merge_w[...])
    grad_input[...] = (grad_one + blocks).astype(BF16)


def params(**kw):
    return pltpu.CompilerParams(vmem_limit_bytes=VMEM_BYTES, **kw)


def fixed(shape):
    zeros = (0,) * len(shape)
    return pl.BlockSpec(shape, lambda *_: zeros, pipeline_mode=pl.Buffered(1))


def tiled(size, width):
    return pl.BlockSpec((size, width), lambda i: (i, 0))


MESH = pl.DeviceIdType.MESH
TABLE_MAJOR = 4
CORES = 2


def here(dims):
    table, batch = lax.axis_index("table"), lax.axis_index("batch")
    return [table // dims[1], lax.rem(table, dims[1]), batch // CORES, lax.rem(batch, CORES)]


def peer(dims, spot, axis, offset):
    other = list(spot)
    other[axis] = lax.rem(spot[axis] + offset, dims[axis])
    return (other[0] * dims[1] + other[1], other[2] * CORES + other[3]), other[axis]


def greet(dims, spot):
    barrier = pltpu.get_barrier_semaphore()
    total = 0
    for axis in range(4):
        for offset in range(1, dims[axis]):
            target, _ = peer(dims, spot, axis, offset)
            pl.semaphore_signal(barrier, inc=1, device_id=target, device_id_type=MESH)
            total += 1
    pl.semaphore_wait(barrier, total)


def gather_kernel(dims, orders, *refs):
    count = len(orders)
    shards, fulls = refs[:count], refs[count : 2 * count]
    local_sem, send_sem, recv_sem = refs[2 * count :]
    spot = here(dims)
    greet(dims, spot)
    sent = {}

    def start(item, stage):
        axis = orders[item][stage]
        done = orders[item][:stage]
        where = tuple(slice(None) if a in done else spot[a] for a in range(4))
        source = fulls[item].at[where] if stage else shards[item]
        for offset in range(1, dims[axis]):
            copy = pltpu.make_async_remote_copy(
                src_ref=source,
                dst_ref=fulls[item].at[where],
                send_sem=send_sem.at[item, stage, offset],
                recv_sem=recv_sem.at[item, stage, offset],
                device_id=peer(dims, spot, axis, offset)[0],
                device_id_type=MESH,
            )
            copy.start()
            sent[item, stage, offset] = copy

    def finish(item, stage):
        for offset in range(1, dims[orders[item][stage]]):
            sent[item, stage, offset].wait_recv()

    kept = []
    for item in range(count):
        copy = pltpu.make_async_copy(shards[item], fulls[item].at[tuple(spot)], local_sem.at[item])
        copy.start()
        kept.append(copy)
        start(item, 0)
    pairs = (count + 1) // 2
    for slot in range(pairs + 3):
        for stage in (3, 2, 1, 0):
            pair = slot - stage
            for item in range(2 * pair, min(2 * pair + 2, count)) if 0 <= pair < pairs else ():
                finish(item, stage)
                if stage == 0:
                    kept[item].wait()
                if stage < 3:
                    start(item, stage + 1)
    for copy in sent.values():
        copy.wait_send()


def scatter_kernel(dims, items, arrays, *refs):
    count = len(items)
    grads, square, outs, total_out = refs[:arrays], refs[arrays], refs[arrays + 1 : 2 * arrays + 1], refs[2 * arrays + 1]
    refs = refs[2 * arrays + 2 :]
    buffers = [refs[i * 7 : (i + 1) * 7] for i in range(count)]
    square_sum, square_got, local_sem, send_sem, recv_sem = refs[7 * count :]
    spot = here(dims)
    greet(dims, spot)
    sent = {}

    def send(key, index, source, landing, axis, offset):
        copy = pltpu.make_async_remote_copy(
            src_ref=source,
            dst_ref=landing,
            send_sem=send_sem.at[index],
            recv_sem=recv_sem.at[index],
            device_id=peer(dims, spot, axis, offset)[0],
            device_id_type=MESH,
        )
        copy.start()
        sent.setdefault(key, []).append(copy)

    def slot_of(item, stage, offset):
        return item, stage, offset

    def square_start(stage):
        axis = 3 - stage
        for offset in range(1, dims[axis]):
            send(("square", stage), (count, stage, offset), square_sum.at[stage], square_got.at[stage, offset - 1], axis, offset)

    def square_finish(stage):
        for copy in sent["square", stage]:
            copy.wait_recv()
        value = square_sum[stage]
        for offset in range(1, dims[3 - stage]):
            value = value + square_got[stage, offset - 1]
        square_sum[stage + 1] = value

    def start(item, stage):
        array, low, size, order = items[item]
        own, first, second, got_core, got_first, got_second, got_last = buffers[item]
        axis = order[stage]
        for offset in range(1, dims[axis]):
            _, other = peer(dims, spot, axis, offset)
            index = slot_of(item, stage, offset)
            if stage == 0:
                source, landing = grads[array].at[:, :, :, other, :, pl.ds(low, size)], got_core
            elif stage == 1:
                source = own.at[:, :, other] if axis == 2 else own.at[:, other]
                landing = got_first.at[offset - 1]
            elif stage == 2:
                source, landing = first.at[:, other], got_second.at[offset - 1]
            else:
                source, landing = second.at[other], got_last.at[offset - 1]
            send((item, stage), index, source, landing, axis, offset)

    def finish(item, stage):
        array, low, size, order = items[item]
        own, first, second, got_core, got_first, got_second, got_last = buffers[item]
        axis = order[stage]
        others = range(dims[axis] - 1)
        mine = spot[axis]
        for copy in sent[item, stage]:
            copy.wait_recv()
        if stage == 0:
            loads[item].wait()

            @pl.loop(0, dims[0] * dims[1] * dims[2])
            def _(i):
                at = (i // (dims[1] * dims[2]), lax.rem(i // dims[2], dims[1]), lax.rem(i, dims[2]))
                own[at] = (own[at].astype(F32) + got_core[at].astype(F32)).astype(BF16)
        elif stage == 1:
            inner = first.shape[1]

            @pl.loop(0, dims[0] * inner)
            def _(i):
                at = (i // inner, lax.rem(i, inner))
                value = own[(*at, mine) if axis == 2 else (at[0], mine, at[1])].astype(F32)
                for k in others:
                    value += got_first[(k, *at)].astype(F32)
                first[at] = value.astype(BF16)
        elif stage == 2:

            @pl.loop(0, dims[0])
            def _(i):
                value = first[i, mine].astype(F32)
                for k in others:
                    value += got_second[k, i].astype(F32)
                second[i] = value.astype(BF16)
        else:
            value = second[mine].astype(F32)
            for k in others:
                value += got_last[k].astype(F32)
            outs[array][:, low : low + size] = value

    square_sum[0] = square[...]
    loads = []
    for item, (array, low, size, _) in enumerate(items):
        copy = pltpu.make_async_copy(
            grads[array].at[:, :, :, spot[3], :, pl.ds(low, size)], buffers[item][0], local_sem.at[item]
        )
        copy.start()
        loads.append(copy)
        start(item, 0)
    square_start(0)
    pairs = (count + 1) // 2
    for slot in range(pairs + 3):
        for stage in (3, 2, 1, 0):
            pair = slot - stage
            for item in range(2 * pair, min(2 * pair + 2, count)) if 0 <= pair < pairs else ():
                finish(item, stage)
                if stage < 3:
                    start(item, stage + 1)
        if slot < 4:
            square_finish(slot)
            if slot < 3:
                square_start(slot + 1)
    total_out[...] = square_sum[4]
    for group in sent.values():
        for copy in group:
            copy.wait_send()


def gather_all(dims, shards, orders):
    anywhere = pl.BlockSpec(memory_space=pl.ANY)
    most = max(dims)
    count = len(shards)
    return pl.pallas_call(
        functools.partial(gather_kernel, dims, orders),
        in_specs=[pl.BlockSpec(memory_space=pltpu.VMEM)] * count,
        out_specs=[anywhere] * count,
        out_shape=[jax.ShapeDtypeStruct((*dims, *a.shape), a.dtype) for a in shards],
        scratch_shapes=[
            pltpu.SemaphoreType.DMA((count,)),
            pltpu.SemaphoreType.DMA((count, 4, most)),
            pltpu.SemaphoreType.DMA((count, 4, most)),
        ],
        compiler_params=params(collective_id=0, has_side_effects=True),
        name="gather_weights",
    )(*shards)


def scatter_all(dims, grads, square, items):
    most = max(dims)
    count = len(items)
    scratch = []
    for array, _, size, order in items:
        tail = (grads[array].shape[4], size)
        inner = dims[order[2]]
        for shape in (
            dims[:3],
            (dims[0], inner),
            (dims[0],),
            dims[:3],
            (dims[order[1]] - 1, dims[0], inner),
            (inner - 1, dims[0]),
            (dims[0] - 1,),
        ):
            scratch.append(pltpu.VMEM((*shape, *tail), BF16))
    vmem = pl.BlockSpec(memory_space=pltpu.VMEM)
    scratch += [
        pltpu.VMEM((5, *square.shape), F32),
        pltpu.VMEM((4, most - 1, *square.shape), F32),
        pltpu.SemaphoreType.DMA((count,)),
        pltpu.SemaphoreType.DMA((count + 1, 4, most)),
        pltpu.SemaphoreType.DMA((count + 1, 4, most)),
    ]
    return pl.pallas_call(
        functools.partial(scatter_kernel, dims, items, len(grads)),
        in_specs=[pl.BlockSpec(memory_space=pl.ANY)] * len(grads) + [vmem],
        out_specs=[vmem] * (len(grads) + 1),
        out_shape=[jax.ShapeDtypeStruct(g.shape[4:], F32) for g in grads] + [jax.ShapeDtypeStruct(square.shape, F32)],
        scratch_shapes=scratch,
        compiler_params=params(collective_id=1, has_side_effects=True),
        name="scatter_grads",
    )(*grads, square)


def body(
    tokens,
    row_blocks,
    block_fill,
    row_table,
    class_count,
    merge_w,
    qkv_w,
    query_bias,
    value_bias,
    out_w,
    out_bias,
    gain_one,
    shift_one,
    up_w,
    up_bias,
    down_w,
    down_bias,
    gain_two,
    shift_two,
    head_w,
    cotangent,
    logit_cotangent,
):
    rows, seq, width = tokens.shape
    count = rows * seq
    ff = up_w.shape[1]
    head = width // HEADS
    per_row = seq // TILE
    tiles = count // TILE
    share = merge_w.shape[0]
    devices = width // share
    wide_ff = ff // width

    def cut(mat, n):
        return [mat[:, i * width : (i + 1) * width] for i in range(n)]

    table_size, batch_size = lax.axis_size("table"), lax.axis_size("batch")
    dims = (TABLE_MAJOR, table_size // TABLE_MAJOR, batch_size // CORES, CORES)
    direct = share % BLOCK == 0
    vec_list = (out_bias, gain_one, shift_one, down_bias, gain_two, shift_two, query_bias, value_bias)
    vec_row = jnp.concatenate([*vec_list, up_bias])
    used = vec_row.shape[0]
    vec_row = jnp.pad(vec_row, (0, 8 * width - used)).reshape(8, width)
    base = (5 + wide_ff) * share
    if direct:
        y_first, x_first = (0, 1, 2, 3), (0, 2, 1, 3)
        qkv_full, down_full, merge_full, up_full, out_full, vec_full = gather_all(
            dims,
            (qkv_w, down_w, merge_w, up_w, out_w, vec_row),
            (y_first, x_first, y_first, y_first, x_first, x_first),
        )
        qkv_full = qkv_full.reshape(width, 3 * width)
        down_full = down_full.reshape(ff, width)
        merge_full = merge_full.reshape(width, width)
        up_full = up_full.reshape(width, ff)
        out_full = out_full.reshape(width, width)
        vec_rows = vec_full.reshape(devices, 8, width)[:, 0].astype(F32)
    else:
        mine = jnp.concatenate([merge_w, out_w, *cut(qkv_w, 3), *cut(up_w, wide_ff), down_w, vec_row], axis=0)
        gathered = lax.all_gather(mine, BOTH, axis=0)

        def unit(start, n):
            part = gathered[:, start : start + n * share]
            part = part.reshape(devices, n, share, width).transpose(0, 2, 1, 3)
            return part.reshape(width, n * width)

        merge_full = unit(0, 1)
        out_full = unit(share, 1)
        qkv_full = unit(2 * share, 3)
        up_full = unit(5 * share, wide_ff)
        down_full = gathered[:, base : base + wide_ff * share].reshape(ff, width)
        vec_rows = gathered[:, base + wide_ff * share].astype(F32)
    vectors = [vec_rows[:, i * share : (i + 1) * share].reshape(1, width) for i in range(8)]
    up_bias_full = vec_rows[:, 8 * share : 8 * share + wide_ff * share].reshape(1, ff)
    query_vec, value_vec = vectors[6], vectors[7]
    qkv_bias = jnp.concatenate([query_vec, jnp.zeros_like(query_vec), value_vec], axis=1)
    vecs = jnp.concatenate(
        [jnp.pad(jnp.concatenate(vectors[:6], axis=0), ((0, 0), (0, ff - width))), up_bias_full, jnp.zeros((1, ff), F32)],
        axis=0,
    )

    position = jnp.arange(seq, dtype=jnp.int32)
    fill_tok = jnp.repeat(block_fill, BLOCK, axis=1)
    live = ((position // BLOCK)[None, :] < row_blocks[:, None]) & ((position % BLOCK)[None, :] < fill_tok)
    live_mask = live.astype(F32)
    live_col = live_mask.reshape(count, 1)
    live_row = live_mask.reshape(tiles, 1, TILE)
    key_bias = jnp.where(live, 0.0, MASKED).astype(F32).reshape(rows, seq, 1)

    batch = lax.axis_size("batch")
    group_rows = rows * batch
    heads = lax.all_gather(head_w[0], "batch", axis=0)
    counts = lax.all_gather(class_count, "batch", axis=0, tiled=True)
    group_dlog_raw = lax.all_gather(logit_cotangent, "batch", axis=0, tiled=True)
    classes = head_w.shape[2]
    own = lax.axis_index("batch")
    my_table = lax.dynamic_slice(row_table, (own * rows,), (rows,))
    class_ids = jnp.arange(classes, dtype=jnp.int32)
    my_select = (my_table[:, None] == jnp.arange(batch, dtype=jnp.int32)[None, :]).astype(F32)
    my_class = (class_ids[None, :] < (my_select * counts[None, :].astype(F32)).sum(1, keepdims=True)).astype(F32)
    my_dlog = logit_cotangent * my_class
    picked = (my_select[:, :, None] * my_dlog[:, None, :]).transpose(1, 0, 2)
    cls_grad = jnp.sum(
        lax.dot_general(picked, heads.astype(F32), (((2,), (2,)), ((0,), (0,))), precision=PRECISE), axis=0
    )

    tok_flat = tokens.reshape(count, width)
    cot_flat = cotangent.reshape(count, width)
    merge_query, hidden, attn_in, packed, squares = pl.pallas_call(
        merge_kernel,
        grid=(tiles,),
        in_specs=[
            tiled(TILE, width),
            pl.BlockSpec((1, 1, TILE), lambda i: (i, 0, 0)),
            tiled(TILE, 1),
            fixed((width, width)),
            fixed((width, 3 * width)),
            fixed((1, 3 * width)),
        ],
        out_specs=[
            tiled(TILE, width),
            tiled(TILE, width),
            tiled(TILE, width),
            tiled(TILE, 3 * width),
            fixed((8, width)),
        ],
        out_shape=[
            jax.ShapeDtypeStruct((count, width), BF16),
            jax.ShapeDtypeStruct((count, width), F32),
            jax.ShapeDtypeStruct((count, width), BF16),
            jax.ShapeDtypeStruct((count, 3 * width), BF16),
            jax.ShapeDtypeStruct((8, width), F32),
        ],
        compiler_params=params(),
        name="merge_qkv",
    )(tok_flat, live_row, live_col, merge_full, qkv_full, qkv_bias)

    packed_rows = packed.reshape(rows, seq, 3 * width)
    pairs = HEADS // 2
    lanes = 2 * head

    def head_block(offset):
        return pl.BlockSpec((1, seq, lanes), lambda r, p: (r, 0, p + offset))

    bias_block = pl.BlockSpec((1, seq, 1), lambda r, p: (r, 0, 0))
    lse_block = pl.BlockSpec((1, 1, 2, seq), lambda r, p: (r, p, 0, 0))
    context, lse = pl.pallas_call(
        functools.partial(attn_kernel, head**-0.5),
        grid=(rows, pairs),
        in_specs=[head_block(0), head_block(pairs), head_block(2 * pairs), bias_block],
        out_specs=[head_block(0), lse_block],
        out_shape=[
            jax.ShapeDtypeStruct((rows, seq, width), BF16),
            jax.ShapeDtypeStruct((rows, pairs, 2, seq), F32),
        ],
        compiler_params=params(),
        name="attention",
    )(packed_rows, packed_rows, packed_rows, key_bias)

    context = context.reshape(count, width)
    (layer_out, activated, grad_up, ffn_in, grad_down, grad_attn, grad_two, grad_ctx, sums, up_sums) = pl.pallas_call(
        functools.partial(ffn_kernel, per_row),
        grid=(tiles,),
        in_specs=[
            tiled(TILE, width),
            tiled(TILE, width),
            tiled(TILE, width),
            pl.BlockSpec((1, 1, width), lambda i: (i // per_row, 0, 0)),
            tiled(TILE, 1),
            fixed((width, width)),
            fixed((width, ff)),
            fixed((ff, width)),
            fixed((8, ff)),
        ],
        out_specs=[
            tiled(TILE, width),
            tiled(TILE, ff),
            tiled(TILE, ff),
            tiled(TILE, width),
            tiled(TILE, width),
            tiled(TILE, width),
            tiled(TILE, width),
            tiled(TILE, width),
            fixed((16, width)),
            fixed((8, ff)),
        ],
        out_shape=[
            jax.ShapeDtypeStruct((count, width), BF16),
            jax.ShapeDtypeStruct((count, ff), BF16),
            jax.ShapeDtypeStruct((count, ff), BF16),
            jax.ShapeDtypeStruct((count, width), BF16),
            jax.ShapeDtypeStruct((count, width), BF16),
            jax.ShapeDtypeStruct((count, width), BF16),
            jax.ShapeDtypeStruct((count, width), F32),
            jax.ShapeDtypeStruct((count, width), BF16),
            jax.ShapeDtypeStruct((16, width), F32),
            jax.ShapeDtypeStruct((8, ff), F32),
        ],
        scratch_shapes=[pltpu.VMEM((TILE, ff), F32)],
        compiler_params=params(),
        name="ffn",
    )(context, hidden, cot_flat, cls_grad.reshape(rows, 1, width), live_col, out_full, up_full, down_full, vecs)

    grad_rows = grad_ctx.reshape(rows, seq, width)
    grad_q, grad_k, grad_v = pl.pallas_call(
        functools.partial(attn_back_kernel, head**-0.5),
        grid=(rows, pairs),
        in_specs=[head_block(0), head_block(pairs), head_block(2 * pairs), bias_block, lse_block, head_block(0)],
        out_specs=[head_block(0)] * 3,
        out_shape=[jax.ShapeDtypeStruct((rows, seq, width), BF16)] * 3,
        compiler_params=params(),
        name="attention_back",
    )(packed_rows, packed_rows, packed_rows, key_bias, lse, grad_rows)

    grad_input, grad_query, grad_packed, bias_sums = pl.pallas_call(
        input_kernel,
        grid=(tiles,),
        in_specs=[
            tiled(TILE, width),
            tiled(TILE, width),
            tiled(TILE, width),
            tiled(TILE, width),
            tiled(TILE, width),
            tiled(TILE, width),
            pl.BlockSpec((1, 1, TILE), lambda i: (i, 0, 0)),
            tiled(TILE, 1),
            fixed((width, width)),
            fixed((width, 3 * width)),
        ],
        out_specs=[tiled(TILE, width), tiled(TILE, width), tiled(TILE, 3 * width), fixed((8, width))],
        out_shape=[
            jax.ShapeDtypeStruct((count, width), BF16),
            jax.ShapeDtypeStruct((count, width), BF16),
            jax.ShapeDtypeStruct((count, 3 * width), BF16),
            jax.ShapeDtypeStruct((8, width), F32),
        ],
        compiler_params=params(),
        name="merge_back",
    )(
        grad_q.reshape(count, width),
        grad_k.reshape(count, width),
        grad_v.reshape(count, width),
        grad_two,
        tok_flat,
        merge_query,
        live_row,
        live_col,
        merge_full,
        qkv_full,
    )

    grad_merge_w = t_mm(tok_flat, grad_query).astype(BF16)
    grad_qkv_w = t_mm(attn_in, grad_packed).astype(BF16)
    grad_out_w = t_mm(context, grad_attn).astype(BF16)
    grad_up_w = t_mm(ffn_in, grad_up).astype(BF16)
    grad_down_w = t_mm(activated, grad_down).astype(BF16)

    vec_grads = (sums[8], sums[3], sums[4], sums[2], sums[0], sums[1], bias_sums[0], bias_sums[1])
    vec_block = jnp.concatenate(
        [v.reshape(devices, share) for v in vec_grads] + [up_sums[0].reshape(devices, wide_ff * share)], axis=1
    )
    vec_block = jnp.pad(vec_block, ((0, 0), (0, 8 * width - used))).astype(BF16).reshape(devices, 8, width)
    partial = jnp.stack(
        [
            jnp.sum(squares[0]),
            jnp.sum(squares[1]),
            jnp.sum(sums[5]),
            jnp.sum(sums[6]),
            jnp.sum(sums[7]),
            jnp.sum(live_mask),
        ]
    )
    if direct:
        y_first, x_first = (3, 1, 2, 0), (3, 2, 1, 0)
        half_ff, half_qkv, half = ff // 2, 3 * width // 2, width // 2
        items = (
            (0, 0, half_ff, x_first),
            (1, 0, half, y_first),
            (0, half_ff, half_ff, x_first),
            (1, half, half, y_first),
            (2, 0, half_qkv, x_first),
            (2, half_qkv, half_qkv, y_first),
            (3, 0, width, x_first),
            (4, 0, width, y_first),
            (5, 0, width, x_first),
        )
        square = jnp.broadcast_to(jnp.pad(partial, (0, 2))[:, None], (8, 128))
        own_up, own_down, own_qkv, own_merge, own_out, own_vec, square = scatter_all(
            dims,
            [
                g.reshape(*dims, -1, g.shape[-1])
                for g in (grad_up_w, grad_down_w, grad_qkv_w, grad_merge_w, grad_out_w, vec_block)
            ],
            square,
            items,
        )
        own_vec = own_vec[0]
        totals = square[:6, 0]
    else:
        def owners(mat, n):
            return mat.reshape(devices, share, n, width).transpose(0, 2, 1, 3).reshape(devices, n * share, width)


        all_grads = jnp.concatenate(
            [
                owners(grad_merge_w, 1),
                owners(grad_out_w, 1),
                owners(grad_qkv_w, 3),
                owners(grad_up_w, wide_ff),
                grad_down_w.reshape(devices, wide_ff * share, width),
                vec_block,
            ],
            axis=1,
        )
        owned = lax.psum_scatter(all_grads, BOTH, scatter_dimension=0, tiled=True)[0].astype(F32)

        def joined(start, n):
            return jnp.concatenate([owned[start + i * share : start + (i + 1) * share] for i in range(n)], axis=1)

        own_vec = owned[base + wide_ff * share]
        own_merge, own_qkv, own_out, own_up = joined(0, 1), joined(2 * share, 3), joined(share, 1), joined(5 * share, wide_ff)
        own_down = owned[base : base + wide_ff * share]
        totals = lax.psum(partial, BOTH)
    own_vecs = [own_vec[i * share : (i + 1) * share] for i in range(8)]
    own_up_bias = own_vec[8 * share : 8 * share + wide_ff * share]

    layer_rows = layer_out.reshape(rows, seq, width)
    cls_rows = layer_rows[:, 0, :]
    my_logits = jnp.sum(
        my_select[:, :, None] * jnp.einsum("rd,kdc->rkc", cls_rows, heads, preferred_element_type=F32), axis=1
    )
    logits = my_logits * my_class
    group_cls = lax.all_gather(cls_rows, "batch", axis=0, tiled=True)
    owner_mask = (row_table == own).astype(F32)[:, None]
    class_live = (class_ids < class_count[0]).astype(F32)[None, :]
    group_dlog = group_dlog_raw * (owner_mask * class_live)
    grad_head = lax.dot_general(
        group_cls.astype(F32), group_dlog, (((0,), (0,)), ((), ())), precision=PRECISE, preferred_element_type=F32
    )[None]
    root_squares = jnp.sqrt(totals[:5] / (totals[5] * width))
    return (
        layer_rows,
        logits,
        grad_input.reshape(rows, seq, width),
        own_merge,
        own_qkv,
        own_vecs[6],
        own_vecs[7],
        own_out,
        own_vecs[0],
        own_vecs[1],
        own_vecs[2],
        own_up,
        own_up_bias,
        own_down,
        own_vecs[3],
        own_vecs[4],
        own_vecs[5],
        grad_head,
        root_squares,
    )


def solution(mesh):
    three = P(BOTH, None, None)
    two = P(BOTH, None)
    one = P(BOTH)
    placed = (
        three, one, two, P("table"), one, two, two, one, one, two, one, one, one, two, one, two, one, one, one, three,
        three, two,
    )
    results = (
        three, two, three, two, two, one, one, two, one, one, one, two, one, two, one, one, one, three, P(),
    )
    return jax.shard_map(body, mesh=mesh, in_specs=placed, out_specs=results, check_vma=False)
```

```python
import functools

import jax
import jax.numpy as jnp
from jax import lax
from jax.experimental import pallas as pl
from jax.experimental.pallas import tpu as pltpu
from jax.sharding import PartitionSpec as P

HEADS = 12
BLOCK = 8
NORM_EPS = 1e-05
MASKED = -1000000000.0
FAR = -3e38
PRECISE = lax.Precision.HIGHEST
TILE = 256
VMEM_BYTES = 64_000_000
BOTH = ("table", "batch")
F32 = jnp.float32
BF16 = jnp.bfloat16


def mm(left, right):
    return jnp.dot(left, right, preferred_element_type=F32)


def mm_t(left, right):
    return lax.dot_general(left, right, (((1,), (1,)), ((), ())), preferred_element_type=F32)


def t_mm(left, right):
    return lax.dot_general(left, right, (((0,), (0,)), ((), ())), preferred_element_type=F32)


def rowsum(values):
    return jnp.sum(values, axis=0, keepdims=True)


def norm_forward(hidden, gain, shift):
    average = jnp.mean(hidden, axis=-1, keepdims=True)
    centered = hidden - average
    variance = jnp.mean(centered * centered, axis=-1, keepdims=True)
    inv_std = lax.rsqrt(variance + NORM_EPS)
    standard = centered * inv_std
    return standard * gain + shift, standard, inv_std


def norm_backward(grad_norm, standard, inv_std, gain):
    scaled = grad_norm * gain
    return inv_std * (
        scaled
        - jnp.mean(scaled, axis=-1, keepdims=True)
        - standard * jnp.mean(scaled * standard, axis=-1, keepdims=True)
    )


def group_probs(query, tok, live_row, scale):
    size = tok.shape[0]
    row = lax.broadcasted_iota(jnp.int32, (size, size), 0) // BLOCK
    col = lax.broadcasted_iota(jnp.int32, (size, size), 1) // BLOCK
    scores = jnp.where(live_row > 0, mm_t(query, tok) * scale, MASKED)
    scores = jnp.where(row == col, scores, FAR)
    terms = jnp.exp(scores - jnp.max(scores, axis=-1, keepdims=True))
    return terms / jnp.sum(terms, axis=-1, keepdims=True), row == col


def merge_kernel(tok, live_row, live_col, merge_w, qkv_w, qkv_bias, query_out, hidden_out, attn_out, packed_out, squares):
    step = pl.program_id(0)
    scale = tok.shape[1] ** -0.5
    x = tok[...]
    live = live_col[...]
    query = mm(x, merge_w[...]).astype(BF16)
    query_out[...] = query
    probs, _ = group_probs(query, x, live_row[0], scale)
    merged = mm(probs.astype(BF16), x) * live
    wide = x.astype(F32)
    hidden = wide + merged
    hidden_out[...] = hidden
    attn_in = hidden.astype(BF16)
    attn_out[...] = attn_in
    packed_out[...] = (mm(attn_in, qkv_w[...]) + qkv_bias[...]).astype(BF16)

    @pl.when(step == 0)
    def _():
        squares[...] = jnp.zeros_like(squares)

    squares[0:1, :] += rowsum(live * wide * wide)
    squares[1:2, :] += rowsum(merged * merged)


def lane_mask(values, low, high):
    lane = lax.broadcasted_iota(jnp.int32, values.shape, 1)
    return jnp.where((lane >= low) & (lane < high), values, jnp.zeros_like(values))


def attn_kernel(scale, q_ref, k_ref, v_ref, bias_ref, ctx_ref, lse_ref):
    seq, lanes = q_ref.shape[1:]
    head = lanes // 2
    q = q_ref[0] * jnp.asarray(scale, BF16)
    k = k_ref[0]
    v_t = v_ref[0].T
    bias = bias_ref[0]
    for c in range(seq // TILE):
        rows = slice(c * TILE, (c + 1) * TILE)
        parts = []
        for h in range(2):
            scores = mm_t(k, lane_mask(q[rows], h * head, (h + 1) * head)) + bias
            top = jnp.max(scores, axis=0, keepdims=True)
            terms = jnp.exp(scores - top)
            total = jnp.sum(terms, axis=0, keepdims=True)
            probs = (terms * (1.0 / total)).astype(BF16)
            lse_ref[0, 0, h : h + 1, rows] = top + jnp.log(total)
            parts.append(mm(v_t[h * head : (h + 1) * head], probs))
        ctx_ref[0, rows, :] = jnp.concatenate(parts, axis=0).T.astype(BF16)


def attn_back_kernel(scale, q_ref, k_ref, v_ref, bias_ref, lse_ref, grad_ref, dq_ref, dk_ref, dv_ref):
    seq, lanes = q_ref.shape[1:]
    head = lanes // 2
    q = q_ref[0] * jnp.asarray(scale, BF16)
    k = k_ref[0]
    v = v_ref[0]
    k_t = k.T
    bias = bias_ref[0]
    grad_k = jnp.zeros((seq, lanes), F32)
    grad_v = jnp.zeros((seq, lanes), F32)
    for c in range(seq // TILE):
        rows = slice(c * TILE, (c + 1) * TILE)
        parts = []
        for h in range(2):
            q_part = lane_mask(q[rows], h * head, (h + 1) * head)
            g_part = lane_mask(grad_ref[0, rows, :], h * head, (h + 1) * head)
            scores = mm_t(k, q_part) + bias
            probs = jnp.exp(scores - lse_ref[0, 0, h : h + 1, rows])
            grad_v += mm(probs.astype(BF16), g_part)
            grad_p = mm_t(v, g_part)
            grad_s = (probs * (grad_p - jnp.sum(probs * grad_p, axis=0, keepdims=True))).astype(BF16)
            grad_k += mm(grad_s, q_part)
            parts.append(mm(k_t[h * head : (h + 1) * head], grad_s))
        dq_ref[0, rows, :] = (jnp.concatenate(parts, axis=0).T * scale).astype(BF16)
    dk_ref[0] = grad_k.astype(BF16)
    dv_ref[0] = grad_v.astype(BF16)


def ffn_kernel(
    per_row,
    ctx,
    hidden,
    cot,
    cls_grad,
    live_col,
    out_w,
    up_w,
    down_w,
    vecs,
    layer_out,
    activated,
    grad_up,
    ffn_in_out,
    grad_down_out,
    grad_attn_out,
    grad_two_out,
    grad_ctx_out,
    sums,
    up_sums,
    slope,
):
    step = pl.program_id(0)
    width = hidden.shape[1]
    chunks = up_w.shape[1] // width

    @pl.when(step == 0)
    def _():
        sums[...] = jnp.zeros_like(sums)
        up_sums[...] = jnp.zeros_like(up_sums)

    live = live_col[...]
    out_bias, gain_one, shift_one, down_bias, gain_two, shift_two = (vecs[i : i + 1, :width] for i in range(6))
    branch = mm(ctx[...], out_w[...]) + out_bias
    norm_one, standard_one, inv_one = norm_forward(hidden[...] + branch, gain_one, shift_one)
    ffn_in = norm_one.astype(BF16)
    ffn_in_out[...] = ffn_in
    down = jnp.zeros_like(norm_one)
    for j in range(chunks):
        cols = slice(j * width, (j + 1) * width)
        pre = mm(ffn_in, up_w[:, cols]) + vecs[6:7, cols]
        cumulative = 0.5 * (1.0 + lax.erf(pre * 0.7071067811865476))
        act = (pre * cumulative).astype(BF16)
        slope[:, cols] = cumulative + pre * (jnp.exp(-0.5 * pre * pre) * 0.3989422804014327)
        activated[:, cols] = act
        down += mm(act, down_w[cols, :])
    down += down_bias
    normed, standard_two, inv_two = norm_forward(norm_one + down, gain_two, shift_two)
    result = (normed * live).astype(BF16)
    layer_out[...] = result
    wide = result.astype(F32)
    sums[5:6, :] += rowsum(live * branch * branch)
    sums[6:7, :] += rowsum(live * down * down)
    sums[7:8, :] += rowsum(wide * wide)
    first = (lax.broadcasted_iota(jnp.int32, (hidden.shape[0], 1), 0) == 0) & (step % per_row == 0)
    grad = live * (cot[...].astype(F32) + jnp.where(first, cls_grad[0], 0.0))
    sums[0:1, :] += rowsum(grad * standard_two)
    sums[1:2, :] += rowsum(grad)
    grad_three = norm_backward(grad, standard_two, inv_two, gain_two)
    grad_down = grad_three.astype(BF16)
    grad_down_out[...] = grad_down
    sums[2:3, :] += rowsum(grad_down.astype(F32))
    total = grad_three
    for j in range(chunks):
        cols = slice(j * width, (j + 1) * width)
        piece = (mm_t(grad_down, down_w[cols, :]) * slope[:, cols]).astype(BF16)
        grad_up[:, cols] = piece
        up_sums[0:1, cols] += rowsum(piece.astype(F32))
        total += mm_t(piece, up_w[:, cols])
    sums[3:4, :] += rowsum(total * standard_one)
    sums[4:5, :] += rowsum(total)
    grad_two = norm_backward(total, standard_one, inv_one, gain_one)
    grad_two_out[...] = grad_two
    grad_attn = grad_two.astype(BF16)
    grad_attn_out[...] = grad_attn
    sums[8:9, :] += rowsum(grad_attn.astype(F32))
    grad_ctx_out[...] = mm_t(grad_attn, out_w[...]).astype(BF16)


def input_kernel(
    dq, dk, dv, grad_two, tok, query, live_row, live_col, merge_w, qkv_w, grad_input, grad_query_out, packed_out, sums
):
    step = pl.program_id(0)
    width = tok.shape[1]
    scale = width**-0.5

    @pl.when(step == 0)
    def _():
        sums[...] = jnp.zeros_like(sums)

    x = tok[...]
    grad_q, grad_v = dq[...], dv[...]
    grad_one = grad_two[...]
    for i, piece in enumerate((grad_q, dk[...], grad_v)):
        cols = slice(i * width, (i + 1) * width)
        packed_out[:, cols] = piece
        grad_one += mm_t(piece, qkv_w[:, cols])
    sums[0:1, :] += rowsum(grad_q.astype(F32))
    sums[1:2, :] += rowsum(grad_v.astype(F32))
    grad_merged = (grad_one * live_col[...]).astype(BF16)
    mq = query[...]
    probs, same = group_probs(mq, x, live_row[0], scale)
    grad_probs = mm_t(grad_merged, x)
    grad_scores = probs * (grad_probs - jnp.sum(probs * grad_probs, axis=-1, keepdims=True))
    grad_scores = jnp.where(same & (live_row[0] > 0), grad_scores, 0.0)
    grad_query = (mm(grad_scores.astype(BF16), x) * scale).astype(BF16)
    grad_query_out[...] = grad_query
    blocks = mm(probs.T.astype(BF16), grad_merged) + mm(grad_scores.T.astype(BF16), mq) * scale
    blocks += mm_t(grad_query, merge_w[...])
    grad_input[...] = (grad_one + blocks).astype(BF16)


def params(**kw):
    return pltpu.CompilerParams(vmem_limit_bytes=VMEM_BYTES, **kw)


def fixed(shape):
    zeros = (0,) * len(shape)
    return pl.BlockSpec(shape, lambda *_: zeros, pipeline_mode=pl.Buffered(1))


def tiled(size, width):
    return pl.BlockSpec((size, width), lambda i: (i, 0))


MESH = pl.DeviceIdType.MESH
TABLE_MAJOR = 4
CORES = 2


def here(dims):
    table, batch = lax.axis_index("table"), lax.axis_index("batch")
    return [table // dims[1], lax.rem(table, dims[1]), batch // CORES, lax.rem(batch, CORES)]


def peer(dims, spot, axis, offset):
    other = list(spot)
    other[axis] = lax.rem(spot[axis] + offset, dims[axis])
    return (other[0] * dims[1] + other[1], other[2] * CORES + other[3]), other[axis]


def greet(dims, spot):
    barrier = pltpu.get_barrier_semaphore()
    total = 0
    for axis in range(4):
        for offset in range(1, dims[axis]):
            target, _ = peer(dims, spot, axis, offset)
            pl.semaphore_signal(barrier, inc=1, device_id=target, device_id_type=MESH)
            total += 1
    pl.semaphore_wait(barrier, total)


def gather_events(dims, spot, items, shards, fulls, local_sem, send_sem, recv_sem):
    def region(item, done):
        array, low, size, order = items[item]
        where = tuple(slice(None) if axis in done else spot[axis] for axis in sorted(order))
        return fulls[array].at[(*where, slice(None), pl.ds(low, size))]

    def copies(item, stage):
        array, low, size, order = items[item]
        place = region(item, order[:stage])
        return [
            pltpu.make_async_remote_copy(
                src_ref=place if stage else shards[array].at[:, pl.ds(low, size)],
                dst_ref=place,
                send_sem=send_sem.at[item, stage, offset],
                recv_sem=recv_sem.at[item, stage, offset],
                device_id=peer(dims, spot, order[stage], offset)[0],
                device_id_type=MESH,
            )
            for offset in range(1, dims[order[stage]])
        ]

    def keep(item):
        array, low, size, _ = items[item]
        return pltpu.make_async_copy(shards[array].at[:, pl.ds(low, size)], region(item, ()), local_sem.at[item])

    def begin():
        for item in range(len(items)):
            keep(item).start()
            for copy in copies(item, 0):
                copy.start()

    def advance(item, stage):
        for copy in copies(item, stage):
            copy.wait_recv()
        if stage == 0:
            keep(item).wait()
        if stage + 1 < len(items[item][3]):
            for copy in copies(item, stage + 1):
                copy.start()

    def end():
        for item in range(len(items)):
            for stage in range(len(items[item][3])):
                for copy in copies(item, stage):
                    copy.wait_send()

    return begin, slots(items, advance), end


def slots(items, advance):
    count = len(items)
    pairs = (count + 1) // 2
    groups = []
    for slot in range(pairs + 3):
        group = []
        for stage in (3, 2, 1, 0):
            pair = slot - stage
            for item in range(2 * pair, min(2 * pair + 2, count)) if 0 <= pair < pairs else ():
                if stage < len(items[item][3]):
                    group.append(functools.partial(advance, item, stage))
        groups.append(group)
    return groups


def scatter_events(dims, spot, items, grads, outs, buffers, local_sem, send_sem, recv_sem):
    buffers = [buffers[i * 7 : (i + 1) * 7] for i in range(len(items))]

    def load(item):
        array, low, size, _ = items[item]
        return pltpu.make_async_copy(
            grads[array].at[:, :, :, spot[3], :, pl.ds(low, size)], buffers[item][0], local_sem.at[item]
        )

    def copies(item, stage):
        array, low, size, order = items[item]
        own, first, second, got_core, got_first, got_second, got_last = buffers[item]
        axis = order[stage]
        made = []
        for offset in range(1, dims[axis]):
            target, other = peer(dims, spot, axis, offset)
            if stage == 0:
                source, landing = grads[array].at[:, :, :, other, :, pl.ds(low, size)], got_core
            elif stage == 1:
                source = own.at[:, :, other] if axis == 2 else own.at[:, other]
                landing = got_first.at[offset - 1]
            elif stage == 2:
                source, landing = first.at[:, other], got_second.at[offset - 1]
            else:
                source, landing = second.at[other], got_last.at[offset - 1]
            made.append(
                pltpu.make_async_remote_copy(
                    src_ref=source,
                    dst_ref=landing,
                    send_sem=send_sem.at[item, stage, offset],
                    recv_sem=recv_sem.at[item, stage, offset],
                    device_id=target,
                    device_id_type=MESH,
                )
            )
        return made

    def begin():
        for item in range(len(items)):
            load(item).start()
            for copy in copies(item, 0):
                copy.start()

    def advance(item, stage):
        array, low, size, order = items[item]
        own, first, second, got_core, got_first, got_second, got_last = buffers[item]
        axis = order[stage]
        others = range(dims[axis] - 1)
        mine = spot[axis]
        for copy in copies(item, stage):
            copy.wait_recv()
        if stage == 0:
            load(item).wait()

            @pl.loop(0, dims[0] * dims[1] * dims[2])
            def _(i):
                at = (i // (dims[1] * dims[2]), lax.rem(i // dims[2], dims[1]), lax.rem(i, dims[2]))
                own[at] = (own[at].astype(F32) + got_core[at].astype(F32)).astype(BF16)
        elif stage == 1:
            inner = first.shape[1]

            @pl.loop(0, dims[0] * inner)
            def _(i):
                at = (i // inner, lax.rem(i, inner))
                value = own[(*at, mine) if axis == 2 else (at[0], mine, at[1])].astype(F32)
                for k in others:
                    value += got_first[(k, *at)].astype(F32)
                first[at] = value.astype(BF16)
        elif stage == 2:

            @pl.loop(0, dims[0])
            def _(i):
                value = first[i, mine].astype(F32)
                for k in others:
                    value += got_second[k, i].astype(F32)
                second[i] = value.astype(BF16)
        else:
            value = second[mine].astype(F32)
            for k in others:
                value += got_last[k].astype(F32)
            outs[array][:, low : low + size] = value
        if stage < 3:
            for copy in copies(item, stage + 1):
                copy.start()

    def end():
        for item in range(len(items)):
            for stage in range(4):
                for copy in copies(item, stage):
                    copy.wait_send()

    return begin, slots(items, advance), end


def square_events(dims, spot, square, total, kept, got, send_sem, recv_sem):
    def copies(stage):
        axis = 3 - stage
        return [
            pltpu.make_async_remote_copy(
                src_ref=kept.at[stage],
                dst_ref=got.at[stage, offset - 1],
                send_sem=send_sem.at[stage, offset],
                recv_sem=recv_sem.at[stage, offset],
                device_id=peer(dims, spot, axis, offset)[0],
                device_id_type=MESH,
            )
            for offset in range(1, dims[axis])
        ]

    def begin():
        kept[0] = square[...]
        for copy in copies(0):
            copy.start()

    def advance(stage):
        for copy in copies(stage):
            copy.wait_recv()
        value = kept[stage]
        for offset in range(1, dims[3 - stage]):
            value = value + got[stage, offset - 1]
        kept[stage + 1] = value
        if stage < 3:
            for copy in copies(stage + 1):
                copy.start()
        else:
            total[...] = value

    def end():
        for stage in range(4):
            for copy in copies(stage):
                copy.wait_send()

    return begin, [[functools.partial(advance, stage)] for stage in range(4)], end


def scatter_scratch(dims, grads, items):
    scratch = []
    for array, _, size, order in items:
        tail = (grads[array].shape[4], size)
        inner = dims[order[2]]
        for shape in (
            dims[:3],
            (dims[0], inner),
            (dims[0],),
            dims[:3],
            (dims[order[1]] - 1, dims[0], inner),
            (inner - 1, dims[0]),
            (dims[0] - 1,),
        ):
            scratch.append(pltpu.VMEM((*shape, *tail), BF16))
    return scratch


def links(count, most):
    return [pltpu.SemaphoreType.DMA((count, 4, most)), pltpu.SemaphoreType.DMA((count, 4, most))]


def moving_call(dims, collective_id, name, kernel, grid, own_in, own_out, gather, scatter, square, pace=1.0):
    most = max(dims)
    vmem, anywhere = (lambda a: fixed(a.shape)), (lambda a: pl.BlockSpec(memory_space=pl.ANY))
    shards, gather_items = gather
    grads, scatter_items = scatter
    squares = [] if square is None else [square]
    in_specs, args = [spec for spec, _ in own_in], [arg for _, arg in own_in]
    in_specs += [vmem(a) for a in shards] + [anywhere(a) for a in grads] + [vmem(a) for a in squares]
    args += [*shards, *grads, *squares]
    out_specs, out_shape = [spec for spec, _ in own_out], [shape for _, shape in own_out]
    orders = {array: sorted(order) for array, _, _, order in gather_items}
    for i, a in enumerate(shards):
        out_specs.append(anywhere(a))
        out_shape.append(jax.ShapeDtypeStruct((*(dims[axis] for axis in orders[i]), *a.shape), a.dtype))
    for g in grads:
        out_shape.append(jax.ShapeDtypeStruct(g.shape[4:], F32))
        out_specs.append(vmem(out_shape[-1]))
    for q in squares:
        out_shape.append(jax.ShapeDtypeStruct(q.shape, F32))
        out_specs.append(vmem(q))
    groups = []
    if shards:
        groups.append([pltpu.SemaphoreType.DMA((len(gather_items),)), *links(len(gather_items), most)])
    if grads:
        buffers = scatter_scratch(dims, grads, scatter_items)
        groups.append([*buffers, pltpu.SemaphoreType.DMA((len(scatter_items),)), *links(len(scatter_items), most)])
    if squares:
        groups.append(
            [
                pltpu.VMEM((5, *square.shape), F32),
                pltpu.VMEM((4, most - 1, *square.shape), F32),
                pltpu.SemaphoreType.DMA((4, most)),
                pltpu.SemaphoreType.DMA((4, most)),
            ]
        )
    steps = 1
    for size in grid:
        steps *= size

    def fused(*refs):
        refs = list(refs)

        def take(n):
            taken = refs[:n]
            del refs[:n]
            return taken

        ins, shard_refs, grad_refs, square_refs = take(len(own_in)), take(len(shards)), take(len(grads)), take(len(squares))
        outs, full_refs, sum_refs, total_refs = take(len(own_out)), take(len(shards)), take(len(grads)), take(len(squares))
        step = 0
        for axis, size in enumerate(grid):
            step = step * size + pl.program_id(axis)
        spot = here(dims)
        plans = []
        scratch = iter(groups)
        if shards:
            plans.append(gather_events(dims, spot, gather_items, shard_refs, full_refs, *take(len(next(scratch)))))
        if grads:
            held = take(len(next(scratch)))
            plans.append(scatter_events(dims, spot, scatter_items, grad_refs, sum_refs, held[:-3], *held[-3:]))
        if squares:
            plans.append(square_events(dims, spot, *square_refs, *total_refs, *take(len(next(scratch)))))

        def open_all():
            greet(dims, spot)
            for begin, _, _ in plans:
                begin()

        depth = max(len(groups_of) for _, groups_of, _ in plans)
        merged = [[e for _, groups_of, _ in plans if i < len(groups_of) for e in groups_of[i]] for i in range(depth)]

        def close_all():
            for _, _, end in plans:
                end()

        if steps == 1:
            open_all()
            for group in merged:
                for event in group:
                    event()
            close_all()
            return
        late = []
        pl.when(step == 0)(open_all)
        for i, group in enumerate(merged):
            at = int((i + 1) * pace)

            def run(group=group):
                for event in group:
                    event()

            if at < steps:
                pl.when(step == at)(run)
            else:
                late.append(run)
        kernel(*ins, *outs)

        @pl.when(step == steps - 1)
        def _():
            for run in late:
                run()
            close_all()

    return pl.pallas_call(
        fused,
        grid=grid,
        in_specs=in_specs,
        out_specs=out_specs,
        out_shape=out_shape,
        scratch_shapes=[piece for group in groups for piece in group],
        compiler_params=params(collective_id=collective_id, has_side_effects=True),
        name=name,
    )(*args)


def body(
    tokens,
    row_blocks,
    block_fill,
    row_table,
    class_count,
    merge_w,
    qkv_w,
    query_bias,
    value_bias,
    out_w,
    out_bias,
    gain_one,
    shift_one,
    up_w,
    up_bias,
    down_w,
    down_bias,
    gain_two,
    shift_two,
    head_w,
    cotangent,
    logit_cotangent,
):
    rows, seq, width = tokens.shape
    count = rows * seq
    ff = up_w.shape[1]
    head = width // HEADS
    per_row = seq // TILE
    tiles = count // TILE
    share = merge_w.shape[0]
    devices = width // share
    wide_ff = ff // width

    def cut(mat, n):
        return [mat[:, i * width : (i + 1) * width] for i in range(n)]

    table_size, batch_size = lax.axis_size("table"), lax.axis_size("batch")
    dims = (TABLE_MAJOR, table_size // TABLE_MAJOR, batch_size // CORES, CORES)
    direct = share % BLOCK == 0
    vec_list = (out_bias, gain_one, shift_one, down_bias, gain_two, shift_two, query_bias, value_bias)
    vec_row = jnp.concatenate([*vec_list, up_bias])
    used = vec_row.shape[0]
    vec_row = jnp.pad(vec_row, (0, 8 * width - used)).reshape(8, width)
    base = (5 + wide_ff) * share
    down_out, up_out = (0, 1, 2, 3), (0, 2, 1, 3)
    down_in, up_in = (3, 1, 2, 0), (3, 2, 1, 0)
    none = ((), ())
    if direct:
        qkv_full, merge_full, vec_full = moving_call(
            dims,
            0,
            "gather_first",
            None,
            (1,),
            [],
            [],
            (
                (qkv_w, merge_w, vec_row),
                (
                    (1, 0, width, down_out),
                    (0, 0, width, up_out),
                    (0, width, width, down_out),
                    (0, 2 * width, width, up_out),
                    (2, 0, width, down_out),
                ),
            ),
            none,
            None,
        )
        qkv_full = qkv_full.reshape(width, 3 * width)
        merge_full = merge_full.reshape(width, width)
        vec_rows = vec_full.reshape(devices, 8, width)[:, 0].astype(F32)
    else:
        mine = jnp.concatenate([merge_w, out_w, *cut(qkv_w, 3), *cut(up_w, wide_ff), down_w, vec_row], axis=0)
        gathered = lax.all_gather(mine, BOTH, axis=0)

        def unit(start, n):
            part = gathered[:, start : start + n * share]
            part = part.reshape(devices, n, share, width).transpose(0, 2, 1, 3)
            return part.reshape(width, n * width)

        merge_full = unit(0, 1)
        out_full = unit(share, 1)
        qkv_full = unit(2 * share, 3)
        up_full = unit(5 * share, wide_ff)
        down_full = gathered[:, base : base + wide_ff * share].reshape(ff, width)
        vec_rows = gathered[:, base + wide_ff * share].astype(F32)
    vectors = [vec_rows[:, i * share : (i + 1) * share].reshape(1, width) for i in range(8)]
    up_bias_full = vec_rows[:, 8 * share : 8 * share + wide_ff * share].reshape(1, ff)
    query_vec, value_vec = vectors[6], vectors[7]
    qkv_bias = jnp.concatenate([query_vec, jnp.zeros_like(query_vec), value_vec], axis=1)
    vecs = jnp.concatenate(
        [jnp.pad(jnp.concatenate(vectors[:6], axis=0), ((0, 0), (0, ff - width))), up_bias_full, jnp.zeros((1, ff), F32)],
        axis=0,
    )

    position = jnp.arange(seq, dtype=jnp.int32)
    fill_tok = jnp.repeat(block_fill, BLOCK, axis=1)
    live = ((position // BLOCK)[None, :] < row_blocks[:, None]) & ((position % BLOCK)[None, :] < fill_tok)
    live_mask = live.astype(F32)
    live_col = live_mask.reshape(count, 1)
    live_row = live_mask.reshape(tiles, 1, TILE)
    key_bias = jnp.where(live, 0.0, MASKED).astype(F32).reshape(rows, seq, 1)

    batch = lax.axis_size("batch")
    classes = head_w.shape[2]
    tok_flat = tokens.reshape(count, width)
    cot_flat = cotangent.reshape(count, width)
    merge_query, hidden, attn_in, packed, squares = pl.pallas_call(
        merge_kernel,
        grid=(tiles,),
        in_specs=[
            tiled(TILE, width),
            pl.BlockSpec((1, 1, TILE), lambda i: (i, 0, 0)),
            tiled(TILE, 1),
            fixed((width, width)),
            fixed((width, 3 * width)),
            fixed((1, 3 * width)),
        ],
        out_specs=[
            tiled(TILE, width),
            tiled(TILE, width),
            tiled(TILE, width),
            tiled(TILE, 3 * width),
            fixed((8, width)),
        ],
        out_shape=[
            jax.ShapeDtypeStruct((count, width), BF16),
            jax.ShapeDtypeStruct((count, width), F32),
            jax.ShapeDtypeStruct((count, width), BF16),
            jax.ShapeDtypeStruct((count, 3 * width), BF16),
            jax.ShapeDtypeStruct((8, width), F32),
        ],
        compiler_params=params(),
        name="merge_qkv",
    )(tok_flat, live_row, live_col, merge_full, qkv_full, qkv_bias)

    packed_rows = packed.reshape(rows, seq, 3 * width)
    pairs = HEADS // 2
    lanes = 2 * head

    def head_block(offset):
        return pl.BlockSpec((1, seq, lanes), lambda r, p: (r, 0, p + offset))

    bias_block = pl.BlockSpec((1, seq, 1), lambda r, p: (r, 0, 0))
    lse_block = pl.BlockSpec((1, 1, 2, seq), lambda r, p: (r, p, 0, 0))
    attn_in_refs = [
        (head_block(0), packed_rows),
        (head_block(pairs), packed_rows),
        (head_block(2 * pairs), packed_rows),
        (bias_block, key_bias),
    ]
    attn_outs = [
        (head_block(0), jax.ShapeDtypeStruct((rows, seq, width), BF16)),
        (lse_block, jax.ShapeDtypeStruct((rows, pairs, 2, seq), F32)),
    ]
    attend = functools.partial(attn_kernel, head**-0.5)
    if direct:
        limit = jnp.broadcast_to(class_count.astype(F32)[:, None], (1, classes))
        spare = -(rows + 1) % 8
        small = jnp.concatenate([logit_cotangent, limit, jnp.zeros((spare, classes), F32)], axis=0)
        third, narrow = ff // 3, width // 3
        gather_items = [(3, 0, classes, (2, 3)), (4, 0, classes, (2, 3))]
        for i in range(3):
            gather_items += [(0, i * third, third, up_out), (1, i * narrow, narrow, down_out)]
        gather_items.append((2, 0, width, down_out))
        context, lse, up_full, down_full, out_full, heads, small = moving_call(
            dims,
            2,
            "attention_gather",
            attend,
            (rows, pairs),
            attn_in_refs,
            attn_outs,
            ((up_w, down_w, out_w, head_w[0], small), gather_items),
            none,
            None,
            pace=2.2,
        )
        up_full = up_full.reshape(width, ff)
        down_full = down_full.reshape(ff, width)
        out_full = out_full.reshape(width, width)
        heads = heads.reshape(batch, width, classes)
        small = small.reshape(batch, -1, classes)
        group_dlog_raw = small[:, :rows].reshape(batch * rows, classes)
        counts = small[:, rows, 0]
    else:
        context, lse = pl.pallas_call(
            attend,
            grid=(rows, pairs),
            in_specs=[spec for spec, _ in attn_in_refs],
            out_specs=[spec for spec, _ in attn_outs],
            out_shape=[shape for _, shape in attn_outs],
            compiler_params=params(),
            name="attention",
        )(*(arg for _, arg in attn_in_refs))
        heads = lax.all_gather(head_w[0], "batch", axis=0)
        counts = lax.all_gather(class_count, "batch", axis=0, tiled=True)
        group_dlog_raw = lax.all_gather(logit_cotangent, "batch", axis=0, tiled=True)
    own = lax.axis_index("batch")
    my_table = lax.dynamic_slice(row_table, (own * rows,), (rows,))
    class_ids = jnp.arange(classes, dtype=jnp.int32)
    my_select = (my_table[:, None] == jnp.arange(batch, dtype=jnp.int32)[None, :]).astype(F32)
    my_class = (class_ids[None, :] < (my_select * counts[None, :].astype(F32)).sum(1, keepdims=True)).astype(F32)
    my_dlog = logit_cotangent * my_class
    picked = (my_select[:, :, None] * my_dlog[:, None, :]).transpose(1, 0, 2)
    cls_grad = jnp.sum(
        lax.dot_general(picked, heads.astype(F32), (((2,), (2,)), ((0,), (0,))), precision=PRECISE), axis=0
    )

    context = context.reshape(count, width)
    (layer_out, activated, grad_up, ffn_in, grad_down, grad_attn, grad_two, grad_ctx, sums, up_sums) = pl.pallas_call(
        functools.partial(ffn_kernel, per_row),
        grid=(tiles,),
        in_specs=[
            tiled(TILE, width),
            tiled(TILE, width),
            tiled(TILE, width),
            pl.BlockSpec((1, 1, width), lambda i: (i // per_row, 0, 0)),
            tiled(TILE, 1),
            fixed((width, width)),
            fixed((width, ff)),
            fixed((ff, width)),
            fixed((8, ff)),
        ],
        out_specs=[
            tiled(TILE, width),
            tiled(TILE, ff),
            tiled(TILE, ff),
            tiled(TILE, width),
            tiled(TILE, width),
            tiled(TILE, width),
            tiled(TILE, width),
            tiled(TILE, width),
            fixed((16, width)),
            fixed((8, ff)),
        ],
        out_shape=[
            jax.ShapeDtypeStruct((count, width), BF16),
            jax.ShapeDtypeStruct((count, ff), BF16),
            jax.ShapeDtypeStruct((count, ff), BF16),
            jax.ShapeDtypeStruct((count, width), BF16),
            jax.ShapeDtypeStruct((count, width), BF16),
            jax.ShapeDtypeStruct((count, width), BF16),
            jax.ShapeDtypeStruct((count, width), F32),
            jax.ShapeDtypeStruct((count, width), BF16),
            jax.ShapeDtypeStruct((16, width), F32),
            jax.ShapeDtypeStruct((8, ff), F32),
        ],
        scratch_shapes=[pltpu.VMEM((TILE, ff), F32)],
        compiler_params=params(),
        name="ffn",
    )(context, hidden, cot_flat, cls_grad.reshape(rows, 1, width), live_col, out_full, up_full, down_full, vecs)

    grad_rows = grad_ctx.reshape(rows, seq, width)
    cls_rows = layer_out.reshape(rows, seq, width)[:, 0, :]
    back_refs = [*attn_in_refs, (lse_block, lse), (head_block(0), grad_rows)]
    back_outs = [(head_block(0), jax.ShapeDtypeStruct((rows, seq, width), BF16))] * 3
    attend_back = functools.partial(attn_back_kernel, head**-0.5)
    grad_out_w = t_mm(context, grad_attn).astype(BF16)
    grad_up_w = t_mm(ffn_in, grad_up).astype(BF16)
    grad_down_w = t_mm(activated, grad_down).astype(BF16)
    if direct:
        ffn_items = []
        for i in range(3):
            ffn_items += [(0, i * third, third, up_in), (1, i * narrow, narrow, down_in)]
        ffn_items.append((2, 0, width, down_in))
        first_rows = jnp.pad(cls_rows, ((0, -rows % 8), (0, 0)))
        grad_q, grad_k, grad_v, group_cls, own_up, own_down, own_out = moving_call(
            dims,
            3,
            "attention_back_scatter",
            attend_back,
            (rows, pairs),
            back_refs,
            back_outs,
            ((first_rows,), ((0, 0, width, (2, 3)),)),
            ([g.reshape(*dims, -1, g.shape[-1]) for g in (grad_up_w, grad_down_w, grad_out_w)], ffn_items),
            None,
            pace=2.4,
        )
        group_cls = group_cls.reshape(batch, -1, width)[:, :rows].reshape(batch * rows, width)
    else:
        grad_q, grad_k, grad_v = pl.pallas_call(
            attend_back,
            grid=(rows, pairs),
            in_specs=[spec for spec, _ in back_refs],
            out_specs=[spec for spec, _ in back_outs],
            out_shape=[shape for _, shape in back_outs],
            compiler_params=params(),
            name="attention_back",
        )(*(arg for _, arg in back_refs))
        group_cls = lax.all_gather(cls_rows, "batch", axis=0, tiled=True)

    grad_input, grad_query, grad_packed, bias_sums = pl.pallas_call(
        input_kernel,
        grid=(tiles,),
        in_specs=[
            tiled(TILE, width),
            tiled(TILE, width),
            tiled(TILE, width),
            tiled(TILE, width),
            tiled(TILE, width),
            tiled(TILE, width),
            pl.BlockSpec((1, 1, TILE), lambda i: (i, 0, 0)),
            tiled(TILE, 1),
            fixed((width, width)),
            fixed((width, 3 * width)),
        ],
        out_specs=[tiled(TILE, width), tiled(TILE, width), tiled(TILE, 3 * width), fixed((8, width))],
        out_shape=[
            jax.ShapeDtypeStruct((count, width), BF16),
            jax.ShapeDtypeStruct((count, width), BF16),
            jax.ShapeDtypeStruct((count, 3 * width), BF16),
            jax.ShapeDtypeStruct((8, width), F32),
        ],
        compiler_params=params(),
        name="merge_back",
    )(
        grad_q.reshape(count, width),
        grad_k.reshape(count, width),
        grad_v.reshape(count, width),
        grad_two,
        tok_flat,
        merge_query,
        live_row,
        live_col,
        merge_full,
        qkv_full,
    )

    grad_merge_w = t_mm(tok_flat, grad_query).astype(BF16)
    grad_qkv_w = t_mm(attn_in, grad_packed).astype(BF16)

    vec_grads = (sums[8], sums[3], sums[4], sums[2], sums[0], sums[1], bias_sums[0], bias_sums[1])
    vec_block = jnp.concatenate(
        [v.reshape(devices, share) for v in vec_grads] + [up_sums[0].reshape(devices, wide_ff * share)], axis=1
    )
    vec_block = jnp.pad(vec_block, ((0, 0), (0, 8 * width - used))).astype(BF16).reshape(devices, 8, width)
    partial = jnp.stack(
        [
            jnp.sum(squares[0]),
            jnp.sum(squares[1]),
            jnp.sum(sums[5]),
            jnp.sum(sums[6]),
            jnp.sum(sums[7]),
            jnp.sum(live_mask),
        ]
    )
    if direct:
        square = jnp.broadcast_to(jnp.pad(partial, (0, 2))[:, None], (8, 128))
        own_qkv, own_merge, own_vec, square = moving_call(
            dims,
            1,
            "scatter_last",
            None,
            (1,),
            [],
            [],
            none,
            (
                [g.reshape(*dims, -1, g.shape[-1]) for g in (grad_qkv_w, grad_merge_w, vec_block)],
                (
                    (0, 0, width, up_in),
                    (0, width, width, down_in),
                    (0, 2 * width, width, up_in),
                    (1, 0, width, down_in),
                    (2, 0, width, up_in),
                ),
            ),
            square,
        )
        own_vec = own_vec[0]
        totals = square[:6, 0]
    else:
        def owners(mat, n):
            return mat.reshape(devices, share, n, width).transpose(0, 2, 1, 3).reshape(devices, n * share, width)


        all_grads = jnp.concatenate(
            [
                owners(grad_merge_w, 1),
                owners(grad_out_w, 1),
                owners(grad_qkv_w, 3),
                owners(grad_up_w, wide_ff),
                grad_down_w.reshape(devices, wide_ff * share, width),
                vec_block,
            ],
            axis=1,
        )
        owned = lax.psum_scatter(all_grads, BOTH, scatter_dimension=0, tiled=True)[0].astype(F32)

        def joined(start, n):
            return jnp.concatenate([owned[start + i * share : start + (i + 1) * share] for i in range(n)], axis=1)

        own_vec = owned[base + wide_ff * share]
        own_merge, own_qkv, own_out, own_up = joined(0, 1), joined(2 * share, 3), joined(share, 1), joined(5 * share, wide_ff)
        own_down = owned[base : base + wide_ff * share]
        totals = lax.psum(partial, BOTH)
    own_vecs = [own_vec[i * share : (i + 1) * share] for i in range(8)]
    own_up_bias = own_vec[8 * share : 8 * share + wide_ff * share]

    layer_rows = layer_out.reshape(rows, seq, width)
    my_logits = jnp.sum(
        my_select[:, :, None] * jnp.einsum("rd,kdc->rkc", cls_rows, heads, preferred_element_type=F32), axis=1
    )
    logits = my_logits * my_class
    owner_mask = (row_table == own).astype(F32)[:, None]
    class_live = (class_ids < class_count[0]).astype(F32)[None, :]
    group_dlog = group_dlog_raw * (owner_mask * class_live)
    grad_head = lax.dot_general(
        group_cls.astype(F32), group_dlog, (((0,), (0,)), ((), ())), precision=PRECISE, preferred_element_type=F32
    )[None]
    root_squares = jnp.sqrt(totals[:5] / (totals[5] * width))
    return (
        layer_rows,
        logits,
        grad_input.reshape(rows, seq, width),
        own_merge,
        own_qkv,
        own_vecs[6],
        own_vecs[7],
        own_out,
        own_vecs[0],
        own_vecs[1],
        own_vecs[2],
        own_up,
        own_up_bias,
        own_down,
        own_vecs[3],
        own_vecs[4],
        own_vecs[5],
        grad_head,
        root_squares,
    )


def solution(mesh):
    three = P(BOTH, None, None)
    two = P(BOTH, None)
    one = P(BOTH)
    placed = (
        three, one, two, P("table"), one, two, two, one, one, two, one, one, one, two, one, two, one, one, one, three,
        three, two,
    )
    results = (
        three, two, three, two, two, one, one, two, one, one, one, two, one, two, one, one, one, three, P(),
    )
    return jax.shard_map(body, mesh=mesh, in_specs=placed, out_specs=results, check_vma=False)
```

```python
import functools

import jax
import jax.numpy as jnp
from jax import lax
from jax.experimental import pallas as pl
from jax.experimental.pallas import tpu as pltpu
from jax.sharding import PartitionSpec as P

HEADS = 12
BLOCK = 8
NORM_EPS = 1e-05
MASKED = -1000000000.0
FAR = -3e38
PRECISE = lax.Precision.HIGHEST
TILE = 256
VMEM_BYTES = 64_000_000
BOTH = ("table", "batch")
F32 = jnp.float32
BF16 = jnp.bfloat16


def mm(left, right):
    return jnp.dot(left, right, preferred_element_type=F32)


def mm_t(left, right):
    return lax.dot_general(left, right, (((1,), (1,)), ((), ())), preferred_element_type=F32)


def t_mm(left, right):
    return lax.dot_general(left, right, (((0,), (0,)), ((), ())), preferred_element_type=F32)


def rowsum(values):
    return jnp.sum(values, axis=0, keepdims=True)


def norm_forward(hidden, gain, shift):
    average = jnp.mean(hidden, axis=-1, keepdims=True)
    centered = hidden - average
    variance = jnp.mean(centered * centered, axis=-1, keepdims=True)
    inv_std = lax.rsqrt(variance + NORM_EPS)
    standard = centered * inv_std
    return standard * gain + shift, standard, inv_std


def norm_backward(grad_norm, standard, inv_std, gain):
    scaled = grad_norm * gain
    return inv_std * (
        scaled
        - jnp.mean(scaled, axis=-1, keepdims=True)
        - standard * jnp.mean(scaled * standard, axis=-1, keepdims=True)
    )


def group_probs(query, tok, live_row, scale):
    size = tok.shape[0]
    row = lax.broadcasted_iota(jnp.int32, (size, size), 0) // BLOCK
    col = lax.broadcasted_iota(jnp.int32, (size, size), 1) // BLOCK
    scores = jnp.where(live_row > 0, mm_t(query, tok) * scale, MASKED)
    scores = jnp.where(row == col, scores, FAR)
    terms = jnp.exp(scores - jnp.max(scores, axis=-1, keepdims=True))
    return terms / jnp.sum(terms, axis=-1, keepdims=True), row == col


def merge_kernel(tok, live_row, live_col, merge_w, qkv_w, qkv_bias, query_out, hidden_out, attn_out, packed_out, squares):
    step = pl.program_id(0)
    scale = tok.shape[1] ** -0.5
    x = tok[...]
    live = live_col[...]
    query = mm(x, merge_w[...]).astype(BF16)
    query_out[...] = query
    probs, _ = group_probs(query, x, live_row[0], scale)
    merged = mm(probs.astype(BF16), x) * live
    wide = x.astype(F32)
    hidden = wide + merged
    hidden_out[...] = hidden
    attn_in = hidden.astype(BF16)
    attn_out[...] = attn_in
    packed_out[...] = (mm(attn_in, qkv_w[...]) + qkv_bias[...]).astype(BF16)

    @pl.when(step == 0)
    def _():
        squares[...] = jnp.zeros_like(squares)

    squares[0:1, :] += rowsum(live * wide * wide)
    squares[1:2, :] += rowsum(merged * merged)


def lane_mask(values, low, high):
    lane = lax.broadcasted_iota(jnp.int32, values.shape, 1)
    return jnp.where((lane >= low) & (lane < high), values, jnp.zeros_like(values))


def attn_kernel(scale, q_ref, k_ref, v_ref, bias_ref, ctx_ref, lse_ref):
    seq, lanes = q_ref.shape[1:]
    head = lanes // 2
    q = q_ref[0] * jnp.asarray(scale, BF16)
    k = k_ref[0]
    v_t = v_ref[0].T
    bias = bias_ref[0]
    for c in range(seq // TILE):
        rows = slice(c * TILE, (c + 1) * TILE)
        parts = []
        for h in range(2):
            scores = mm_t(k, lane_mask(q[rows], h * head, (h + 1) * head)) + bias
            top = jnp.max(scores, axis=0, keepdims=True)
            terms = jnp.exp(scores - top)
            total = jnp.sum(terms, axis=0, keepdims=True)
            probs = (terms * (1.0 / total)).astype(BF16)
            lse_ref[0, 0, h : h + 1, rows] = top + jnp.log(total)
            parts.append(mm(v_t[h * head : (h + 1) * head], probs))
        ctx_ref[0, rows, :] = jnp.concatenate(parts, axis=0).T.astype(BF16)


def attn_back_kernel(scale, q_ref, k_ref, v_ref, bias_ref, lse_ref, grad_ref, out_ref):
    seq, lanes = q_ref.shape[1:]
    head = lanes // 2
    q = q_ref[0] * jnp.asarray(scale, BF16)
    k = k_ref[0]
    v = v_ref[0]
    k_t = k.T
    bias = bias_ref[0]
    grad_k = jnp.zeros((seq, lanes), F32)
    grad_v = jnp.zeros((seq, lanes), F32)
    for c in range(seq // TILE):
        rows = slice(c * TILE, (c + 1) * TILE)
        parts = []
        for h in range(2):
            q_part = lane_mask(q[rows], h * head, (h + 1) * head)
            g_part = lane_mask(grad_ref[0, rows, :], h * head, (h + 1) * head)
            scores = mm_t(k, q_part) + bias
            probs = jnp.exp(scores - lse_ref[0, 0, h : h + 1, rows])
            grad_v += mm(probs.astype(BF16), g_part)
            grad_p = mm_t(v, g_part)
            grad_s = (probs * (grad_p - jnp.sum(probs * grad_p, axis=0, keepdims=True))).astype(BF16)
            grad_k += mm(grad_s, q_part)
            parts.append(mm(k_t[h * head : (h + 1) * head], grad_s))
        out_ref[0, 0, rows, :] = (jnp.concatenate(parts, axis=0).T * scale).astype(BF16)
    out_ref[1, 0] = grad_k.astype(BF16)
    out_ref[2, 0] = grad_v.astype(BF16)


def share_out(low, cols, value):
    rows = low.shape[4]
    spots = [(a, b, c, d) for a in range(low.shape[0]) for b in range(low.shape[1]) for c in range(low.shape[2]) for d in range(low.shape[3])]
    for i, spot in enumerate(spots):
        low[(*spot, slice(None), cols)] = value[i * rows : (i + 1) * rows].astype(BF16)


def attn_back_weights_kernel(
    scale, pairs, cuts, q, k, v, bias, lse, grad, ffn_in, grad_up, ctx, grad_attn, out_ref, low_up, low_out, turned
):
    step = pl.program_id(0) * pairs + pl.program_id(1)
    part = grad_up.shape[1]

    @pl.when(step == 0)
    def _():
        turned[...] = ffn_in[...].T

    @pl.when(step < cuts)
    def _():
        cols = pl.ds(pl.multiple_of(step * part, part), part)
        share_out(low_up, cols, mm(turned[...], grad_up[...]))

    @pl.when(step == cuts)
    def _():
        share_out(low_out, slice(None), mm(ctx[...].T, grad_attn[...]))

    attn_back_kernel(scale, q, k, v, bias, lse, grad, out_ref)


def qkv_grad_kernel(attn_in, grad, weight_grad, sums, turned):
    @pl.when(pl.program_id(0) == 0)
    def _():
        turned[...] = attn_in[...].T

    piece = grad[0]
    weight_grad[...] = mm(turned[...], piece).astype(BF16)
    sums[...] = jnp.broadcast_to(rowsum(piece.astype(F32)), sums.shape)


def ffn_kernel(
    per_row,
    ctx,
    hidden,
    cot,
    cls_grad,
    live_col,
    out_w,
    up_w,
    down_w,
    vecs,
    layer_out,
    activated,
    grad_up,
    ffn_in_out,
    grad_down_out,
    grad_attn_out,
    grad_two_out,
    grad_ctx_out,
    sums,
    up_sums,
    slope,
):
    step = pl.program_id(0)
    width = hidden.shape[1]
    chunks = up_w.shape[1] // width

    @pl.when(step == 0)
    def _():
        sums[...] = jnp.zeros_like(sums)
        up_sums[...] = jnp.zeros_like(up_sums)

    live = live_col[...]
    out_bias, gain_one, shift_one, down_bias, gain_two, shift_two = (vecs[i : i + 1, :width] for i in range(6))
    branch = mm(ctx[...], out_w[...]) + out_bias
    norm_one, standard_one, inv_one = norm_forward(hidden[...] + branch, gain_one, shift_one)
    ffn_in = norm_one.astype(BF16)
    ffn_in_out[...] = ffn_in
    down = jnp.zeros_like(norm_one)
    for j in range(chunks):
        cols = slice(j * width, (j + 1) * width)
        pre = mm(ffn_in, up_w[:, cols]) + vecs[6:7, cols]
        cumulative = 0.5 * (1.0 + lax.erf(pre * 0.7071067811865476))
        act = (pre * cumulative).astype(BF16)
        slope[:, cols] = cumulative + pre * (jnp.exp(-0.5 * pre * pre) * 0.3989422804014327)
        activated[:, cols] = act
        down += mm(act, down_w[cols, :])
    down += down_bias
    normed, standard_two, inv_two = norm_forward(norm_one + down, gain_two, shift_two)
    result = (normed * live).astype(BF16)
    layer_out[...] = result
    wide = result.astype(F32)
    sums[5:6, :] += rowsum(live * branch * branch)
    sums[6:7, :] += rowsum(live * down * down)
    sums[7:8, :] += rowsum(wide * wide)
    first = (lax.broadcasted_iota(jnp.int32, (hidden.shape[0], 1), 0) == 0) & (step % per_row == 0)
    grad = live * (cot[...].astype(F32) + jnp.where(first, cls_grad[0], 0.0))
    sums[0:1, :] += rowsum(grad * standard_two)
    sums[1:2, :] += rowsum(grad)
    grad_three = norm_backward(grad, standard_two, inv_two, gain_two)
    grad_down = grad_three.astype(BF16)
    grad_down_out[...] = grad_down
    sums[2:3, :] += rowsum(grad_down.astype(F32))
    total = grad_three
    for j in range(chunks):
        cols = slice(j * width, (j + 1) * width)
        piece = (mm_t(grad_down, down_w[cols, :]) * slope[:, cols]).astype(BF16)
        grad_up[:, cols] = piece
        up_sums[0:1, cols] += rowsum(piece.astype(F32))
        total += mm_t(piece, up_w[:, cols])
    sums[3:4, :] += rowsum(total * standard_one)
    sums[4:5, :] += rowsum(total)
    grad_two = norm_backward(total, standard_one, inv_one, gain_one)
    grad_two_out[...] = grad_two
    grad_attn = grad_two.astype(BF16)
    grad_attn_out[...] = grad_attn
    sums[8:9, :] += rowsum(grad_attn.astype(F32))
    grad_ctx_out[...] = mm_t(grad_attn, out_w[...]).astype(BF16)


def input_kernel(
    grad_qkv, grad_two, tok, query, live_row, live_col, merge_w, qkv_w, grad_input, merge_grad
):
    step = pl.program_id(0)
    width = tok.shape[1]
    scale = width**-0.5

    @pl.when(step == 0)
    def _():
        merge_grad[...] = jnp.zeros_like(merge_grad)

    x = tok[...]
    grad_one = grad_two[...]
    for i in range(3):
        cols = slice(i * width, (i + 1) * width)
        grad_one += mm_t(grad_qkv[i], qkv_w[:, cols])
    grad_merged = (grad_one * live_col[...]).astype(BF16)
    mq = query[...]
    probs, same = group_probs(mq, x, live_row[0], scale)
    grad_probs = mm_t(grad_merged, x)
    grad_scores = probs * (grad_probs - jnp.sum(probs * grad_probs, axis=-1, keepdims=True))
    grad_scores = jnp.where(same & (live_row[0] > 0), grad_scores, 0.0)
    grad_query = (mm(grad_scores.astype(BF16), x) * scale).astype(BF16)
    merge_grad[...] += mm(x.T, grad_query)
    blocks = mm(probs.T.astype(BF16), grad_merged) + mm(grad_scores.T.astype(BF16), mq) * scale
    blocks += mm_t(grad_query, merge_w[...])
    grad_input[...] = (grad_one + blocks).astype(BF16)


def params(**kw):
    return pltpu.CompilerParams(vmem_limit_bytes=VMEM_BYTES, **kw)


def fixed(shape):
    zeros = (0,) * len(shape)
    return pl.BlockSpec(shape, lambda *_: zeros, pipeline_mode=pl.Buffered(1))


def tiled(size, width):
    return pl.BlockSpec((size, width), lambda i: (i, 0))


MESH = pl.DeviceIdType.MESH
TABLE_MAJOR = 4
UP_CUTS = 6
CORES = 2


def here(dims):
    table, batch = lax.axis_index("table"), lax.axis_index("batch")
    return [table // dims[1], lax.rem(table, dims[1]), batch // CORES, lax.rem(batch, CORES)]


def peer(dims, spot, axis, offset):
    other = list(spot)
    other[axis] = lax.rem(spot[axis] + offset, dims[axis])
    return (other[0] * dims[1] + other[1], other[2] * CORES + other[3]), other[axis]


def greet(dims, spot):
    barrier = pltpu.get_barrier_semaphore()
    total = 0
    for axis in range(4):
        for offset in range(1, dims[axis]):
            target, _ = peer(dims, spot, axis, offset)
            pl.semaphore_signal(barrier, inc=1, device_id=target, device_id_type=MESH)
            total += 1
    pl.semaphore_wait(barrier, total)


def gather_events(dims, spot, items, shards, fulls, local_sem, send_sem, recv_sem):
    def region(item, done):
        array, low, size, order = items[item]
        where = tuple(slice(None) if axis in done else spot[axis] for axis in sorted(order))
        return fulls[array].at[(*where, pl.ds(low, size))]

    def copies(item, stage):
        array, low, size, order = items[item]
        place = region(item, order[:stage])
        return [
            pltpu.make_async_remote_copy(
                src_ref=place if stage else shards[array].at[pl.ds(low, size)],
                dst_ref=place,
                send_sem=send_sem.at[item, stage, offset],
                recv_sem=recv_sem.at[item, stage, offset],
                device_id=peer(dims, spot, order[stage], offset)[0],
                device_id_type=MESH,
            )
            for offset in range(1, dims[order[stage]])
        ]

    def keep(item):
        array, low, size, _ = items[item]
        return pltpu.make_async_copy(shards[array].at[pl.ds(low, size)], region(item, ()), local_sem.at[item])

    def begin():
        for item in range(len(items)):
            keep(item).start()
            for copy in copies(item, 0):
                copy.start()

    def advance(item, stage):
        for copy in copies(item, stage):
            copy.wait_recv()
        if stage == 0:
            keep(item).wait()
        if stage + 1 < len(items[item][3]):
            for copy in copies(item, stage + 1):
                copy.start()

    def end():
        for item in range(len(items)):
            for stage in range(len(items[item][3])):
                for copy in copies(item, stage):
                    copy.wait_send()

    return begin, slots(items, advance), end


def slots(items, advance):
    count = len(items)
    pairs = (count + 1) // 2
    groups = []
    for slot in range(pairs + 3):
        group = []
        for stage in (3, 2, 1, 0):
            pair = slot - stage
            for item in range(2 * pair, min(2 * pair + 2, count)) if 0 <= pair < pairs else ():
                if stage < len(items[item][3]):
                    group.append(functools.partial(advance, item, stage))
        groups.append(group)
    return groups


def scatter_events(dims, spot, items, grads, outs, buffers, local_sem, send_sem, recv_sem):
    buffers = [buffers[i * 7 : (i + 1) * 7] for i in range(len(items))]

    def piece(item, core):
        array, low, size, _ = items[item]
        if size <= grads[array].shape[4]:
            return grads[array].at[:, :, :, core, pl.ds(low, size)]
        return grads[array].at[:, :, :, core, :, pl.ds(low, size)]

    def load(item):
        return pltpu.make_async_copy(
            piece(item, spot[3]), buffers[item][0], local_sem.at[item]
        )

    def copies(item, stage):
        array, low, size, order = items[item]
        own, first, second, got_core, got_first, got_second, got_last = buffers[item]
        axis = order[stage]
        made = []
        for offset in range(1, dims[axis]):
            target, other = peer(dims, spot, axis, offset)
            if stage == 0:
                source, landing = piece(item, other), got_core
            elif stage == 1:
                source = own.at[:, :, other] if axis == 2 else own.at[:, other]
                landing = got_first.at[offset - 1]
            elif stage == 2:
                source, landing = first.at[:, other], got_second.at[offset - 1]
            else:
                source, landing = second.at[other], got_last.at[offset - 1]
            made.append(
                pltpu.make_async_remote_copy(
                    src_ref=source,
                    dst_ref=landing,
                    send_sem=send_sem.at[item, stage, offset],
                    recv_sem=recv_sem.at[item, stage, offset],
                    device_id=target,
                    device_id_type=MESH,
                )
            )
        return made

    def begin(chosen=tuple(range(len(items)))):
        for item in chosen:
            load(item).start()
            for copy in copies(item, 0):
                copy.start()

    def advance(item, stage):
        array, low, size, order = items[item]
        own, first, second, got_core, got_first, got_second, got_last = buffers[item]
        axis = order[stage]
        others = range(dims[axis] - 1)
        mine = spot[axis]
        for copy in copies(item, stage):
            copy.wait_recv()
        if stage == 0:
            load(item).wait()

            @pl.loop(0, dims[0] * dims[1] * dims[2])
            def _(i):
                at = (i // (dims[1] * dims[2]), lax.rem(i // dims[2], dims[1]), lax.rem(i, dims[2]))
                own[at] = (own[at].astype(F32) + got_core[at].astype(F32)).astype(BF16)
        elif stage == 1:
            inner = first.shape[1]

            @pl.loop(0, dims[0] * inner)
            def _(i):
                at = (i // inner, lax.rem(i, inner))
                value = own[(*at, mine) if axis == 2 else (at[0], mine, at[1])].astype(F32)
                for k in others:
                    value += got_first[(k, *at)].astype(F32)
                first[at] = value.astype(BF16)
        elif stage == 2:

            @pl.loop(0, dims[0])
            def _(i):
                value = first[i, mine].astype(F32)
                for k in others:
                    value += got_second[k, i].astype(F32)
                second[i] = value.astype(BF16)
        else:
            value = second[mine].astype(F32)
            for k in others:
                value += got_last[k].astype(F32)
            if size <= grads[array].shape[4]:
                outs[array][low : low + size] = value
            else:
                outs[array][:, low : low + size] = value
        if stage < 3:
            for copy in copies(item, stage + 1):
                copy.start()

    def end():
        for item in range(len(items)):
            for stage in range(4):
                for copy in copies(item, stage):
                    copy.wait_send()

    return begin, slots(items, advance), end


def square_events(dims, spot, square, total, kept, got, send_sem, recv_sem):
    def copies(stage):
        axis = 3 - stage
        return [
            pltpu.make_async_remote_copy(
                src_ref=kept.at[stage],
                dst_ref=got.at[stage, offset - 1],
                send_sem=send_sem.at[stage, offset],
                recv_sem=recv_sem.at[stage, offset],
                device_id=peer(dims, spot, axis, offset)[0],
                device_id_type=MESH,
            )
            for offset in range(1, dims[axis])
        ]

    def begin():
        kept[0] = square[...]
        for copy in copies(0):
            copy.start()

    def advance(stage):
        for copy in copies(stage):
            copy.wait_recv()
        value = kept[stage]
        for offset in range(1, dims[3 - stage]):
            value = value + got[stage, offset - 1]
        kept[stage + 1] = value
        if stage < 3:
            for copy in copies(stage + 1):
                copy.start()
        else:
            total[...] = value

    def end():
        for stage in range(4):
            for copy in copies(stage):
                copy.wait_send()

    return begin, [[functools.partial(advance, stage)] for stage in range(4)], end


def scatter_scratch(dims, grads, items):
    scratch = []
    for array, _, size, order in items:
        rows, cols = grads[array].shape[4:]
        tail = (size, cols) if size <= rows else (rows, size)
        inner = dims[order[2]]
        for shape in (
            dims[:3],
            (dims[0], inner),
            (dims[0],),
            dims[:3],
            (dims[order[1]] - 1, dims[0], inner),
            (inner - 1, dims[0]),
            (dims[0] - 1,),
        ):
            scratch.append(pltpu.VMEM((*shape, *tail), BF16))
    return scratch


def links(count, most):
    return [pltpu.SemaphoreType.DMA((count, 4, most)), pltpu.SemaphoreType.DMA((count, 4, most))]


def split(array, size, pieces, *orders):
    part = size // pieces
    return [(array, i * part, part, orders[i % len(orders)]) for i in range(pieces)]


def plain_call(kernel, grid, refs, outs, name):
    return pl.pallas_call(
        kernel,
        grid=grid,
        in_specs=[spec for spec, _ in refs],
        out_specs=[spec for spec, _ in outs],
        out_shape=[shape for _, shape in outs],
        compiler_params=params(),
        name=name,
    )(*(arg for _, arg in refs))


def moving_call(dims, collective_id, name, kernel, grid, own_in, own_out, gather, scatter, square, pace=1.0, made=(), early=(), after=None, extra=()):
    most = max(dims)
    total = dims[0] * dims[1] * dims[2] * dims[3]
    vmem, anywhere = (lambda a: fixed(a.shape)), (lambda a: pl.BlockSpec(memory_space=pl.ANY))
    shards, gather_items = gather
    grads, scatter_items = scatter
    squares = [] if square is None else [square]
    in_specs, args = [spec for spec, _ in own_in], [arg for _, arg in own_in]
    in_specs += [vmem(a) for a in shards] + [anywhere(a) for a in grads] + [vmem(a) for a in squares]
    args += [*shards, *grads, *squares]
    out_specs, out_shape = [spec for spec, _ in own_out], [shape for _, shape in own_out]
    orders = {array: sorted(order) for array, _, _, order in gather_items}
    for i, a in enumerate(shards):
        out_specs.append(anywhere(a))
        out_shape.append(jax.ShapeDtypeStruct((*(dims[axis] for axis in orders[i]), *a.shape), a.dtype))
    whole = [*grads, *early]
    after = after or {}
    for g in whole:
        out_shape.append(jax.ShapeDtypeStruct(g.shape[4:], F32))
        out_specs.append(vmem(out_shape[-1]))
    for g in made:
        out_shape.append(jax.ShapeDtypeStruct((g.shape[0] // total, g.shape[1]), F32))
        out_specs.append(vmem(out_shape[-1]))
    for q in squares:
        out_shape.append(jax.ShapeDtypeStruct(q.shape, F32))
        out_specs.append(vmem(q))
    groups = []
    if shards:
        groups.append([pltpu.SemaphoreType.DMA((len(gather_items),)), *links(len(gather_items), most)])
    if grads:
        buffers = scatter_scratch(dims, whole, scatter_items)
        groups.append([*extra, *(pltpu.VMEM(g.shape, BF16) for g in early), *buffers, pltpu.SemaphoreType.DMA((len(scatter_items),)), *links(len(scatter_items), most)])
    if squares:
        groups.append(
            [
                pltpu.VMEM((5, *square.shape), F32),
                pltpu.VMEM((4, most - 1, *square.shape), F32),
                pltpu.SemaphoreType.DMA((4, most)),
                pltpu.SemaphoreType.DMA((4, most)),
            ]
        )
    if made:
        made_shapes = [jax.ShapeDtypeStruct((*dims, g.shape[0] // total, g.shape[1]), BF16) for g in made]
        made_items = [(i, 0, g.shape[4], (3, 2, 1, 0) if i % 2 == 0 else (3, 1, 2, 0)) for i, g in enumerate(made_shapes)]
        buffers = [pltpu.VMEM(g.shape, F32) for g in made] + [pltpu.VMEM(g.shape, BF16) for g in made_shapes]
        buffers += scatter_scratch(dims, made_shapes, made_items)
        groups.append([*buffers, pltpu.SemaphoreType.DMA((len(made),)), *links(len(made), most)])
    steps = 1
    for size in grid:
        steps *= size

    def fused(*refs):
        refs = list(refs)

        def take(n):
            taken = refs[:n]
            del refs[:n]
            return taken

        ins, shard_refs, grad_refs, square_refs = take(len(own_in)), take(len(shards)), take(len(grads)), take(len(squares))
        outs, full_refs, sum_refs = take(len(own_out)), take(len(shards)), take(len(whole))
        made_outs, total_refs = take(len(made)), take(len(squares))
        step = 0
        for axis, size in enumerate(grid):
            step = step * size + pl.program_id(axis)
        spot = here(dims)
        plans = []
        scratch = iter(groups)
        if shards:
            plans.append(gather_events(dims, spot, gather_items, shard_refs, full_refs, *take(len(next(scratch)))))
        if grads:
            held = take(len(next(scratch)))
            turned, held = held[: len(extra)], held[len(extra) :]
            early_refs, held = held[: len(early)], held[len(early) :]
            begin_some, some_groups, end_some = scatter_events(
                dims, spot, scatter_items, grad_refs + early_refs, sum_refs, held[:-3], *held[-3:]
            )
            ready = [item for item in range(len(scatter_items)) if item not in after]
            plans.append((functools.partial(begin_some, ready), some_groups, end_some))
        else:
            turned, early_refs = [], []
        if squares:
            plans.append(square_events(dims, spot, *square_refs, *total_refs, *take(len(next(scratch)))))

        if made:
            held = take(len(next(scratch)))
            sums, lows = held[: len(made)], held[len(made) : 2 * len(made)]
            begin_made, made_groups, end_made = scatter_events(
                dims, spot, made_items, lows, made_outs, held[2 * len(made) : -3], *held[-3:]
            )
        else:
            sums, made_groups = [], []

        def round_made():
            for value, low in zip(sums, lows):
                rows = low.shape[4]

                @pl.loop(0, total)
                def _(i):
                    at = (
                        i // (dims[1] * dims[2] * dims[3]),
                        lax.rem(i // (dims[2] * dims[3]), dims[1]),
                        lax.rem(i // dims[3], dims[2]),
                        lax.rem(i, dims[3]),
                    )
                    low[at] = value[pl.ds(pl.multiple_of(i * rows, rows), rows), :].astype(BF16)

        def open_all():
            greet(dims, spot)
            for begin, _, _ in plans:
                begin()

        depth = max(len(groups_of) for _, groups_of, _ in plans)
        merged = [[e for _, groups_of, _ in plans if i < len(groups_of) for e in groups_of[i]] for i in range(depth)]

        def close_all():
            for _, _, end in plans:
                end()

        if steps == 1:
            open_all()
            for group in merged:
                for event in group:
                    event()
            close_all()
            return
        late = []
        pl.when(step == 0)(open_all)
        for i, group in enumerate(merged):
            at = int((i + 1) * pace)

            def run(group=group):
                for event in group:
                    event()

            if at < steps:
                pl.when(step == at)(run)
            else:
                late.append(run)
        kernel(*ins, *outs, *sums, *early_refs, *turned)
        for item, at in after.items():
            pl.when(step == at)(functools.partial(begin_some, (item,)))

        @pl.when(step == steps - 1)
        def _():
            if made:
                round_made()
                begin_made()
            for i in range(max(len(late), len(made_groups))):
                if i < len(late):
                    late[i]()
                for event in made_groups[i] if i < len(made_groups) else ():
                    event()
            close_all()
            if made:
                end_made()

    return pl.pallas_call(
        fused,
        grid=grid,
        in_specs=in_specs,
        out_specs=out_specs,
        out_shape=out_shape,
        scratch_shapes=[piece for group in groups for piece in group],
        compiler_params=params(collective_id=collective_id, has_side_effects=True),
        name=name,
    )(*args)


def body(
    tokens,
    row_blocks,
    block_fill,
    row_table,
    class_count,
    merge_w,
    qkv_w,
    query_bias,
    value_bias,
    out_w,
    out_bias,
    gain_one,
    shift_one,
    up_w,
    up_bias,
    down_w,
    down_bias,
    gain_two,
    shift_two,
    head_w,
    cotangent,
    logit_cotangent,
):
    rows, seq, width = tokens.shape
    count = rows * seq
    ff = up_w.shape[1]
    head = width // HEADS
    per_row = seq // TILE
    tiles = count // TILE
    share = merge_w.shape[0]
    devices = width // share
    wide_ff = ff // width

    def cut(mat, n):
        return [mat[:, i * width : (i + 1) * width] for i in range(n)]

    table_size, batch_size = lax.axis_size("table"), lax.axis_size("batch")
    dims = (TABLE_MAJOR, table_size // TABLE_MAJOR, batch_size // CORES, CORES)
    direct = share % BLOCK == 0
    vec_list = (out_bias, gain_one, shift_one, down_bias, gain_two, shift_two, query_bias, value_bias)
    vec_row = jnp.concatenate([*vec_list, up_bias])
    used = vec_row.shape[0]
    vec_row = jnp.pad(vec_row, (0, 8 * width - used)).reshape(8, width)
    base = (5 + wide_ff) * share
    down_out, up_out = (0, 1, 2, 3), (0, 2, 1, 3)
    down_in, up_in = (3, 1, 2, 0), (3, 2, 1, 0)
    none = ((), ())
    if direct:
        qkv_full, merge_full, vec_full = moving_call(
            dims,
            0,
            "gather_first",
            None,
            (1,),
            [],
            [],
            (
                (qkv_w, merge_w, vec_row),
                (
                    (1, 0, share, down_out),
                    *split(0, share, 3, up_out, down_out),
                    (2, 0, 8, up_out),
                ),
            ),
            none,
            None,
        )
        qkv_full = qkv_full.reshape(width, 3 * width)
        merge_full = merge_full.reshape(width, width)
        vec_rows = vec_full.reshape(devices, 8, width)[:, 0].astype(F32)
    else:
        mine = jnp.concatenate([merge_w, out_w, *cut(qkv_w, 3), *cut(up_w, wide_ff), down_w, vec_row], axis=0)
        gathered = lax.all_gather(mine, BOTH, axis=0)

        def unit(start, n):
            part = gathered[:, start : start + n * share]
            part = part.reshape(devices, n, share, width).transpose(0, 2, 1, 3)
            return part.reshape(width, n * width)

        merge_full = unit(0, 1)
        out_full = unit(share, 1)
        qkv_full = unit(2 * share, 3)
        up_full = unit(5 * share, wide_ff)
        down_full = gathered[:, base : base + wide_ff * share].reshape(ff, width)
        vec_rows = gathered[:, base + wide_ff * share].astype(F32)
    vectors = [vec_rows[:, i * share : (i + 1) * share].reshape(1, width) for i in range(8)]
    up_bias_full = vec_rows[:, 8 * share : 8 * share + wide_ff * share].reshape(1, ff)
    query_vec, value_vec = vectors[6], vectors[7]
    qkv_bias = jnp.concatenate([query_vec, jnp.zeros_like(query_vec), value_vec], axis=1)
    vecs = jnp.concatenate(
        [jnp.pad(jnp.concatenate(vectors[:6], axis=0), ((0, 0), (0, ff - width))), up_bias_full, jnp.zeros((1, ff), F32)],
        axis=0,
    )

    position = jnp.arange(seq, dtype=jnp.int32)
    fill_tok = jnp.repeat(block_fill, BLOCK, axis=1)
    live = ((position // BLOCK)[None, :] < row_blocks[:, None]) & ((position % BLOCK)[None, :] < fill_tok)
    live_mask = live.astype(F32)
    live_col = live_mask.reshape(count, 1)
    live_row = live_mask.reshape(tiles, 1, TILE)
    key_bias = jnp.where(live, 0.0, MASKED).astype(F32).reshape(rows, seq, 1)

    batch = lax.axis_size("batch")
    classes = head_w.shape[2]
    tok_flat = tokens.reshape(count, width)
    cot_flat = cotangent.reshape(count, width)
    merge_query, hidden, attn_in, packed, squares = pl.pallas_call(
        merge_kernel,
        grid=(tiles,),
        in_specs=[
            tiled(TILE, width),
            pl.BlockSpec((1, 1, TILE), lambda i: (i, 0, 0)),
            tiled(TILE, 1),
            fixed((width, width)),
            fixed((width, 3 * width)),
            fixed((1, 3 * width)),
        ],
        out_specs=[
            tiled(TILE, width),
            tiled(TILE, width),
            tiled(TILE, width),
            tiled(TILE, 3 * width),
            fixed((8, width)),
        ],
        out_shape=[
            jax.ShapeDtypeStruct((count, width), BF16),
            jax.ShapeDtypeStruct((count, width), F32),
            jax.ShapeDtypeStruct((count, width), BF16),
            jax.ShapeDtypeStruct((count, 3 * width), BF16),
            jax.ShapeDtypeStruct((8, width), F32),
        ],
        compiler_params=params(),
        name="merge_qkv",
    )(tok_flat, live_row, live_col, merge_full, qkv_full, qkv_bias)

    packed_rows = packed.reshape(rows, seq, 3 * width)
    pairs = HEADS // 2
    lanes = 2 * head

    def head_block(offset):
        return pl.BlockSpec((1, seq, lanes), lambda r, p: (r, 0, p + offset))

    bias_block = pl.BlockSpec((1, seq, 1), lambda r, p: (r, 0, 0))
    lse_block = pl.BlockSpec((1, 1, 2, seq), lambda r, p: (r, p, 0, 0))
    attn_in_refs = [
        (head_block(0), packed_rows),
        (head_block(pairs), packed_rows),
        (head_block(2 * pairs), packed_rows),
        (bias_block, key_bias),
    ]
    attn_outs = [
        (head_block(0), jax.ShapeDtypeStruct((rows, seq, width), BF16)),
        (lse_block, jax.ShapeDtypeStruct((rows, pairs, 2, seq), F32)),
    ]
    attend = functools.partial(attn_kernel, head**-0.5)
    if direct:
        limit = jnp.broadcast_to(class_count.astype(F32)[:, None], (1, classes))
        spare = -(rows + 1) % 8
        small = jnp.concatenate([logit_cotangent, limit, jnp.zeros((spare, classes), F32)], axis=0)
        gather_items = [(3, 0, width, (2, 3)), (4, 0, small.shape[0], (2, 3))]
        up_items, down_items = split(0, share, 3, up_out), split(1, wide_ff * share, 3, down_out)
        for pair in zip(up_items, down_items):
            gather_items += pair
        gather_items.append((2, 0, share, down_out))
        context, lse, up_full, down_full, out_full, heads, small = moving_call(
            dims,
            2,
            "attention_gather",
            attend,
            (rows, pairs),
            attn_in_refs,
            attn_outs,
            ((up_w, down_w, out_w, head_w[0], small), gather_items),
            none,
            None,
            pace=2.2,
        )
        up_full = up_full.reshape(width, ff)
        down_full = down_full.reshape(ff, width)
        out_full = out_full.reshape(width, width)
        heads = heads.reshape(batch, width, classes)
        small = small.reshape(batch, -1, classes)
        group_dlog_raw = small[:, :rows].reshape(batch * rows, classes)
        counts = small[:, rows, 0]
    else:
        context, lse = pl.pallas_call(
            attend,
            grid=(rows, pairs),
            in_specs=[spec for spec, _ in attn_in_refs],
            out_specs=[spec for spec, _ in attn_outs],
            out_shape=[shape for _, shape in attn_outs],
            compiler_params=params(),
            name="attention",
        )(*(arg for _, arg in attn_in_refs))
        heads = lax.all_gather(head_w[0], "batch", axis=0)
        counts = lax.all_gather(class_count, "batch", axis=0, tiled=True)
        group_dlog_raw = lax.all_gather(logit_cotangent, "batch", axis=0, tiled=True)
    own = lax.axis_index("batch")
    my_table = lax.dynamic_slice(row_table, (own * rows,), (rows,))
    class_ids = jnp.arange(classes, dtype=jnp.int32)
    my_select = (my_table[:, None] == jnp.arange(batch, dtype=jnp.int32)[None, :]).astype(F32)
    my_class = (class_ids[None, :] < (my_select * counts[None, :].astype(F32)).sum(1, keepdims=True)).astype(F32)
    my_dlog = logit_cotangent * my_class
    picked = (my_select[:, :, None] * my_dlog[:, None, :]).transpose(1, 0, 2)
    cls_grad = jnp.sum(
        lax.dot_general(picked, heads.astype(F32), (((2,), (2,)), ((0,), (0,))), precision=PRECISE), axis=0
    )

    context = context.reshape(count, width)
    (layer_out, activated, grad_up, ffn_in, grad_down, grad_attn, grad_two, grad_ctx, sums, up_sums) = pl.pallas_call(
        functools.partial(ffn_kernel, per_row),
        grid=(tiles,),
        in_specs=[
            tiled(TILE, width),
            tiled(TILE, width),
            tiled(TILE, width),
            pl.BlockSpec((1, 1, width), lambda i: (i // per_row, 0, 0)),
            tiled(TILE, 1),
            fixed((width, width)),
            fixed((width, ff)),
            fixed((ff, width)),
            fixed((8, ff)),
        ],
        out_specs=[
            tiled(TILE, width),
            tiled(TILE, ff),
            tiled(TILE, ff),
            tiled(TILE, width),
            tiled(TILE, width),
            tiled(TILE, width),
            tiled(TILE, width),
            tiled(TILE, width),
            fixed((16, width)),
            fixed((8, ff)),
        ],
        out_shape=[
            jax.ShapeDtypeStruct((count, width), BF16),
            jax.ShapeDtypeStruct((count, ff), BF16),
            jax.ShapeDtypeStruct((count, ff), BF16),
            jax.ShapeDtypeStruct((count, width), BF16),
            jax.ShapeDtypeStruct((count, width), BF16),
            jax.ShapeDtypeStruct((count, width), BF16),
            jax.ShapeDtypeStruct((count, width), F32),
            jax.ShapeDtypeStruct((count, width), BF16),
            jax.ShapeDtypeStruct((16, width), F32),
            jax.ShapeDtypeStruct((8, ff), F32),
        ],
        scratch_shapes=[pltpu.VMEM((TILE, ff), F32)],
        compiler_params=params(),
        name="ffn",
    )(context, hidden, cot_flat, cls_grad.reshape(rows, 1, width), live_col, out_full, up_full, down_full, vecs)

    grad_rows = grad_ctx.reshape(rows, seq, width)
    cls_rows = layer_out.reshape(rows, seq, width)[:, 0, :]
    back_refs = [*attn_in_refs, (lse_block, lse), (head_block(0), grad_rows)]
    back_outs = [
        (
            pl.BlockSpec((3, 1, seq, lanes), lambda r, p: (0, r, 0, p)),
            jax.ShapeDtypeStruct((3, rows, seq, width), BF16),
        )
    ]
    grad_down_w = t_mm(activated, grad_down).astype(BF16)
    if direct:
        part = ff // UP_CUTS
        back_refs += [
            (fixed((count, width)), ffn_in),
            (pl.BlockSpec((count, part), lambda r, p: (0, jnp.minimum(r * pairs + p, UP_CUTS - 1))), grad_up),
            (fixed((count, width)), context),
            (fixed((count, width)), grad_attn),
        ]
        ffn_items = [
            *split(0, wide_ff * share, 3, up_in, down_in),
            *split(1, ff, 3, down_in, up_in),
            (2, 0, share, up_in),
        ]
        first_rows = jnp.pad(cls_rows, ((0, -rows % 8), (0, 0)))
        grad_qkv, group_cls, own_down, own_up, own_out = moving_call(
            dims,
            3,
            "attention_back_scatter",
            functools.partial(attn_back_weights_kernel, head**-0.5, pairs, UP_CUTS),
            (rows, pairs),
            back_refs,
            back_outs,
            ((first_rows,), ((0, 0, first_rows.shape[0], (2, 3)),)),
            ([grad_down_w.reshape(*dims, -1, width)], ffn_items),
            None,
            pace=2.4,
            early=(jax.ShapeDtypeStruct((*dims, share, ff), BF16), jax.ShapeDtypeStruct((*dims, share, width), BF16)),
            after={3: UP_CUTS // 3 - 1, 4: 2 * UP_CUTS // 3 - 1, 5: UP_CUTS - 1, 6: UP_CUTS},
            extra=(pltpu.VMEM((width, count), BF16),),
        )
        group_cls = group_cls.reshape(batch, -1, width)[:, :rows].reshape(batch * rows, width)
    else:
        grad_out_w = t_mm(context, grad_attn).astype(BF16)
        grad_up_w = t_mm(ffn_in, grad_up).astype(BF16)
        attend_back = functools.partial(attn_back_kernel, head**-0.5)
        (grad_qkv,) = plain_call(attend_back, (rows, pairs), back_refs, back_outs, "attention_back")
        group_cls = lax.all_gather(cls_rows, "batch", axis=0, tiled=True)

    grad_qkv = grad_qkv.reshape(3, count, width)
    grad_qkv_w, qkv_sums = pl.pallas_call(
        qkv_grad_kernel,
        grid=(3,),
        in_specs=[fixed((count, width)), pl.BlockSpec((1, count, width), lambda i: (i, 0, 0))],
        out_specs=[pl.BlockSpec((width, width), lambda i: (0, i)), pl.BlockSpec((8, width), lambda i: (0, i))],
        out_shape=[jax.ShapeDtypeStruct((width, 3 * width), BF16), jax.ShapeDtypeStruct((8, 3 * width), F32)],
        scratch_shapes=[pltpu.VMEM((width, count), BF16)],
        compiler_params=params(),
        name="qkv_grad",
    )(attn_in, grad_qkv)
    bias_sums = [qkv_sums[0, :width], qkv_sums[0, 2 * width :]]
    input_refs = [
        (pl.BlockSpec((3, TILE, width), lambda i: (0, i, 0)), grad_qkv),
        *((tiled(TILE, width), a) for a in (grad_two, tok_flat, merge_query)),
        (pl.BlockSpec((1, 1, TILE), lambda i: (i, 0, 0)), live_row),
        (tiled(TILE, 1), live_col),
        (fixed((width, width)), merge_full),
        (fixed((width, 3 * width)), qkv_full),
    ]
    input_outs = [(tiled(TILE, width), jax.ShapeDtypeStruct((count, width), BF16))]
    merge_grad = jax.ShapeDtypeStruct((width, width), F32)

    vec_grads = (sums[8], sums[3], sums[4], sums[2], sums[0], sums[1], bias_sums[0], bias_sums[1])
    vec_block = jnp.concatenate(
        [v.reshape(devices, share) for v in vec_grads] + [up_sums[0].reshape(devices, wide_ff * share)], axis=1
    )
    vec_block = jnp.pad(vec_block, ((0, 0), (0, 8 * width - used))).astype(BF16).reshape(devices, 8, width)
    partial = jnp.stack(
        [
            jnp.sum(squares[0]),
            jnp.sum(squares[1]),
            jnp.sum(sums[5]),
            jnp.sum(sums[6]),
            jnp.sum(sums[7]),
            jnp.sum(live_mask),
        ]
    )
    if direct:
        square = jnp.broadcast_to(jnp.pad(partial, (0, 2))[:, None], (8, 128))
        grad_input, own_qkv, own_vec, own_merge, square = moving_call(
            dims,
            1,
            "merge_back_scatter",
            input_kernel,
            (tiles,),
            input_refs,
            input_outs,
            none,
            (
                [g.reshape(*dims, -1, g.shape[-1]) for g in (grad_qkv_w, vec_block)],
                (*split(0, share, 3, up_in, down_in), (1, 0, 8, down_in)),
            ),
            square,
            made=(merge_grad,),
        )
        own_vec = own_vec[0]
        totals = square[:6, 0]
    else:
        input_outs.append((fixed((width, width)), merge_grad))
        grad_input, grad_merge_w = plain_call(input_kernel, (tiles,), input_refs, input_outs, "merge_back")
        grad_merge_w = grad_merge_w.astype(BF16)

        def owners(mat, n):
            return mat.reshape(devices, share, n, width).transpose(0, 2, 1, 3).reshape(devices, n * share, width)


        all_grads = jnp.concatenate(
            [
                owners(grad_merge_w, 1),
                owners(grad_out_w, 1),
                owners(grad_qkv_w, 3),
                owners(grad_up_w, wide_ff),
                grad_down_w.reshape(devices, wide_ff * share, width),
                vec_block,
            ],
            axis=1,
        )
        owned = lax.psum_scatter(all_grads, BOTH, scatter_dimension=0, tiled=True)[0].astype(F32)

        def joined(start, n):
            return jnp.concatenate([owned[start + i * share : start + (i + 1) * share] for i in range(n)], axis=1)

        own_vec = owned[base + wide_ff * share]
        own_merge, own_qkv, own_out, own_up = joined(0, 1), joined(2 * share, 3), joined(share, 1), joined(5 * share, wide_ff)
        own_down = owned[base : base + wide_ff * share]
        totals = lax.psum(partial, BOTH)
    own_vecs = [own_vec[i * share : (i + 1) * share] for i in range(8)]
    own_up_bias = own_vec[8 * share : 8 * share + wide_ff * share]

    layer_rows = layer_out.reshape(rows, seq, width)
    my_logits = jnp.sum(
        my_select[:, :, None] * jnp.einsum("rd,kdc->rkc", cls_rows, heads, preferred_element_type=F32), axis=1
    )
    logits = my_logits * my_class
    owner_mask = (row_table == own).astype(F32)[:, None]
    class_live = (class_ids < class_count[0]).astype(F32)[None, :]
    group_dlog = group_dlog_raw * (owner_mask * class_live)
    grad_head = lax.dot_general(
        group_cls.astype(F32), group_dlog, (((0,), (0,)), ((), ())), precision=PRECISE, preferred_element_type=F32
    )[None]
    root_squares = jnp.sqrt(totals[:5] / (totals[5] * width))
    return (
        layer_rows,
        logits,
        grad_input.reshape(rows, seq, width),
        own_merge,
        own_qkv,
        own_vecs[6],
        own_vecs[7],
        own_out,
        own_vecs[0],
        own_vecs[1],
        own_vecs[2],
        own_up,
        own_up_bias,
        own_down,
        own_vecs[3],
        own_vecs[4],
        own_vecs[5],
        grad_head,
        root_squares,
    )


def solution(mesh):
    three = P(BOTH, None, None)
    two = P(BOTH, None)
    one = P(BOTH)
    placed = (
        three, one, two, P("table"), one, two, two, one, one, two, one, one, one, two, one, two, one, one, one, three,
        three, two,
    )
    results = (
        three, two, three, two, two, one, one, two, one, one, one, two, one, two, one, one, one, three, P(),
    )
    return jax.shard_map(body, mesh=mesh, in_specs=placed, out_specs=results, check_vma=False)
```

```python
import functools

import jax
import jax.numpy as jnp
from jax import lax
from jax.experimental import pallas as pl
from jax.experimental.pallas import tpu as pltpu
from jax.sharding import PartitionSpec as P

HEADS = 12
BLOCK = 8
NORM_EPS = 1e-05
MASKED = -1000000000.0
FAR = -3e38
PRECISE = lax.Precision.HIGHEST
TILE = 256
VMEM_BYTES = 64_000_000
BOTH = ("table", "batch")
F32 = jnp.float32
BF16 = jnp.bfloat16


def mm(left, right):
    return jnp.dot(left, right, preferred_element_type=F32)


def mm_t(left, right):
    return lax.dot_general(left, right, (((1,), (1,)), ((), ())), preferred_element_type=F32)


def t_mm(left, right):
    return lax.dot_general(left, right, (((0,), (0,)), ((), ())), preferred_element_type=F32)


def rowsum(values):
    return jnp.sum(values, axis=0, keepdims=True)


def norm_forward(hidden, gain, shift):
    average = jnp.mean(hidden, axis=-1, keepdims=True)
    centered = hidden - average
    variance = jnp.mean(centered * centered, axis=-1, keepdims=True)
    inv_std = lax.rsqrt(variance + NORM_EPS)
    standard = centered * inv_std
    return standard * gain + shift, standard, inv_std


def norm_backward(grad_norm, standard, inv_std, gain):
    scaled = grad_norm * gain
    return inv_std * (
        scaled
        - jnp.mean(scaled, axis=-1, keepdims=True)
        - standard * jnp.mean(scaled * standard, axis=-1, keepdims=True)
    )


def group_probs(query, tok, live_row, scale):
    size = tok.shape[0]
    row = lax.broadcasted_iota(jnp.int32, (size, size), 0) // BLOCK
    col = lax.broadcasted_iota(jnp.int32, (size, size), 1) // BLOCK
    scores = jnp.where(live_row > 0, mm_t(query, tok) * scale, MASKED)
    scores = jnp.where(row == col, scores, FAR)
    terms = jnp.exp(scores - jnp.max(scores, axis=-1, keepdims=True))
    return terms / jnp.sum(terms, axis=-1, keepdims=True), row == col


def merge_kernel(tok, live_row, live_col, merge_w, qkv_w, qkv_bias, query_out, hidden_out, attn_out, packed_out, squares):
    step = pl.program_id(0)
    scale = tok.shape[1] ** -0.5
    x = tok[...]
    live = live_col[...]
    query = mm(x, merge_w[...]).astype(BF16)
    query_out[...] = query
    probs, _ = group_probs(query, x, live_row[0], scale)
    merged = mm(probs.astype(BF16), x) * live
    wide = x.astype(F32)
    hidden = wide + merged
    hidden_out[...] = hidden
    attn_in = hidden.astype(BF16)
    attn_out[...] = attn_in
    packed_out[...] = (mm(attn_in, qkv_w[...]) + qkv_bias[...]).astype(BF16)

    @pl.when(step == 0)
    def _():
        squares[...] = jnp.zeros_like(squares)

    squares[0:1, :] += rowsum(live * wide * wide)
    squares[1:2, :] += rowsum(merged * merged)


def lane_mask(values, low, high):
    lane = lax.broadcasted_iota(jnp.int32, values.shape, 1)
    return jnp.where((lane >= low) & (lane < high), values, jnp.zeros_like(values))


def attn_kernel(scale, q_ref, k_ref, v_ref, bias_ref, ctx_ref, lse_ref):
    seq, lanes = q_ref.shape[1:]
    head = lanes // 2
    q = q_ref[0] * jnp.asarray(scale, BF16)
    k = k_ref[0]
    v_t = v_ref[0].T
    bias = bias_ref[0]
    for c in range(seq // TILE):
        rows = slice(c * TILE, (c + 1) * TILE)
        parts = []
        for h in range(2):
            scores = mm_t(k, lane_mask(q[rows], h * head, (h + 1) * head)) + bias
            top = jnp.max(scores, axis=0, keepdims=True)
            terms = jnp.exp(scores - top)
            total = jnp.sum(terms, axis=0, keepdims=True)
            probs = (terms * (1.0 / total)).astype(BF16)
            lse_ref[0, 0, h : h + 1, rows] = top + jnp.log(total)
            parts.append(mm(v_t[h * head : (h + 1) * head], probs))
        ctx_ref[0, rows, :] = jnp.concatenate(parts, axis=0).T.astype(BF16)


def attn_back_kernel(scale, q_ref, k_ref, v_ref, bias_ref, lse_ref, grad_ref, out_ref):
    seq, lanes = q_ref.shape[1:]
    head = lanes // 2
    q = q_ref[0] * jnp.asarray(scale, BF16)
    k = k_ref[0]
    v = v_ref[0]
    k_t = k.T
    bias = bias_ref[0]
    grad_k = jnp.zeros((seq, lanes), F32)
    grad_v = jnp.zeros((seq, lanes), F32)
    for c in range(seq // TILE):
        rows = slice(c * TILE, (c + 1) * TILE)
        parts = []
        for h in range(2):
            q_part = lane_mask(q[rows], h * head, (h + 1) * head)
            g_part = lane_mask(grad_ref[0, rows, :], h * head, (h + 1) * head)
            scores = mm_t(k, q_part) + bias
            probs = jnp.exp(scores - lse_ref[0, 0, h : h + 1, rows])
            grad_v += mm(probs.astype(BF16), g_part)
            grad_p = mm_t(v, g_part)
            grad_s = (probs * (grad_p - jnp.sum(probs * grad_p, axis=0, keepdims=True))).astype(BF16)
            grad_k += mm(grad_s, q_part)
            parts.append(mm(k_t[h * head : (h + 1) * head], grad_s))
        out_ref[0, 0, rows, :] = (jnp.concatenate(parts, axis=0).T * scale).astype(BF16)
    out_ref[1, 0] = grad_k.astype(BF16)
    out_ref[2, 0] = grad_v.astype(BF16)


def share_out(low, cols, value):
    rows = low.shape[4]
    spots = [(a, b, c, d) for a in range(low.shape[0]) for b in range(low.shape[1]) for c in range(low.shape[2]) for d in range(low.shape[3])]
    for i, spot in enumerate(spots):
        low[(*spot, slice(None), cols)] = value[i * rows : (i + 1) * rows].astype(BF16)


def attn_back_weights_kernel(
    scale, pairs, cuts, q, k, v, bias, lse, grad, ffn_in, grad_up, ctx, grad_attn, out_ref, low_up, low_out, turned
):
    step = pl.program_id(0) * pairs + pl.program_id(1)
    part = grad_up.shape[1]

    @pl.when(step == 0)
    def _():
        turned[...] = ffn_in[...].T

    @pl.when(step < cuts)
    def _():
        cols = pl.ds(pl.multiple_of(step * part, part), part)
        share_out(low_up, cols, mm(turned[...], grad_up[...]))

    @pl.when(step == cuts)
    def _():
        share_out(low_out, slice(None), mm(ctx[...].T, grad_attn[...]))

    attn_back_kernel(scale, q, k, v, bias, lse, grad, out_ref)


def qkv_grad_kernel(attn_in, grad, weight_grad, sums, turned):
    @pl.when(pl.program_id(0) == 0)
    def _():
        turned[...] = attn_in[...].T

    piece = grad[0]
    weight_grad[...] = mm(turned[...], piece).astype(BF16)
    sums[...] = jnp.broadcast_to(rowsum(piece.astype(F32)), sums.shape)


def ffn_kernel(
    per_row,
    ctx,
    hidden,
    cot,
    cls_grad,
    live_col,
    out_w,
    up_w,
    down_w,
    vecs,
    layer_out,
    activated,
    grad_up,
    ffn_in_out,
    grad_down_out,
    grad_attn_out,
    grad_two_out,
    grad_ctx_out,
    sums,
    up_sums,
    slope,
):
    step = pl.program_id(0)
    width = hidden.shape[1]
    chunks = up_w.shape[1] // width

    @pl.when(step == 0)
    def _():
        sums[...] = jnp.zeros_like(sums)
        up_sums[...] = jnp.zeros_like(up_sums)

    live = live_col[...]
    out_bias, gain_one, shift_one, down_bias, gain_two, shift_two = (vecs[i : i + 1, :width] for i in range(6))
    branch = mm(ctx[...], out_w[...]) + out_bias
    norm_one, standard_one, inv_one = norm_forward(hidden[...] + branch, gain_one, shift_one)
    ffn_in = norm_one.astype(BF16)
    ffn_in_out[...] = ffn_in
    down = jnp.zeros_like(norm_one)
    for j in range(chunks):
        cols = slice(j * width, (j + 1) * width)
        pre = mm(ffn_in, up_w[:, cols]) + vecs[6:7, cols]
        cumulative = 0.5 * (1.0 + lax.erf(pre * 0.7071067811865476))
        act = (pre * cumulative).astype(BF16)
        slope[:, cols] = cumulative + pre * (jnp.exp(-0.5 * pre * pre) * 0.3989422804014327)
        activated[:, cols] = act
        down += mm(act, down_w[cols, :])
    down += down_bias
    normed, standard_two, inv_two = norm_forward(norm_one + down, gain_two, shift_two)
    result = (normed * live).astype(BF16)
    layer_out[...] = result
    wide = result.astype(F32)
    sums[5:6, :] += rowsum(live * branch * branch)
    sums[6:7, :] += rowsum(live * down * down)
    sums[7:8, :] += rowsum(wide * wide)
    first = (lax.broadcasted_iota(jnp.int32, (hidden.shape[0], 1), 0) == 0) & (step % per_row == 0)
    grad = live * (cot[...].astype(F32) + jnp.where(first, cls_grad[0], 0.0))
    sums[0:1, :] += rowsum(grad * standard_two)
    sums[1:2, :] += rowsum(grad)
    grad_three = norm_backward(grad, standard_two, inv_two, gain_two)
    grad_down = grad_three.astype(BF16)
    grad_down_out[...] = grad_down
    sums[2:3, :] += rowsum(grad_down.astype(F32))
    total = grad_three
    for j in range(chunks):
        cols = slice(j * width, (j + 1) * width)
        piece = (mm_t(grad_down, down_w[cols, :]) * slope[:, cols]).astype(BF16)
        grad_up[:, cols] = piece
        up_sums[0:1, cols] += rowsum(piece.astype(F32))
        total += mm_t(piece, up_w[:, cols])
    sums[3:4, :] += rowsum(total * standard_one)
    sums[4:5, :] += rowsum(total)
    grad_two = norm_backward(total, standard_one, inv_one, gain_one)
    grad_two_out[...] = grad_two
    grad_attn = grad_two.astype(BF16)
    grad_attn_out[...] = grad_attn
    sums[8:9, :] += rowsum(grad_attn.astype(F32))
    grad_ctx_out[...] = mm_t(grad_attn, out_w[...]).astype(BF16)


def input_kernel(
    grad_qkv, grad_two, tok, query, live_row, live_col, merge_w, qkv_w, grad_input, merge_grad
):
    step = pl.program_id(0)
    width = tok.shape[1]
    scale = width**-0.5

    @pl.when(step == 0)
    def _():
        merge_grad[...] = jnp.zeros_like(merge_grad)

    x = tok[...]
    grad_one = grad_two[...]
    for i in range(3):
        cols = slice(i * width, (i + 1) * width)
        grad_one += mm_t(grad_qkv[i], qkv_w[:, cols])
    grad_merged = (grad_one * live_col[...]).astype(BF16)
    mq = query[...]
    probs, same = group_probs(mq, x, live_row[0], scale)
    grad_probs = mm_t(grad_merged, x)
    grad_scores = probs * (grad_probs - jnp.sum(probs * grad_probs, axis=-1, keepdims=True))
    grad_scores = jnp.where(same & (live_row[0] > 0), grad_scores, 0.0)
    grad_query = (mm(grad_scores.astype(BF16), x) * scale).astype(BF16)
    merge_grad[...] += mm(x.T, grad_query)
    blocks = mm(probs.T.astype(BF16), grad_merged) + mm(grad_scores.T.astype(BF16), mq) * scale
    blocks += mm_t(grad_query, merge_w[...])
    grad_input[...] = (grad_one + blocks).astype(BF16)


def params(**kw):
    return pltpu.CompilerParams(vmem_limit_bytes=VMEM_BYTES, **kw)


def fixed(shape):
    zeros = (0,) * len(shape)
    return pl.BlockSpec(shape, lambda *_: zeros, pipeline_mode=pl.Buffered(1))


def tiled(size, width):
    return pl.BlockSpec((size, width), lambda i: (i, 0))


MESH = pl.DeviceIdType.MESH
TABLE_MAJOR = 4
UP_CUTS = 6
ATTN_PACE, BACK_PACE, LAST_PACE = 3.0, 2.4, 2.5
CORES = 2


def here(dims):
    table, batch = lax.axis_index("table"), lax.axis_index("batch")
    return [table // dims[1], lax.rem(table, dims[1]), batch // CORES, lax.rem(batch, CORES)]


def peer(dims, spot, axis, offset):
    other = list(spot)
    other[axis] = lax.rem(spot[axis] + offset, dims[axis])
    return (other[0] * dims[1] + other[1], other[2] * CORES + other[3]), other[axis]


def greet(dims, spot):
    barrier = pltpu.get_barrier_semaphore()
    total = 0
    for axis in range(4):
        for offset in range(1, dims[axis]):
            target, _ = peer(dims, spot, axis, offset)
            pl.semaphore_signal(barrier, inc=1, device_id=target, device_id_type=MESH)
            total += 1
    pl.semaphore_wait(barrier, total)


def gather_events(dims, spot, items, shards, fulls, local_sem, send_sem, recv_sem):
    def region(item, done):
        array, low, size, order = items[item]
        where = tuple(slice(None) if axis in done else spot[axis] for axis in sorted(order))
        return fulls[array].at[(*where, pl.ds(low, size))]

    def copies(item, stage):
        array, low, size, order = items[item]
        place = region(item, order[:stage])
        return [
            pltpu.make_async_remote_copy(
                src_ref=place if stage else shards[array].at[pl.ds(low, size)],
                dst_ref=place,
                send_sem=send_sem.at[item, stage, offset],
                recv_sem=recv_sem.at[item, stage, offset],
                device_id=peer(dims, spot, order[stage], offset)[0],
                device_id_type=MESH,
            )
            for offset in range(1, dims[order[stage]])
        ]

    def keep(item):
        array, low, size, _ = items[item]
        return pltpu.make_async_copy(shards[array].at[pl.ds(low, size)], region(item, ()), local_sem.at[item])

    def begin():
        for item in range(len(items)):
            keep(item).start()
            for copy in copies(item, 0):
                copy.start()

    def advance(item, stage):
        for copy in copies(item, stage):
            copy.wait_recv()
        if stage == 0:
            keep(item).wait()
        if stage + 1 < len(items[item][3]):
            for copy in copies(item, stage + 1):
                copy.start()

    def end():
        for item in range(len(items)):
            for stage in range(len(items[item][3])):
                for copy in copies(item, stage):
                    copy.wait_send()

    return begin, slots(items, advance), end


def slots(items, advance):
    count = len(items)
    pairs = (count + 1) // 2
    groups = []
    for slot in range(pairs + 3):
        group = []
        for stage in (3, 2, 1, 0):
            pair = slot - stage
            for item in range(2 * pair, min(2 * pair + 2, count)) if 0 <= pair < pairs else ():
                if stage < len(items[item][3]):
                    group.append(functools.partial(advance, item, stage))
        groups.append(group)
    return groups


def scatter_events(dims, spot, items, grads, outs, buffers, local_sem, send_sem, recv_sem):
    buffers = [buffers[i * 7 : (i + 1) * 7] for i in range(len(items))]

    def piece(item, core):
        array, low, size, _ = items[item]
        if size <= grads[array].shape[4]:
            return grads[array].at[:, :, :, core, pl.ds(low, size)]
        return grads[array].at[:, :, :, core, :, pl.ds(low, size)]

    def load(item):
        return pltpu.make_async_copy(
            piece(item, spot[3]), buffers[item][0], local_sem.at[item]
        )

    def copies(item, stage):
        array, low, size, order = items[item]
        own, first, second, got_core, got_first, got_second, got_last = buffers[item]
        axis = order[stage]
        made = []
        for offset in range(1, dims[axis]):
            target, other = peer(dims, spot, axis, offset)
            if stage == 0:
                source, landing = piece(item, other), got_core
            elif stage == 1:
                source = own.at[:, :, other] if axis == 2 else own.at[:, other]
                landing = got_first.at[offset - 1]
            elif stage == 2:
                source, landing = first.at[:, other], got_second.at[offset - 1]
            else:
                source, landing = second.at[other], got_last.at[offset - 1]
            made.append(
                pltpu.make_async_remote_copy(
                    src_ref=source,
                    dst_ref=landing,
                    send_sem=send_sem.at[item, stage, offset],
                    recv_sem=recv_sem.at[item, stage, offset],
                    device_id=target,
                    device_id_type=MESH,
                )
            )
        return made

    def begin(chosen=tuple(range(len(items)))):
        for item in chosen:
            load(item).start()
            for copy in copies(item, 0):
                copy.start()

    def advance(item, stage):
        array, low, size, order = items[item]
        own, first, second, got_core, got_first, got_second, got_last = buffers[item]
        axis = order[stage]
        others = range(dims[axis] - 1)
        mine = spot[axis]
        for copy in copies(item, stage):
            copy.wait_recv()
        if stage == 0:
            load(item).wait()

            @pl.loop(0, dims[0] * dims[1] * dims[2])
            def _(i):
                at = (i // (dims[1] * dims[2]), lax.rem(i // dims[2], dims[1]), lax.rem(i, dims[2]))
                own[at] = (own[at].astype(F32) + got_core[at].astype(F32)).astype(BF16)
        elif stage == 1:
            inner = first.shape[1]

            @pl.loop(0, dims[0] * inner)
            def _(i):
                at = (i // inner, lax.rem(i, inner))
                value = own[(*at, mine) if axis == 2 else (at[0], mine, at[1])].astype(F32)
                for k in others:
                    value += got_first[(k, *at)].astype(F32)
                first[at] = value.astype(BF16)
        elif stage == 2:

            @pl.loop(0, dims[0])
            def _(i):
                value = first[i, mine].astype(F32)
                for k in others:
                    value += got_second[k, i].astype(F32)
                second[i] = value.astype(BF16)
        else:
            value = second[mine].astype(F32)
            for k in others:
                value += got_last[k].astype(F32)
            if size <= grads[array].shape[4]:
                outs[array][low : low + size] = value
            else:
                outs[array][:, low : low + size] = value
        if stage < 3:
            for copy in copies(item, stage + 1):
                copy.start()

    def end():
        for item in range(len(items)):
            for stage in range(4):
                for copy in copies(item, stage):
                    copy.wait_send()

    return begin, slots(items, advance), end


def square_events(dims, spot, square, total, kept, got, send_sem, recv_sem):
    def copies(stage):
        axis = 3 - stage
        return [
            pltpu.make_async_remote_copy(
                src_ref=kept.at[stage],
                dst_ref=got.at[stage, offset - 1],
                send_sem=send_sem.at[stage, offset],
                recv_sem=recv_sem.at[stage, offset],
                device_id=peer(dims, spot, axis, offset)[0],
                device_id_type=MESH,
            )
            for offset in range(1, dims[axis])
        ]

    def begin():
        kept[0] = square[...]
        for copy in copies(0):
            copy.start()

    def advance(stage):
        for copy in copies(stage):
            copy.wait_recv()
        value = kept[stage]
        for offset in range(1, dims[3 - stage]):
            value = value + got[stage, offset - 1]
        kept[stage + 1] = value
        if stage < 3:
            for copy in copies(stage + 1):
                copy.start()
        else:
            total[...] = value

    def end():
        for stage in range(4):
            for copy in copies(stage):
                copy.wait_send()

    return begin, [[functools.partial(advance, stage)] for stage in range(4)], end


def scatter_scratch(dims, grads, items):
    scratch = []
    for array, _, size, order in items:
        rows, cols = grads[array].shape[4:]
        tail = (size, cols) if size <= rows else (rows, size)
        inner = dims[order[2]]
        for shape in (
            dims[:3],
            (dims[0], inner),
            (dims[0],),
            dims[:3],
            (dims[order[1]] - 1, dims[0], inner),
            (inner - 1, dims[0]),
            (dims[0] - 1,),
        ):
            scratch.append(pltpu.VMEM((*shape, *tail), BF16))
    return scratch


def links(count, most):
    return [pltpu.SemaphoreType.DMA((count, 4, most)), pltpu.SemaphoreType.DMA((count, 4, most))]


def split(array, size, pieces, *orders):
    part = size // pieces
    return [(array, i * part, part, orders[i % len(orders)]) for i in range(pieces)]


def plain_call(kernel, grid, refs, outs, name):
    return pl.pallas_call(
        kernel,
        grid=grid,
        in_specs=[spec for spec, _ in refs],
        out_specs=[spec for spec, _ in outs],
        out_shape=[shape for _, shape in outs],
        compiler_params=params(),
        name=name,
    )(*(arg for _, arg in refs))


def moving_call(dims, collective_id, name, kernel, grid, own_in, own_out, gather, scatter, square, pace=1.0, made=(), early=(), after=None, extra=()):
    most = max(dims)
    total = dims[0] * dims[1] * dims[2] * dims[3]
    vmem, anywhere = (lambda a: fixed(a.shape)), (lambda a: pl.BlockSpec(memory_space=pl.ANY))
    shards, gather_items = gather
    grads, scatter_items = scatter
    squares = [] if square is None else [square]
    in_specs, args = [spec for spec, _ in own_in], [arg for _, arg in own_in]
    in_specs += [vmem(a) for a in shards] + [anywhere(a) for a in grads] + [vmem(a) for a in squares]
    args += [*shards, *grads, *squares]
    out_specs, out_shape = [spec for spec, _ in own_out], [shape for _, shape in own_out]
    orders = {array: sorted(order) for array, _, _, order in gather_items}
    for i, a in enumerate(shards):
        out_specs.append(anywhere(a))
        out_shape.append(jax.ShapeDtypeStruct((*(dims[axis] for axis in orders[i]), *a.shape), a.dtype))
    whole = [*grads, *early]
    after = after or {}
    for g in whole:
        out_shape.append(jax.ShapeDtypeStruct(g.shape[4:], F32))
        out_specs.append(vmem(out_shape[-1]))
    for g in made:
        out_shape.append(jax.ShapeDtypeStruct((g.shape[0] // total, g.shape[1]), F32))
        out_specs.append(vmem(out_shape[-1]))
    for q in squares:
        out_shape.append(jax.ShapeDtypeStruct(q.shape, F32))
        out_specs.append(vmem(q))
    groups = []
    if shards:
        groups.append([pltpu.SemaphoreType.DMA((len(gather_items),)), *links(len(gather_items), most)])
    if grads:
        buffers = scatter_scratch(dims, whole, scatter_items)
        groups.append([*extra, *(pltpu.VMEM(g.shape, BF16) for g in early), *buffers, pltpu.SemaphoreType.DMA((len(scatter_items),)), *links(len(scatter_items), most)])
    if squares:
        groups.append(
            [
                pltpu.VMEM((5, *square.shape), F32),
                pltpu.VMEM((4, most - 1, *square.shape), F32),
                pltpu.SemaphoreType.DMA((4, most)),
                pltpu.SemaphoreType.DMA((4, most)),
            ]
        )
    if made:
        made_shapes = [jax.ShapeDtypeStruct((*dims, g.shape[0] // total, g.shape[1]), BF16) for g in made]
        made_items = [(i, 0, g.shape[4], (3, 2, 1, 0) if i % 2 == 0 else (3, 1, 2, 0)) for i, g in enumerate(made_shapes)]
        buffers = [pltpu.VMEM(g.shape, F32) for g in made] + [pltpu.VMEM(g.shape, BF16) for g in made_shapes]
        buffers += scatter_scratch(dims, made_shapes, made_items)
        groups.append([*buffers, pltpu.SemaphoreType.DMA((len(made),)), *links(len(made), most)])
    steps = 1
    for size in grid:
        steps *= size

    def fused(*refs):
        refs = list(refs)

        def take(n):
            taken = refs[:n]
            del refs[:n]
            return taken

        ins, shard_refs, grad_refs, square_refs = take(len(own_in)), take(len(shards)), take(len(grads)), take(len(squares))
        outs, full_refs, sum_refs = take(len(own_out)), take(len(shards)), take(len(whole))
        made_outs, total_refs = take(len(made)), take(len(squares))
        step = 0
        for axis, size in enumerate(grid):
            step = step * size + pl.program_id(axis)
        spot = here(dims)
        plans = []
        scratch = iter(groups)
        if shards:
            plans.append(gather_events(dims, spot, gather_items, shard_refs, full_refs, *take(len(next(scratch)))))
        if grads:
            held = take(len(next(scratch)))
            turned, held = held[: len(extra)], held[len(extra) :]
            early_refs, held = held[: len(early)], held[len(early) :]
            begin_some, some_groups, end_some = scatter_events(
                dims, spot, scatter_items, grad_refs + early_refs, sum_refs, held[:-3], *held[-3:]
            )
            ready = [item for item in range(len(scatter_items)) if item not in after]
            plans.append((functools.partial(begin_some, ready), some_groups, end_some))
        else:
            turned, early_refs = [], []
        if squares:
            plans.append(square_events(dims, spot, *square_refs, *total_refs, *take(len(next(scratch)))))

        if made:
            held = take(len(next(scratch)))
            sums, lows = held[: len(made)], held[len(made) : 2 * len(made)]
            begin_made, made_groups, end_made = scatter_events(
                dims, spot, made_items, lows, made_outs, held[2 * len(made) : -3], *held[-3:]
            )
        else:
            sums, made_groups = [], []

        def round_made():
            for value, low in zip(sums, lows):
                rows = low.shape[4]

                @pl.loop(0, total)
                def _(i):
                    at = (
                        i // (dims[1] * dims[2] * dims[3]),
                        lax.rem(i // (dims[2] * dims[3]), dims[1]),
                        lax.rem(i // dims[3], dims[2]),
                        lax.rem(i, dims[3]),
                    )
                    low[at] = value[pl.ds(pl.multiple_of(i * rows, rows), rows), :].astype(BF16)

        def open_all():
            greet(dims, spot)
            for begin, _, _ in plans:
                begin()

        depth = max(len(groups_of) for _, groups_of, _ in plans)
        merged = [[e for _, groups_of, _ in plans if i < len(groups_of) for e in groups_of[i]] for i in range(depth)]

        def close_all():
            for _, _, end in plans:
                end()

        if steps == 1:
            open_all()
            for group in merged:
                for event in group:
                    event()
            close_all()
            return
        late = []
        pl.when(step == 0)(open_all)
        for i, group in enumerate(merged):
            at = int((i + 1) * pace)

            def run(group=group):
                for event in group:
                    event()

            if at < steps:
                pl.when(step == at)(run)
            else:
                late.append(run)
        kernel(*ins, *outs, *sums, *early_refs, *turned)
        for item, at in after.items():
            pl.when(step == at)(functools.partial(begin_some, (item,)))

        @pl.when(step == steps - 1)
        def _():
            if made:
                round_made()
                begin_made()
            for i in range(max(len(late), len(made_groups))):
                if i < len(late):
                    late[i]()
                for event in made_groups[i] if i < len(made_groups) else ():
                    event()
            close_all()
            if made:
                end_made()

    return pl.pallas_call(
        fused,
        grid=grid,
        in_specs=in_specs,
        out_specs=out_specs,
        out_shape=out_shape,
        scratch_shapes=[piece for group in groups for piece in group],
        compiler_params=params(collective_id=collective_id, has_side_effects=True),
        name=name,
    )(*args)


def body(
    tokens,
    row_blocks,
    block_fill,
    row_table,
    class_count,
    merge_w,
    qkv_w,
    query_bias,
    value_bias,
    out_w,
    out_bias,
    gain_one,
    shift_one,
    up_w,
    up_bias,
    down_w,
    down_bias,
    gain_two,
    shift_two,
    head_w,
    cotangent,
    logit_cotangent,
):
    rows, seq, width = tokens.shape
    count = rows * seq
    ff = up_w.shape[1]
    head = width // HEADS
    per_row = seq // TILE
    tiles = count // TILE
    share = merge_w.shape[0]
    devices = width // share
    wide_ff = ff // width

    def cut(mat, n):
        return [mat[:, i * width : (i + 1) * width] for i in range(n)]

    table_size, batch_size = lax.axis_size("table"), lax.axis_size("batch")
    dims = (TABLE_MAJOR, table_size // TABLE_MAJOR, batch_size // CORES, CORES)
    direct = share % BLOCK == 0
    vec_list = (out_bias, gain_one, shift_one, down_bias, gain_two, shift_two, query_bias, value_bias)
    used = 8 * share + up_bias.shape[0]
    spare = jnp.zeros((8 * width - used,), F32)
    vec_row = jnp.concatenate([*(v.astype(F32) for v in (*vec_list, up_bias)), spare])
    vec_row = vec_row.reshape(8, width).astype(BF16)
    base = (5 + wide_ff) * share
    down_out, up_out = (0, 1, 2, 3), (0, 2, 1, 3)
    down_in, up_in = (3, 1, 2, 0), (3, 2, 1, 0)
    none = ((), ())
    if direct:
        qkv_full, merge_full, vec_full = moving_call(
            dims,
            0,
            "gather_first",
            None,
            (1,),
            [],
            [],
            (
                (qkv_w, merge_w, vec_row),
                (
                    (1, 0, share, down_out),
                    *split(0, share, 3, up_out, down_out),
                    (2, 0, 8, up_out),
                ),
            ),
            none,
            None,
        )
        qkv_full = qkv_full.reshape(width, 3 * width)
        merge_full = merge_full.reshape(width, width)
        vec_rows = vec_full.reshape(devices, 8, width)[:, 0].astype(F32)
    else:
        mine = jnp.concatenate([merge_w, out_w, *cut(qkv_w, 3), *cut(up_w, wide_ff), down_w, vec_row], axis=0)
        gathered = lax.all_gather(mine, BOTH, axis=0)

        def unit(start, n):
            part = gathered[:, start : start + n * share]
            part = part.reshape(devices, n, share, width).transpose(0, 2, 1, 3)
            return part.reshape(width, n * width)

        merge_full = unit(0, 1)
        out_full = unit(share, 1)
        qkv_full = unit(2 * share, 3)
        up_full = unit(5 * share, wide_ff)
        down_full = gathered[:, base : base + wide_ff * share].reshape(ff, width)
        vec_rows = gathered[:, base + wide_ff * share].astype(F32)
    vectors = [vec_rows[:, i * share : (i + 1) * share].reshape(1, width) for i in range(8)]
    up_bias_full = vec_rows[:, 8 * share : 8 * share + wide_ff * share].reshape(1, ff)
    query_vec, value_vec = vectors[6], vectors[7]
    qkv_bias = jnp.concatenate([query_vec, jnp.zeros_like(query_vec), value_vec], axis=1)
    vecs = jnp.concatenate(
        [jnp.pad(jnp.concatenate(vectors[:6], axis=0), ((0, 0), (0, ff - width))), up_bias_full, jnp.zeros((1, ff), F32)],
        axis=0,
    )

    position = jnp.arange(seq, dtype=jnp.int32)
    fill_tok = jnp.repeat(block_fill, BLOCK, axis=1)
    live = ((position // BLOCK)[None, :] < row_blocks[:, None]) & ((position % BLOCK)[None, :] < fill_tok)
    live_mask = live.astype(F32)
    live_col = live_mask.reshape(count, 1)
    live_row = live_mask.reshape(tiles, 1, TILE)
    key_bias = jnp.where(live, 0.0, MASKED).astype(F32).reshape(rows, seq, 1)

    batch = lax.axis_size("batch")
    classes = head_w.shape[2]
    tok_flat = tokens.reshape(count, width)
    cot_flat = cotangent.reshape(count, width)
    merge_query, hidden, attn_in, packed, squares = pl.pallas_call(
        merge_kernel,
        grid=(tiles,),
        in_specs=[
            tiled(TILE, width),
            pl.BlockSpec((1, 1, TILE), lambda i: (i, 0, 0)),
            tiled(TILE, 1),
            fixed((width, width)),
            fixed((width, 3 * width)),
            fixed((1, 3 * width)),
        ],
        out_specs=[
            tiled(TILE, width),
            tiled(TILE, width),
            tiled(TILE, width),
            tiled(TILE, 3 * width),
            fixed((8, width)),
        ],
        out_shape=[
            jax.ShapeDtypeStruct((count, width), BF16),
            jax.ShapeDtypeStruct((count, width), F32),
            jax.ShapeDtypeStruct((count, width), BF16),
            jax.ShapeDtypeStruct((count, 3 * width), BF16),
            jax.ShapeDtypeStruct((8, width), F32),
        ],
        compiler_params=params(),
        name="merge_qkv",
    )(tok_flat, live_row, live_col, merge_full, qkv_full, qkv_bias)

    packed_rows = packed.reshape(rows, seq, 3 * width)
    pairs = HEADS // 2
    lanes = 2 * head

    def head_block(offset):
        return pl.BlockSpec((1, seq, lanes), lambda r, p: (r, 0, p + offset))

    bias_block = pl.BlockSpec((1, seq, 1), lambda r, p: (r, 0, 0))
    lse_block = pl.BlockSpec((1, 1, 2, seq), lambda r, p: (r, p, 0, 0))
    attn_in_refs = [
        (head_block(0), packed_rows),
        (head_block(pairs), packed_rows),
        (head_block(2 * pairs), packed_rows),
        (bias_block, key_bias),
    ]
    attn_outs = [
        (head_block(0), jax.ShapeDtypeStruct((rows, seq, width), BF16)),
        (lse_block, jax.ShapeDtypeStruct((rows, pairs, 2, seq), F32)),
    ]
    attend = functools.partial(attn_kernel, head**-0.5)
    if direct:
        limit = jnp.broadcast_to(class_count.astype(F32)[:, None], (1, classes))
        spare = -(rows + 1) % 8
        small = jnp.concatenate([logit_cotangent, limit, jnp.zeros((spare, classes), F32)], axis=0)
        up_items, down_items = split(0, share, 3, up_out), split(1, wide_ff * share, 3, down_out)
        gather_items = [
            *(up_items[0], down_items[0], up_items[1], down_items[1]),
            (2, 0, share, (2, 1, 0, 3)),
            (3, 0, width, (2, 3)),
            *(up_items[2], down_items[2]),
            (4, 0, small.shape[0], (2, 3)),
        ]
        context, lse, up_full, down_full, out_full, heads, small = moving_call(
            dims,
            2,
            "attention_gather",
            attend,
            (rows, pairs),
            attn_in_refs,
            attn_outs,
            ((up_w, down_w, out_w, head_w[0], small), gather_items),
            none,
            None,
            pace=ATTN_PACE,
        )
        up_full = up_full.reshape(width, ff)
        down_full = down_full.reshape(ff, width)
        out_full = out_full.reshape(width, width)
        heads = heads.reshape(batch, width, classes)
        small = small.reshape(batch, -1, classes)
        group_dlog_raw = small[:, :rows].reshape(batch * rows, classes)
        counts = small[:, rows, 0]
    else:
        context, lse = pl.pallas_call(
            attend,
            grid=(rows, pairs),
            in_specs=[spec for spec, _ in attn_in_refs],
            out_specs=[spec for spec, _ in attn_outs],
            out_shape=[shape for _, shape in attn_outs],
            compiler_params=params(),
            name="attention",
        )(*(arg for _, arg in attn_in_refs))
        heads = lax.all_gather(head_w[0], "batch", axis=0)
        counts = lax.all_gather(class_count, "batch", axis=0, tiled=True)
        group_dlog_raw = lax.all_gather(logit_cotangent, "batch", axis=0, tiled=True)
    own = lax.axis_index("batch")
    my_table = lax.dynamic_slice(row_table, (own * rows,), (rows,))
    class_ids = jnp.arange(classes, dtype=jnp.int32)
    my_select = (my_table[:, None] == jnp.arange(batch, dtype=jnp.int32)[None, :]).astype(F32)
    my_class = (class_ids[None, :] < (my_select * counts[None, :].astype(F32)).sum(1, keepdims=True)).astype(F32)
    my_dlog = logit_cotangent * my_class
    picked = (my_select[:, :, None] * my_dlog[:, None, :]).transpose(1, 0, 2)
    cls_grad = jnp.sum(
        lax.dot_general(picked, heads.astype(F32), (((2,), (2,)), ((0,), (0,))), precision=PRECISE), axis=0
    )

    context = context.reshape(count, width)
    (layer_out, activated, grad_up, ffn_in, grad_down, grad_attn, grad_two, grad_ctx, sums, up_sums) = pl.pallas_call(
        functools.partial(ffn_kernel, per_row),
        grid=(tiles,),
        in_specs=[
            tiled(TILE, width),
            tiled(TILE, width),
            tiled(TILE, width),
            pl.BlockSpec((1, 1, width), lambda i: (i // per_row, 0, 0)),
            tiled(TILE, 1),
            fixed((width, width)),
            fixed((width, ff)),
            fixed((ff, width)),
            fixed((8, ff)),
        ],
        out_specs=[
            tiled(TILE, width),
            tiled(TILE, ff),
            tiled(TILE, ff),
            tiled(TILE, width),
            tiled(TILE, width),
            tiled(TILE, width),
            tiled(TILE, width),
            tiled(TILE, width),
            fixed((16, width)),
            fixed((8, ff)),
        ],
        out_shape=[
            jax.ShapeDtypeStruct((count, width), BF16),
            jax.ShapeDtypeStruct((count, ff), BF16),
            jax.ShapeDtypeStruct((count, ff), BF16),
            jax.ShapeDtypeStruct((count, width), BF16),
            jax.ShapeDtypeStruct((count, width), BF16),
            jax.ShapeDtypeStruct((count, width), BF16),
            jax.ShapeDtypeStruct((count, width), F32),
            jax.ShapeDtypeStruct((count, width), BF16),
            jax.ShapeDtypeStruct((16, width), F32),
            jax.ShapeDtypeStruct((8, ff), F32),
        ],
        scratch_shapes=[pltpu.VMEM((TILE, ff), F32)],
        compiler_params=params(),
        name="ffn",
    )(context, hidden, cot_flat, cls_grad.reshape(rows, 1, width), live_col, out_full, up_full, down_full, vecs)

    grad_rows = grad_ctx.reshape(rows, seq, width)
    cls_rows = layer_out.reshape(rows, seq, width)[:, 0, :]
    back_refs = [*attn_in_refs, (lse_block, lse), (head_block(0), grad_rows)]
    back_outs = [
        (
            pl.BlockSpec((3, 1, seq, lanes), lambda r, p: (0, r, 0, p)),
            jax.ShapeDtypeStruct((3, rows, seq, width), BF16),
        )
    ]
    grad_down_w = t_mm(activated, grad_down).astype(BF16)
    if direct:
        part = ff // UP_CUTS
        back_refs += [
            (fixed((count, width)), ffn_in),
            (pl.BlockSpec((count, part), lambda r, p: (0, jnp.minimum(r * pairs + p, UP_CUTS - 1))), grad_up),
            (fixed((count, width)), context),
            (fixed((count, width)), grad_attn),
        ]
        ffn_items = [
            *split(0, wide_ff * share, 3, up_in, down_in),
            *split(1, ff, 3, down_in, up_in),
            (2, 0, share, up_in),
        ]
        first_rows = jnp.pad(cls_rows, ((0, -rows % 8), (0, 0)))
        grad_qkv, group_cls, own_down, own_up, own_out = moving_call(
            dims,
            3,
            "attention_back_scatter",
            functools.partial(attn_back_weights_kernel, head**-0.5, pairs, UP_CUTS),
            (rows, pairs),
            back_refs,
            back_outs,
            ((first_rows,), ((0, 0, first_rows.shape[0], (2, 3)),)),
            ([grad_down_w.reshape(*dims, -1, width)], ffn_items),
            None,
            pace=BACK_PACE,
            early=(jax.ShapeDtypeStruct((*dims, share, ff), BF16), jax.ShapeDtypeStruct((*dims, share, width), BF16)),
            after={3: UP_CUTS // 3 - 1, 4: 2 * UP_CUTS // 3 - 1, 5: UP_CUTS - 1, 6: UP_CUTS},
            extra=(pltpu.VMEM((width, count), BF16),),
        )
        group_cls = group_cls.reshape(batch, -1, width)[:, :rows].reshape(batch * rows, width)
    else:
        grad_out_w = t_mm(context, grad_attn).astype(BF16)
        grad_up_w = t_mm(ffn_in, grad_up).astype(BF16)
        attend_back = functools.partial(attn_back_kernel, head**-0.5)
        (grad_qkv,) = plain_call(attend_back, (rows, pairs), back_refs, back_outs, "attention_back")
        group_cls = lax.all_gather(cls_rows, "batch", axis=0, tiled=True)

    grad_qkv = grad_qkv.reshape(3, count, width)
    grad_qkv_w, qkv_sums = pl.pallas_call(
        qkv_grad_kernel,
        grid=(3,),
        in_specs=[fixed((count, width)), pl.BlockSpec((1, count, width), lambda i: (i, 0, 0))],
        out_specs=[pl.BlockSpec((width, width), lambda i: (0, i)), pl.BlockSpec((8, width), lambda i: (0, i))],
        out_shape=[jax.ShapeDtypeStruct((width, 3 * width), BF16), jax.ShapeDtypeStruct((8, 3 * width), F32)],
        scratch_shapes=[pltpu.VMEM((width, count), BF16)],
        compiler_params=params(),
        name="qkv_grad",
    )(attn_in, grad_qkv)
    bias_sums = [qkv_sums[0, :width], qkv_sums[0, 2 * width :]]
    input_refs = [
        (pl.BlockSpec((3, TILE, width), lambda i: (0, i, 0)), grad_qkv),
        *((tiled(TILE, width), a) for a in (grad_two, tok_flat, merge_query)),
        (pl.BlockSpec((1, 1, TILE), lambda i: (i, 0, 0)), live_row),
        (tiled(TILE, 1), live_col),
        (fixed((width, width)), merge_full),
        (fixed((width, 3 * width)), qkv_full),
    ]
    input_outs = [(tiled(TILE, width), jax.ShapeDtypeStruct((count, width), BF16))]
    merge_grad = jax.ShapeDtypeStruct((width, width), F32)

    vec_grads = (sums[8], sums[3], sums[4], sums[2], sums[0], sums[1], bias_sums[0], bias_sums[1])
    vec_block = jnp.concatenate(
        [v.reshape(devices, share) for v in vec_grads] + [up_sums[0].reshape(devices, wide_ff * share)], axis=1
    )
    vec_block = jnp.pad(vec_block, ((0, 0), (0, 8 * width - used))).astype(BF16).reshape(devices, 8, width)
    live_sums = jnp.sum(live_mask.reshape(-1, width), axis=0, keepdims=True)
    square = jnp.concatenate([squares[:2], sums[5:8], live_sums, jnp.zeros((2, width), F32)], axis=0)
    if direct:
        grad_input, own_qkv, own_vec, own_merge, square = moving_call(
            dims,
            1,
            "merge_back_scatter",
            input_kernel,
            (tiles,),
            input_refs,
            input_outs,
            none,
            (
                [g.reshape(*dims, -1, g.shape[-1]) for g in (grad_qkv_w, vec_block)],
                (*split(0, share, 3, up_in, down_in), (1, 0, 8, down_in)),
            ),
            square,
            pace=LAST_PACE,
            made=(merge_grad,),
        )
        own_vec = own_vec[0]
    else:
        input_outs.append((fixed((width, width)), merge_grad))
        grad_input, grad_merge_w = plain_call(input_kernel, (tiles,), input_refs, input_outs, "merge_back")
        grad_merge_w = grad_merge_w.astype(BF16)

        def owners(mat, n):
            return mat.reshape(devices, share, n, width).transpose(0, 2, 1, 3).reshape(devices, n * share, width)


        all_grads = jnp.concatenate(
            [
                owners(grad_merge_w, 1),
                owners(grad_out_w, 1),
                owners(grad_qkv_w, 3),
                owners(grad_up_w, wide_ff),
                grad_down_w.reshape(devices, wide_ff * share, width),
                vec_block,
            ],
            axis=1,
        )
        owned = lax.psum_scatter(all_grads, BOTH, scatter_dimension=0, tiled=True)[0].astype(F32)

        def joined(start, n):
            return jnp.concatenate([owned[start + i * share : start + (i + 1) * share] for i in range(n)], axis=1)

        own_vec = owned[base + wide_ff * share]
        own_merge, own_qkv, own_out, own_up = joined(0, 1), joined(2 * share, 3), joined(share, 1), joined(5 * share, wide_ff)
        own_down = owned[base : base + wide_ff * share]
        square = lax.psum(square, BOTH)
    own_vecs = [own_vec[i * share : (i + 1) * share] for i in range(8)]
    own_up_bias = own_vec[8 * share : 8 * share + wide_ff * share]

    layer_rows = layer_out.reshape(rows, seq, width)
    my_logits = jnp.sum(
        my_select[:, :, None] * jnp.einsum("rd,kdc->rkc", cls_rows, heads, preferred_element_type=F32), axis=1
    )
    logits = my_logits * my_class
    owner_mask = (row_table == own).astype(F32)[:, None]
    class_live = (class_ids < class_count[0]).astype(F32)[None, :]
    group_dlog = group_dlog_raw * (owner_mask * class_live)
    grad_head = lax.dot_general(
        group_cls.astype(F32), group_dlog, (((0,), (0,)), ((), ())), precision=PRECISE, preferred_element_type=F32
    )[None]
    totals = jnp.sum(square[:6], axis=1)
    root_squares = jnp.sqrt(totals[:5] / (totals[5] * width))
    return (
        layer_rows,
        logits,
        grad_input.reshape(rows, seq, width),
        own_merge,
        own_qkv,
        own_vecs[6],
        own_vecs[7],
        own_out,
        own_vecs[0],
        own_vecs[1],
        own_vecs[2],
        own_up,
        own_up_bias,
        own_down,
        own_vecs[3],
        own_vecs[4],
        own_vecs[5],
        grad_head,
        root_squares,
    )


def solution(mesh):
    three = P(BOTH, None, None)
    two = P(BOTH, None)
    one = P(BOTH)
    placed = (
        three, one, two, P("table"), one, two, two, one, one, two, one, one, one, two, one, two, one, one, one, three,
        three, two,
    )
    results = (
        three, two, three, two, two, one, one, two, one, one, one, two, one, two, one, one, one, three, P(),
    )
    return jax.shard_map(body, mesh=mesh, in_specs=placed, out_specs=results, check_vma=False)
```

```python
import functools

import jax
import jax.numpy as jnp
from jax import lax
from jax.experimental import pallas as pl
from jax.experimental.pallas import tpu as pltpu
from jax.sharding import PartitionSpec as P

HEADS = 12
BLOCK = 8
NORM_EPS = 1e-05
MASKED = -1000000000.0
FAR = -3e38
PRECISE = lax.Precision.HIGHEST
TILE = 256
VMEM_BYTES = 64_000_000
BOTH = ("table", "batch")
F32 = jnp.float32
BF16 = jnp.bfloat16


def mm(left, right):
    return jnp.dot(left, right, preferred_element_type=F32)


def mm_t(left, right):
    return lax.dot_general(left, right, (((1,), (1,)), ((), ())), preferred_element_type=F32)


def t_mm(left, right):
    return lax.dot_general(left, right, (((0,), (0,)), ((), ())), preferred_element_type=F32)


def rowsum(values):
    return jnp.sum(values, axis=0, keepdims=True)


def norm_forward(hidden, gain, shift):
    average = jnp.mean(hidden, axis=-1, keepdims=True)
    centered = hidden - average
    variance = jnp.mean(centered * centered, axis=-1, keepdims=True)
    inv_std = lax.rsqrt(variance + NORM_EPS)
    standard = centered * inv_std
    return standard * gain + shift, standard, inv_std


def norm_backward(grad_norm, standard, inv_std, gain):
    scaled = grad_norm * gain
    return inv_std * (
        scaled
        - jnp.mean(scaled, axis=-1, keepdims=True)
        - standard * jnp.mean(scaled * standard, axis=-1, keepdims=True)
    )


def group_probs(query, tok, live_row, scale):
    size = tok.shape[0]
    row = lax.broadcasted_iota(jnp.int32, (size, size), 0) // BLOCK
    col = lax.broadcasted_iota(jnp.int32, (size, size), 1) // BLOCK
    scores = jnp.where(live_row > 0, mm_t(query, tok) * scale, MASKED)
    scores = jnp.where(row == col, scores, FAR)
    terms = jnp.exp(scores - jnp.max(scores, axis=-1, keepdims=True))
    return terms / jnp.sum(terms, axis=-1, keepdims=True), row == col


def merge_kernel(tok, live_row, live_col, merge_w, qkv_w, qkv_bias, query_out, hidden_out, attn_out, packed_out, squares):
    step = pl.program_id(0)
    scale = tok.shape[1] ** -0.5
    x = tok[...]
    live = live_col[...]
    query = mm(x, merge_w[...]).astype(BF16)
    query_out[...] = query
    probs, _ = group_probs(query, x, live_row[0], scale)
    merged = mm(probs.astype(BF16), x) * live
    wide = x.astype(F32)
    hidden = wide + merged
    hidden_out[...] = hidden
    attn_in = hidden.astype(BF16)
    attn_out[...] = attn_in
    packed_out[...] = (mm(attn_in, qkv_w[...]) + qkv_bias[...]).astype(BF16)

    @pl.when(step == 0)
    def _():
        squares[...] = jnp.zeros_like(squares)

    squares[0:1, :] += rowsum(live * wide * wide)
    squares[1:2, :] += rowsum(merged * merged)


def lane_mask(values, low, high):
    lane = lax.broadcasted_iota(jnp.int32, values.shape, 1)
    return jnp.where((lane >= low) & (lane < high), values, jnp.zeros_like(values))


def attn_kernel(scale, q_ref, k_ref, v_ref, bias_ref, ctx_ref, lse_ref):
    seq, lanes = q_ref.shape[1:]
    head = lanes // 2
    q = q_ref[0] * jnp.asarray(scale, BF16)
    k = k_ref[0]
    v_t = v_ref[0].T
    bias = bias_ref[0]
    for c in range(seq // TILE):
        rows = slice(c * TILE, (c + 1) * TILE)
        parts = []
        for h in range(2):
            scores = mm_t(k, lane_mask(q[rows], h * head, (h + 1) * head)) + bias
            top = jnp.max(scores, axis=0, keepdims=True)
            terms = jnp.exp(scores - top)
            total = jnp.sum(terms, axis=0, keepdims=True)
            probs = (terms * (1.0 / total)).astype(BF16)
            lse_ref[0, 0, h : h + 1, rows] = top + jnp.log(total)
            parts.append(mm(v_t[h * head : (h + 1) * head], probs))
        ctx_ref[0, rows, :] = jnp.concatenate(parts, axis=0).T.astype(BF16)


def attn_back_kernel(scale, q_ref, k_ref, v_ref, bias_ref, lse_ref, grad_ref, out_ref):
    seq, lanes = q_ref.shape[1:]
    head = lanes // 2
    q = q_ref[0] * jnp.asarray(scale, BF16)
    k = k_ref[0]
    v = v_ref[0]
    k_t = k.T
    bias = bias_ref[0]
    grad_k = jnp.zeros((seq, lanes), F32)
    grad_v = jnp.zeros((seq, lanes), F32)
    for c in range(seq // TILE):
        rows = slice(c * TILE, (c + 1) * TILE)
        parts = []
        for h in range(2):
            q_part = lane_mask(q[rows], h * head, (h + 1) * head)
            g_part = lane_mask(grad_ref[0, rows, :], h * head, (h + 1) * head)
            scores = mm_t(k, q_part) + bias
            probs = jnp.exp(scores - lse_ref[0, 0, h : h + 1, rows])
            grad_v += mm(probs.astype(BF16), g_part)
            grad_p = mm_t(v, g_part)
            grad_s = (probs * (grad_p - jnp.sum(probs * grad_p, axis=0, keepdims=True))).astype(BF16)
            grad_k += mm(grad_s, q_part)
            parts.append(mm(k_t[h * head : (h + 1) * head], grad_s))
        out_ref[0, 0, rows, :] = (jnp.concatenate(parts, axis=0).T * scale).astype(BF16)
    out_ref[1, 0] = grad_k.astype(BF16)
    out_ref[2, 0] = grad_v.astype(BF16)


def share_out(low, cols, value):
    rows = low.shape[4]
    spots = [(a, b, c, d) for a in range(low.shape[0]) for b in range(low.shape[1]) for c in range(low.shape[2]) for d in range(low.shape[3])]
    for i, spot in enumerate(spots):
        low[(*spot, slice(None), cols)] = value[i * rows : (i + 1) * rows].astype(BF16)


def attn_back_weights_kernel(
    scale, pairs, cuts, q, k, v, bias, lse, grad, ffn_in, grad_up, ctx, grad_attn, out_ref, low_up, low_out, turned
):
    step = pl.program_id(0) * pairs + pl.program_id(1)
    part = grad_up.shape[1]

    @pl.when(step == 0)
    def _():
        turned[...] = ffn_in[...].T

    @pl.when(step < cuts)
    def _():
        cols = pl.ds(pl.multiple_of(step * part, part), part)
        share_out(low_up, cols, mm(turned[...], grad_up[...]))

    @pl.when(step == cuts)
    def _():
        share_out(low_out, slice(None), mm(ctx[...].T, grad_attn[...]))

    attn_back_kernel(scale, q, k, v, bias, lse, grad, out_ref)


def qkv_grad_kernel(attn_in, grad, weight_grad, sums, turned):
    @pl.when(pl.program_id(0) == 0)
    def _():
        turned[...] = attn_in[...].T

    piece = grad[0]
    weight_grad[...] = mm(turned[...], piece).astype(BF16)
    sums[...] = jnp.broadcast_to(rowsum(piece.astype(F32)), sums.shape)


def ffn_kernel(
    per_row,
    ctx,
    hidden,
    cot,
    cls_grad,
    live_col,
    out_w,
    up_w,
    down_w,
    vecs,
    layer_out,
    activated,
    grad_up,
    ffn_in_out,
    grad_down_out,
    grad_attn_out,
    grad_two_out,
    grad_ctx_out,
    sums,
    up_sums,
    slope,
):
    step = pl.program_id(0)
    width = hidden.shape[1]
    chunks = up_w.shape[1] // width

    @pl.when(step == 0)
    def _():
        sums[...] = jnp.zeros_like(sums)
        up_sums[...] = jnp.zeros_like(up_sums)

    live = live_col[...]
    out_bias, gain_one, shift_one, down_bias, gain_two, shift_two = (vecs[i : i + 1, :width] for i in range(6))
    branch = mm(ctx[...], out_w[...]) + out_bias
    norm_one, standard_one, inv_one = norm_forward(hidden[...] + branch, gain_one, shift_one)
    ffn_in = norm_one.astype(BF16)
    ffn_in_out[...] = ffn_in
    down = jnp.zeros_like(norm_one)
    for j in range(chunks):
        cols = slice(j * width, (j + 1) * width)
        pre = mm(ffn_in, up_w[:, cols]) + vecs[6:7, cols]
        cumulative = 0.5 * (1.0 + lax.erf(pre * 0.7071067811865476))
        act = (pre * cumulative).astype(BF16)
        slope[:, cols] = cumulative + pre * (jnp.exp(-0.5 * pre * pre) * 0.3989422804014327)
        activated[:, cols] = act
        down += mm(act, down_w[cols, :])
    down += down_bias
    normed, standard_two, inv_two = norm_forward(norm_one + down, gain_two, shift_two)
    result = (normed * live).astype(BF16)
    layer_out[...] = result
    wide = result.astype(F32)
    sums[5:6, :] += rowsum(live * branch * branch)
    sums[6:7, :] += rowsum(live * down * down)
    sums[7:8, :] += rowsum(wide * wide)
    first = (lax.broadcasted_iota(jnp.int32, (hidden.shape[0], 1), 0) == 0) & (step % per_row == 0)
    grad = live * (cot[...].astype(F32) + jnp.where(first, cls_grad[0], 0.0))
    sums[0:1, :] += rowsum(grad * standard_two)
    sums[1:2, :] += rowsum(grad)
    grad_three = norm_backward(grad, standard_two, inv_two, gain_two)
    grad_down = grad_three.astype(BF16)
    grad_down_out[...] = grad_down
    sums[2:3, :] += rowsum(grad_down.astype(F32))
    total = grad_three
    for j in range(chunks):
        cols = slice(j * width, (j + 1) * width)
        piece = (mm_t(grad_down, down_w[cols, :]) * slope[:, cols]).astype(BF16)
        grad_up[:, cols] = piece
        up_sums[0:1, cols] += rowsum(piece.astype(F32))
        total += mm_t(piece, up_w[:, cols])
    sums[3:4, :] += rowsum(total * standard_one)
    sums[4:5, :] += rowsum(total)
    grad_two = norm_backward(total, standard_one, inv_one, gain_one)
    grad_two_out[...] = grad_two
    grad_attn = grad_two.astype(BF16)
    grad_attn_out[...] = grad_attn
    sums[8:9, :] += rowsum(grad_attn.astype(F32))
    grad_ctx_out[...] = mm_t(grad_attn, out_w[...]).astype(BF16)


def input_kernel(
    grad_qkv, grad_two, tok, query, live_row, live_col, merge_w, qkv_w, grad_input, merge_grad
):
    step = pl.program_id(0)
    width = tok.shape[1]
    scale = width**-0.5

    @pl.when(step == 0)
    def _():
        merge_grad[...] = jnp.zeros_like(merge_grad)

    x = tok[...]
    grad_one = grad_two[...]
    for i in range(3):
        cols = slice(i * width, (i + 1) * width)
        grad_one += mm_t(grad_qkv[i], qkv_w[:, cols])
    grad_merged = (grad_one * live_col[...]).astype(BF16)
    mq = query[...]
    probs, same = group_probs(mq, x, live_row[0], scale)
    grad_probs = mm_t(grad_merged, x)
    grad_scores = probs * (grad_probs - jnp.sum(probs * grad_probs, axis=-1, keepdims=True))
    grad_scores = jnp.where(same & (live_row[0] > 0), grad_scores, 0.0)
    grad_query = (mm(grad_scores.astype(BF16), x) * scale).astype(BF16)
    merge_grad[...] += mm(x.T, grad_query)
    blocks = mm(probs.T.astype(BF16), grad_merged) + mm(grad_scores.T.astype(BF16), mq) * scale
    blocks += mm_t(grad_query, merge_w[...])
    grad_input[...] = (grad_one + blocks).astype(BF16)


def params(**kw):
    return pltpu.CompilerParams(vmem_limit_bytes=VMEM_BYTES, **kw)


def fixed(shape):
    zeros = (0,) * len(shape)
    return pl.BlockSpec(shape, lambda *_: zeros, pipeline_mode=pl.Buffered(1))


def tiled(size, width):
    return pl.BlockSpec((size, width), lambda i: (i, 0))


MESH = pl.DeviceIdType.MESH
TABLE_MAJOR = 4
UP_CUTS = 6
ATTN_PACE, BACK_PACE, LAST_PACE = 3.0, 2.7, 2.5
CORES = 2


def here(dims):
    table, batch = lax.axis_index("table"), lax.axis_index("batch")
    return [table // dims[1], lax.rem(table, dims[1]), batch // CORES, lax.rem(batch, CORES)]


def peer(dims, spot, axis, offset):
    other = list(spot)
    other[axis] = lax.rem(spot[axis] + offset, dims[axis])
    return (other[0] * dims[1] + other[1], other[2] * CORES + other[3]), other[axis]


def greet(dims, spot):
    barrier = pltpu.get_barrier_semaphore()
    total = 0
    for axis in range(4):
        for offset in range(1, dims[axis]):
            target, _ = peer(dims, spot, axis, offset)
            pl.semaphore_signal(barrier, inc=1, device_id=target, device_id_type=MESH)
            total += 1
    pl.semaphore_wait(barrier, total)


def gather_events(dims, spot, items, shards, fulls, local_sem, send_sem, recv_sem):
    def region(item, done):
        array, low, size, order = items[item]
        where = tuple(slice(None) if axis in done else spot[axis] for axis in sorted(order))
        return fulls[array].at[(*where, pl.ds(low, size))]

    def copies(item, stage):
        array, low, size, order = items[item]
        place = region(item, order[:stage])
        return [
            pltpu.make_async_remote_copy(
                src_ref=place if stage else shards[array].at[pl.ds(low, size)],
                dst_ref=place,
                send_sem=send_sem.at[item, stage, offset],
                recv_sem=recv_sem.at[item, stage, offset],
                device_id=peer(dims, spot, order[stage], offset)[0],
                device_id_type=MESH,
            )
            for offset in range(1, dims[order[stage]])
        ]

    def keep(item):
        array, low, size, _ = items[item]
        return pltpu.make_async_copy(shards[array].at[pl.ds(low, size)], region(item, ()), local_sem.at[item])

    def begin():
        for item in range(len(items)):
            keep(item).start()
            for copy in copies(item, 0):
                copy.start()

    def advance(item, stage):
        for copy in copies(item, stage):
            copy.wait_recv()
        if stage == 0:
            keep(item).wait()
        if stage + 1 < len(items[item][3]):
            for copy in copies(item, stage + 1):
                copy.start()

    def end():
        for item in range(len(items)):
            for stage in range(len(items[item][3])):
                for copy in copies(item, stage):
                    copy.wait_send()

    return begin, slots(items, advance), end


def slots(items, advance):
    count = len(items)
    pairs = (count + 1) // 2
    groups = []
    for slot in range(pairs + 3):
        group = []
        for stage in (3, 2, 1, 0):
            pair = slot - stage
            for item in range(2 * pair, min(2 * pair + 2, count)) if 0 <= pair < pairs else ():
                if stage < len(items[item][3]):
                    group.append(functools.partial(advance, item, stage))
        groups.append(group)
    return groups


def scatter_events(dims, spot, items, grads, outs, buffers, local_sem, send_sem, recv_sem):
    buffers = [buffers[i * 7 : (i + 1) * 7] for i in range(len(items))]

    def piece(item, core):
        array, low, size, _ = items[item]
        if size <= grads[array].shape[4]:
            return grads[array].at[:, :, :, core, pl.ds(low, size)]
        return grads[array].at[:, :, :, core, :, pl.ds(low, size)]

    def load(item):
        return pltpu.make_async_copy(
            piece(item, spot[3]), buffers[item][0], local_sem.at[item]
        )

    def copies(item, stage):
        array, low, size, order = items[item]
        own, first, second, got_core, got_first, got_second, got_last = buffers[item]
        axis = order[stage]
        made = []
        for offset in range(1, dims[axis]):
            target, other = peer(dims, spot, axis, offset)
            if stage == 0:
                source, landing = piece(item, other), got_core
            elif stage == 1:
                source = own.at[:, :, other] if axis == 2 else own.at[:, other]
                landing = got_first.at[offset - 1]
            elif stage == 2:
                source, landing = first.at[:, other], got_second.at[offset - 1]
            else:
                source, landing = second.at[other], got_last.at[offset - 1]
            made.append(
                pltpu.make_async_remote_copy(
                    src_ref=source,
                    dst_ref=landing,
                    send_sem=send_sem.at[item, stage, offset],
                    recv_sem=recv_sem.at[item, stage, offset],
                    device_id=target,
                    device_id_type=MESH,
                )
            )
        return made

    def begin(chosen=tuple(range(len(items)))):
        for item in chosen:
            load(item).start()
            for copy in copies(item, 0):
                copy.start()

    def advance(item, stage):
        array, low, size, order = items[item]
        own, first, second, got_core, got_first, got_second, got_last = buffers[item]
        axis = order[stage]
        others = range(dims[axis] - 1)
        mine = spot[axis]
        for copy in copies(item, stage):
            copy.wait_recv()
        if stage == 0:
            load(item).wait()

            @pl.loop(0, dims[0] * dims[1] * dims[2])
            def _(i):
                at = (i // (dims[1] * dims[2]), lax.rem(i // dims[2], dims[1]), lax.rem(i, dims[2]))
                own[at] = (own[at].astype(F32) + got_core[at].astype(F32)).astype(BF16)
        elif stage == 1:
            inner = first.shape[1]

            @pl.loop(0, dims[0] * inner)
            def _(i):
                at = (i // inner, lax.rem(i, inner))
                value = own[(*at, mine) if axis == 2 else (at[0], mine, at[1])].astype(F32)
                for k in others:
                    value += got_first[(k, *at)].astype(F32)
                first[at] = value.astype(BF16)
        elif stage == 2:

            @pl.loop(0, dims[0])
            def _(i):
                value = first[i, mine].astype(F32)
                for k in others:
                    value += got_second[k, i].astype(F32)
                second[i] = value.astype(BF16)
        else:
            value = second[mine].astype(F32)
            for k in others:
                value += got_last[k].astype(F32)
            if size <= grads[array].shape[4]:
                outs[array][low : low + size] = value
            else:
                outs[array][:, low : low + size] = value
        if stage < 3:
            for copy in copies(item, stage + 1):
                copy.start()

    def end():
        for item in range(len(items)):
            for stage in range(4):
                for copy in copies(item, stage):
                    copy.wait_send()

    return begin, slots(items, advance), end


def square_events(dims, spot, square, total, kept, got, send_sem, recv_sem):
    def copies(stage):
        axis = 3 - stage
        return [
            pltpu.make_async_remote_copy(
                src_ref=kept.at[stage],
                dst_ref=got.at[stage, offset - 1],
                send_sem=send_sem.at[stage, offset],
                recv_sem=recv_sem.at[stage, offset],
                device_id=peer(dims, spot, axis, offset)[0],
                device_id_type=MESH,
            )
            for offset in range(1, dims[axis])
        ]

    def begin():
        kept[0] = square[...]
        for copy in copies(0):
            copy.start()

    def advance(stage):
        for copy in copies(stage):
            copy.wait_recv()
        value = kept[stage]
        for offset in range(1, dims[3 - stage]):
            value = value + got[stage, offset - 1]
        kept[stage + 1] = value
        if stage < 3:
            for copy in copies(stage + 1):
                copy.start()
        else:
            total[...] = value

    def end():
        for stage in range(4):
            for copy in copies(stage):
                copy.wait_send()

    return begin, [[functools.partial(advance, stage)] for stage in range(4)], end


def scatter_scratch(dims, grads, items):
    scratch = []
    for array, _, size, order in items:
        rows, cols = grads[array].shape[4:]
        tail = (size, cols) if size <= rows else (rows, size)
        inner = dims[order[2]]
        for shape in (
            dims[:3],
            (dims[0], inner),
            (dims[0],),
            dims[:3],
            (dims[order[1]] - 1, dims[0], inner),
            (inner - 1, dims[0]),
            (dims[0] - 1,),
        ):
            scratch.append(pltpu.VMEM((*shape, *tail), BF16))
    return scratch


def links(count, most):
    return [pltpu.SemaphoreType.DMA((count, 4, most)), pltpu.SemaphoreType.DMA((count, 4, most))]


def split(array, size, pieces, *orders):
    part = size // pieces
    return [(array, i * part, part, orders[i % len(orders)]) for i in range(pieces)]


def plain_call(kernel, grid, refs, outs, name):
    return pl.pallas_call(
        kernel,
        grid=grid,
        in_specs=[spec for spec, _ in refs],
        out_specs=[spec for spec, _ in outs],
        out_shape=[shape for _, shape in outs],
        compiler_params=params(),
        name=name,
    )(*(arg for _, arg in refs))


def moving_call(dims, collective_id, name, kernel, grid, own_in, own_out, gather, scatter, square, pace=1.0, made=(), early=(), after=None, extra=()):
    most = max(dims)
    total = dims[0] * dims[1] * dims[2] * dims[3]
    vmem, anywhere = (lambda a: fixed(a.shape)), (lambda a: pl.BlockSpec(memory_space=pl.ANY))
    shards, gather_items = gather
    grads, scatter_items = scatter
    squares = [] if square is None else [square]
    in_specs, args = [spec for spec, _ in own_in], [arg for _, arg in own_in]
    in_specs += [vmem(a) for a in shards] + [anywhere(a) for a in grads] + [vmem(a) for a in squares]
    args += [*shards, *grads, *squares]
    out_specs, out_shape = [spec for spec, _ in own_out], [shape for _, shape in own_out]
    orders = {array: sorted(order) for array, _, _, order in gather_items}
    for i, a in enumerate(shards):
        out_specs.append(anywhere(a))
        out_shape.append(jax.ShapeDtypeStruct((*(dims[axis] for axis in orders[i]), *a.shape), a.dtype))
    whole = [*grads, *early]
    after = after or {}
    for g in whole:
        out_shape.append(jax.ShapeDtypeStruct(g.shape[4:], F32))
        out_specs.append(vmem(out_shape[-1]))
    for g in made:
        out_shape.append(jax.ShapeDtypeStruct((g.shape[0] // total, g.shape[1]), F32))
        out_specs.append(vmem(out_shape[-1]))
    for q in squares:
        out_shape.append(jax.ShapeDtypeStruct(q.shape, F32))
        out_specs.append(vmem(q))
    groups = []
    if shards:
        groups.append([pltpu.SemaphoreType.DMA((len(gather_items),)), *links(len(gather_items), most)])
    if grads:
        buffers = scatter_scratch(dims, whole, scatter_items)
        groups.append([*extra, *(pltpu.VMEM(g.shape, BF16) for g in early), *buffers, pltpu.SemaphoreType.DMA((len(scatter_items),)), *links(len(scatter_items), most)])
    if squares:
        groups.append(
            [
                pltpu.VMEM((5, *square.shape), F32),
                pltpu.VMEM((4, most - 1, *square.shape), F32),
                pltpu.SemaphoreType.DMA((4, most)),
                pltpu.SemaphoreType.DMA((4, most)),
            ]
        )
    if made:
        made_shapes = [jax.ShapeDtypeStruct((*dims, g.shape[0] // total, g.shape[1]), BF16) for g in made]
        made_items = [(i, 0, g.shape[4], (3, 2, 1, 0) if i % 2 == 0 else (3, 1, 2, 0)) for i, g in enumerate(made_shapes)]
        buffers = [pltpu.VMEM(g.shape, F32) for g in made] + [pltpu.VMEM(g.shape, BF16) for g in made_shapes]
        buffers += scatter_scratch(dims, made_shapes, made_items)
        groups.append([*buffers, pltpu.SemaphoreType.DMA((len(made),)), *links(len(made), most)])
    steps = 1
    for size in grid:
        steps *= size

    def fused(*refs):
        refs = list(refs)

        def take(n):
            taken = refs[:n]
            del refs[:n]
            return taken

        ins, shard_refs, grad_refs, square_refs = take(len(own_in)), take(len(shards)), take(len(grads)), take(len(squares))
        outs, full_refs, sum_refs = take(len(own_out)), take(len(shards)), take(len(whole))
        made_outs, total_refs = take(len(made)), take(len(squares))
        step = 0
        for axis, size in enumerate(grid):
            step = step * size + pl.program_id(axis)
        spot = here(dims)
        plans = []
        scratch = iter(groups)
        if shards:
            plans.append(gather_events(dims, spot, gather_items, shard_refs, full_refs, *take(len(next(scratch)))))
        if grads:
            held = take(len(next(scratch)))
            turned, held = held[: len(extra)], held[len(extra) :]
            early_refs, held = held[: len(early)], held[len(early) :]
            begin_some, some_groups, end_some = scatter_events(
                dims, spot, scatter_items, grad_refs + early_refs, sum_refs, held[:-3], *held[-3:]
            )
            ready = [item for item in range(len(scatter_items)) if item not in after]
            plans.append((functools.partial(begin_some, ready), some_groups, end_some))
        else:
            turned, early_refs = [], []
        if squares:
            plans.append(square_events(dims, spot, *square_refs, *total_refs, *take(len(next(scratch)))))

        if made:
            held = take(len(next(scratch)))
            sums, lows = held[: len(made)], held[len(made) : 2 * len(made)]
            begin_made, made_groups, end_made = scatter_events(
                dims, spot, made_items, lows, made_outs, held[2 * len(made) : -3], *held[-3:]
            )
        else:
            sums, made_groups = [], []

        def round_made():
            for value, low in zip(sums, lows):
                rows = low.shape[4]

                @pl.loop(0, total)
                def _(i):
                    at = (
                        i // (dims[1] * dims[2] * dims[3]),
                        lax.rem(i // (dims[2] * dims[3]), dims[1]),
                        lax.rem(i // dims[3], dims[2]),
                        lax.rem(i, dims[3]),
                    )
                    low[at] = value[pl.ds(pl.multiple_of(i * rows, rows), rows), :].astype(BF16)

        def open_all():
            greet(dims, spot)
            for begin, _, _ in plans:
                begin()

        depth = max(len(groups_of) for _, groups_of, _ in plans)
        merged = [[e for _, groups_of, _ in plans if i < len(groups_of) for e in groups_of[i]] for i in range(depth)]

        def close_all():
            for _, _, end in plans:
                end()

        if steps == 1:
            open_all()
            for group in merged:
                for event in group:
                    event()
            close_all()
            return
        late = []
        pl.when(step == 0)(open_all)
        for i, group in enumerate(merged):
            at = int((i + 1) * pace)

            def run(group=group):
                for event in group:
                    event()

            if at < steps:
                pl.when(step == at)(run)
            else:
                late.append(run)
        kernel(*ins, *outs, *sums, *early_refs, *turned)
        for item, at in after.items():
            pl.when(step == at)(functools.partial(begin_some, (item,)))

        @pl.when(step == steps - 1)
        def _():
            if made:
                round_made()
                begin_made()
            for i in range(max(len(late), len(made_groups))):
                if i < len(late):
                    late[i]()
                for event in made_groups[i] if i < len(made_groups) else ():
                    event()
            close_all()
            if made:
                end_made()

    return pl.pallas_call(
        fused,
        grid=grid,
        in_specs=in_specs,
        out_specs=out_specs,
        out_shape=out_shape,
        scratch_shapes=[piece for group in groups for piece in group],
        compiler_params=params(collective_id=collective_id, has_side_effects=True),
        name=name,
    )(*args)


def body(
    tokens,
    row_blocks,
    block_fill,
    row_table,
    class_count,
    merge_w,
    qkv_w,
    query_bias,
    value_bias,
    out_w,
    out_bias,
    gain_one,
    shift_one,
    up_w,
    up_bias,
    down_w,
    down_bias,
    gain_two,
    shift_two,
    head_w,
    cotangent,
    logit_cotangent,
):
    rows, seq, width = tokens.shape
    count = rows * seq
    ff = up_w.shape[1]
    head = width // HEADS
    per_row = seq // TILE
    tiles = count // TILE
    share = merge_w.shape[0]
    devices = width // share
    wide_ff = ff // width

    def cut(mat, n):
        return [mat[:, i * width : (i + 1) * width] for i in range(n)]

    table_size, batch_size = lax.axis_size("table"), lax.axis_size("batch")
    dims = (TABLE_MAJOR, table_size // TABLE_MAJOR, batch_size // CORES, CORES)
    direct = share % BLOCK == 0
    vec_list = (out_bias, gain_one, shift_one, down_bias, gain_two, shift_two, query_bias, value_bias)
    used = 8 * share + up_bias.shape[0]
    spare = jnp.zeros((8 * width - used,), F32)
    vec_row = jnp.concatenate([*(v.astype(F32) for v in (*vec_list, up_bias)), spare])
    vec_row = vec_row.reshape(8, width).astype(BF16)
    base = (5 + wide_ff) * share
    down_out, up_out = (0, 1, 2, 3), (0, 2, 1, 3)
    down_in, up_in = (3, 1, 2, 0), (3, 2, 1, 0)
    none = ((), ())
    if direct:
        qkv_full, merge_full, vec_full = moving_call(
            dims,
            0,
            "gather_first",
            None,
            (1,),
            [],
            [],
            (
                (qkv_w, merge_w, vec_row),
                (
                    (1, 0, share, down_out),
                    *split(0, share, 3, up_out, down_out),
                    (2, 0, 8, up_out),
                ),
            ),
            none,
            None,
        )
        qkv_full = qkv_full.reshape(width, 3 * width)
        merge_full = merge_full.reshape(width, width)
        vec_rows = vec_full.reshape(devices, 8, width)[:, 0].astype(F32)
    else:
        mine = jnp.concatenate([merge_w, out_w, *cut(qkv_w, 3), *cut(up_w, wide_ff), down_w, vec_row], axis=0)
        gathered = lax.all_gather(mine, BOTH, axis=0)

        def unit(start, n):
            part = gathered[:, start : start + n * share]
            part = part.reshape(devices, n, share, width).transpose(0, 2, 1, 3)
            return part.reshape(width, n * width)

        merge_full = unit(0, 1)
        out_full = unit(share, 1)
        qkv_full = unit(2 * share, 3)
        up_full = unit(5 * share, wide_ff)
        down_full = gathered[:, base : base + wide_ff * share].reshape(ff, width)
        vec_rows = gathered[:, base + wide_ff * share].astype(F32)
    vectors = [vec_rows[:, i * share : (i + 1) * share].reshape(1, width) for i in range(8)]
    up_bias_full = vec_rows[:, 8 * share : 8 * share + wide_ff * share].reshape(1, ff)
    query_vec, value_vec = vectors[6], vectors[7]
    qkv_bias = jnp.concatenate([query_vec, jnp.zeros_like(query_vec), value_vec], axis=1)
    vecs = jnp.concatenate(
        [jnp.pad(jnp.concatenate(vectors[:6], axis=0), ((0, 0), (0, ff - width))), up_bias_full, jnp.zeros((1, ff), F32)],
        axis=0,
    )

    position = jnp.arange(seq, dtype=jnp.int32)
    fill_tok = jnp.repeat(block_fill, BLOCK, axis=1)
    live = ((position // BLOCK)[None, :] < row_blocks[:, None]) & ((position % BLOCK)[None, :] < fill_tok)
    live_mask = live.astype(F32)
    live_col = live_mask.reshape(count, 1)
    live_row = live_mask.reshape(tiles, 1, TILE)
    key_bias = jnp.where(live, 0.0, MASKED).astype(F32).reshape(rows, seq, 1)

    batch = lax.axis_size("batch")
    classes = head_w.shape[2]
    tok_flat = tokens.reshape(count, width)
    cot_flat = cotangent.reshape(count, width)
    merge_query, hidden, attn_in, packed, squares = pl.pallas_call(
        merge_kernel,
        grid=(tiles,),
        in_specs=[
            tiled(TILE, width),
            pl.BlockSpec((1, 1, TILE), lambda i: (i, 0, 0)),
            tiled(TILE, 1),
            fixed((width, width)),
            fixed((width, 3 * width)),
            fixed((1, 3 * width)),
        ],
        out_specs=[
            tiled(TILE, width),
            tiled(TILE, width),
            tiled(TILE, width),
            tiled(TILE, 3 * width),
            fixed((8, width)),
        ],
        out_shape=[
            jax.ShapeDtypeStruct((count, width), BF16),
            jax.ShapeDtypeStruct((count, width), F32),
            jax.ShapeDtypeStruct((count, width), BF16),
            jax.ShapeDtypeStruct((count, 3 * width), BF16),
            jax.ShapeDtypeStruct((8, width), F32),
        ],
        compiler_params=params(),
        name="merge_qkv",
    )(tok_flat, live_row, live_col, merge_full, qkv_full, qkv_bias)

    packed_rows = packed.reshape(rows, seq, 3 * width)
    pairs = HEADS // 2
    lanes = 2 * head

    def head_block(offset):
        return pl.BlockSpec((1, seq, lanes), lambda r, p: (r, 0, p + offset))

    bias_block = pl.BlockSpec((1, seq, 1), lambda r, p: (r, 0, 0))
    lse_block = pl.BlockSpec((1, 1, 2, seq), lambda r, p: (r, p, 0, 0))
    attn_in_refs = [
        (head_block(0), packed_rows),
        (head_block(pairs), packed_rows),
        (head_block(2 * pairs), packed_rows),
        (bias_block, key_bias),
    ]
    attn_outs = [
        (head_block(0), jax.ShapeDtypeStruct((rows, seq, width), BF16)),
        (lse_block, jax.ShapeDtypeStruct((rows, pairs, 2, seq), F32)),
    ]
    attend = functools.partial(attn_kernel, head**-0.5)
    if direct:
        limit = jnp.broadcast_to(class_count.astype(F32)[:, None], (1, classes))
        spare = -(rows + 1) % 8
        small = jnp.concatenate([logit_cotangent, limit, jnp.zeros((spare, classes), F32)], axis=0)
        up_items, down_items = split(0, share, 3, up_out), split(1, wide_ff * share, 3, down_out)
        gather_items = [
            *(up_items[0], down_items[0], up_items[1], down_items[1]),
            (2, 0, share, (2, 1, 0, 3)),
            (3, 0, width, (2, 3)),
            *(up_items[2], down_items[2]),
            (4, 0, small.shape[0], (2, 3)),
        ]
        context, lse, up_full, down_full, out_full, heads, small = moving_call(
            dims,
            2,
            "attention_gather",
            attend,
            (rows, pairs),
            attn_in_refs,
            attn_outs,
            ((up_w, down_w, out_w, head_w[0], small), gather_items),
            none,
            None,
            pace=ATTN_PACE,
        )
        up_full = up_full.reshape(width, ff)
        down_full = down_full.reshape(ff, width)
        out_full = out_full.reshape(width, width)
        heads = heads.reshape(batch, width, classes)
        small = small.reshape(batch, -1, classes)
        group_dlog_raw = small[:, :rows].reshape(batch * rows, classes)
        counts = small[:, rows, 0]
    else:
        context, lse = pl.pallas_call(
            attend,
            grid=(rows, pairs),
            in_specs=[spec for spec, _ in attn_in_refs],
            out_specs=[spec for spec, _ in attn_outs],
            out_shape=[shape for _, shape in attn_outs],
            compiler_params=params(),
            name="attention",
        )(*(arg for _, arg in attn_in_refs))
        heads = lax.all_gather(head_w[0], "batch", axis=0)
        counts = lax.all_gather(class_count, "batch", axis=0, tiled=True)
        group_dlog_raw = lax.all_gather(logit_cotangent, "batch", axis=0, tiled=True)
    own = lax.axis_index("batch")
    my_table = lax.dynamic_slice(row_table, (own * rows,), (rows,))
    class_ids = jnp.arange(classes, dtype=jnp.int32)
    my_select = (my_table[:, None] == jnp.arange(batch, dtype=jnp.int32)[None, :]).astype(F32)
    my_class = (class_ids[None, :] < (my_select * counts[None, :].astype(F32)).sum(1, keepdims=True)).astype(F32)
    my_dlog = logit_cotangent * my_class
    picked = (my_select[:, :, None] * my_dlog[:, None, :]).transpose(1, 0, 2)
    cls_grad = jnp.sum(
        lax.dot_general(picked, heads.astype(F32), (((2,), (2,)), ((0,), (0,))), precision=PRECISE), axis=0
    )

    context = context.reshape(count, width)
    (layer_out, activated, grad_up, ffn_in, grad_down, grad_attn, grad_two, grad_ctx, sums, up_sums) = pl.pallas_call(
        functools.partial(ffn_kernel, per_row),
        grid=(tiles,),
        in_specs=[
            tiled(TILE, width),
            tiled(TILE, width),
            tiled(TILE, width),
            pl.BlockSpec((1, 1, width), lambda i: (i // per_row, 0, 0)),
            tiled(TILE, 1),
            fixed((width, width)),
            fixed((width, ff)),
            fixed((ff, width)),
            fixed((8, ff)),
        ],
        out_specs=[
            tiled(TILE, width),
            tiled(TILE, ff),
            tiled(TILE, ff),
            tiled(TILE, width),
            tiled(TILE, width),
            tiled(TILE, width),
            tiled(TILE, width),
            tiled(TILE, width),
            fixed((16, width)),
            fixed((8, ff)),
        ],
        out_shape=[
            jax.ShapeDtypeStruct((count, width), BF16),
            jax.ShapeDtypeStruct((count, ff), BF16),
            jax.ShapeDtypeStruct((count, ff), BF16),
            jax.ShapeDtypeStruct((count, width), BF16),
            jax.ShapeDtypeStruct((count, width), BF16),
            jax.ShapeDtypeStruct((count, width), BF16),
            jax.ShapeDtypeStruct((count, width), F32),
            jax.ShapeDtypeStruct((count, width), BF16),
            jax.ShapeDtypeStruct((16, width), F32),
            jax.ShapeDtypeStruct((8, ff), F32),
        ],
        scratch_shapes=[pltpu.VMEM((TILE, ff), F32)],
        compiler_params=params(),
        name="ffn",
    )(context, hidden, cot_flat, cls_grad.reshape(rows, 1, width), live_col, out_full, up_full, down_full, vecs)

    grad_rows = grad_ctx.reshape(rows, seq, width)
    cls_rows = layer_out.reshape(rows, seq, width)[:, 0, :]
    back_refs = [*attn_in_refs, (lse_block, lse), (head_block(0), grad_rows)]
    back_outs = [
        (
            pl.BlockSpec((3, 1, seq, lanes), lambda r, p: (0, r, 0, p)),
            jax.ShapeDtypeStruct((3, rows, seq, width), BF16),
        )
    ]
    grad_down_w = t_mm(activated, grad_down).astype(BF16)
    if direct:
        part = ff // UP_CUTS
        back_refs += [
            (fixed((count, width)), ffn_in),
            (pl.BlockSpec((count, part), lambda r, p: (0, jnp.minimum(r * pairs + p, UP_CUTS - 1))), grad_up),
            (fixed((count, width)), context),
            (fixed((count, width)), grad_attn),
        ]
        ffn_items = [
            *split(0, wide_ff * share, 3, up_in, down_in),
            *split(1, ff, 3, down_in, up_in),
            (2, 0, share, up_in),
        ]
        first_rows = jnp.pad(cls_rows, ((0, -rows % 8), (0, 0)))
        grad_qkv, group_cls, own_down, own_up, own_out = moving_call(
            dims,
            3,
            "attention_back_scatter",
            functools.partial(attn_back_weights_kernel, head**-0.5, pairs, UP_CUTS),
            (rows, pairs),
            back_refs,
            back_outs,
            ((first_rows,), ((0, 0, first_rows.shape[0], (2, 3)),)),
            ([grad_down_w.reshape(*dims, -1, width)], ffn_items),
            None,
            pace=BACK_PACE,
            early=(jax.ShapeDtypeStruct((*dims, share, ff), BF16), jax.ShapeDtypeStruct((*dims, share, width), BF16)),
            after={3: UP_CUTS // 3 - 1, 4: 2 * UP_CUTS // 3 - 1, 5: UP_CUTS - 1, 6: UP_CUTS},
            extra=(pltpu.VMEM((width, count), BF16),),
        )
        group_cls = group_cls.reshape(batch, -1, width)[:, :rows].reshape(batch * rows, width)
    else:
        grad_out_w = t_mm(context, grad_attn).astype(BF16)
        grad_up_w = t_mm(ffn_in, grad_up).astype(BF16)
        attend_back = functools.partial(attn_back_kernel, head**-0.5)
        (grad_qkv,) = plain_call(attend_back, (rows, pairs), back_refs, back_outs, "attention_back")
        group_cls = lax.all_gather(cls_rows, "batch", axis=0, tiled=True)

    grad_qkv = grad_qkv.reshape(3, count, width)
    grad_qkv_w, qkv_sums = pl.pallas_call(
        qkv_grad_kernel,
        grid=(3,),
        in_specs=[fixed((count, width)), pl.BlockSpec((1, count, width), lambda i: (i, 0, 0))],
        out_specs=[pl.BlockSpec((width, width), lambda i: (0, i)), pl.BlockSpec((8, width), lambda i: (0, i))],
        out_shape=[jax.ShapeDtypeStruct((width, 3 * width), BF16), jax.ShapeDtypeStruct((8, 3 * width), F32)],
        scratch_shapes=[pltpu.VMEM((width, count), BF16)],
        compiler_params=params(),
        name="qkv_grad",
    )(attn_in, grad_qkv)
    bias_sums = [qkv_sums[0, :width], qkv_sums[0, 2 * width :]]
    input_refs = [
        (pl.BlockSpec((3, TILE, width), lambda i: (0, i, 0)), grad_qkv),
        *((tiled(TILE, width), a) for a in (grad_two, tok_flat, merge_query)),
        (pl.BlockSpec((1, 1, TILE), lambda i: (i, 0, 0)), live_row),
        (tiled(TILE, 1), live_col),
        (fixed((width, width)), merge_full),
        (fixed((width, 3 * width)), qkv_full),
    ]
    input_outs = [(tiled(TILE, width), jax.ShapeDtypeStruct((count, width), BF16))]
    merge_grad = jax.ShapeDtypeStruct((width, width), F32)

    vec_grads = (sums[8], sums[3], sums[4], sums[2], sums[0], sums[1], bias_sums[0], bias_sums[1])
    vec_block = jnp.concatenate(
        [v.reshape(devices, share) for v in vec_grads] + [up_sums[0].reshape(devices, wide_ff * share)], axis=1
    )
    vec_block = jnp.pad(vec_block, ((0, 0), (0, 8 * width - used))).astype(BF16).reshape(devices, 8, width)
    live_sums = jnp.sum(live_mask.reshape(-1, width), axis=0, keepdims=True)
    square = jnp.concatenate([squares[:2], sums[5:8], live_sums, jnp.zeros((2, width), F32)], axis=0)
    if direct:
        grad_input, own_qkv, own_vec, own_merge, square = moving_call(
            dims,
            1,
            "merge_back_scatter",
            input_kernel,
            (tiles,),
            input_refs,
            input_outs,
            none,
            (
                [g.reshape(*dims, -1, g.shape[-1]) for g in (grad_qkv_w, vec_block)],
                (*split(0, share, 3, up_in, down_in), (1, 0, 8, down_in)),
            ),
            square,
            pace=LAST_PACE,
            made=(merge_grad,),
        )
        own_vec = own_vec[0]
    else:
        input_outs.append((fixed((width, width)), merge_grad))
        grad_input, grad_merge_w = plain_call(input_kernel, (tiles,), input_refs, input_outs, "merge_back")
        grad_merge_w = grad_merge_w.astype(BF16)

        def owners(mat, n):
            return mat.reshape(devices, share, n, width).transpose(0, 2, 1, 3).reshape(devices, n * share, width)


        all_grads = jnp.concatenate(
            [
                owners(grad_merge_w, 1),
                owners(grad_out_w, 1),
                owners(grad_qkv_w, 3),
                owners(grad_up_w, wide_ff),
                grad_down_w.reshape(devices, wide_ff * share, width),
                vec_block,
            ],
            axis=1,
        )
        owned = lax.psum_scatter(all_grads, BOTH, scatter_dimension=0, tiled=True)[0].astype(F32)

        def joined(start, n):
            return jnp.concatenate([owned[start + i * share : start + (i + 1) * share] for i in range(n)], axis=1)

        own_vec = owned[base + wide_ff * share]
        own_merge, own_qkv, own_out, own_up = joined(0, 1), joined(2 * share, 3), joined(share, 1), joined(5 * share, wide_ff)
        own_down = owned[base : base + wide_ff * share]
        square = lax.psum(square, BOTH)
    own_vecs = [own_vec[i * share : (i + 1) * share] for i in range(8)]
    own_up_bias = own_vec[8 * share : 8 * share + wide_ff * share]

    layer_rows = layer_out.reshape(rows, seq, width)
    my_logits = jnp.sum(
        my_select[:, :, None] * jnp.einsum("rd,kdc->rkc", cls_rows, heads, preferred_element_type=F32), axis=1
    )
    logits = my_logits * my_class
    owner_mask = (row_table == own).astype(F32)[:, None]
    class_live = (class_ids < class_count[0]).astype(F32)[None, :]
    group_dlog = group_dlog_raw * (owner_mask * class_live)
    grad_head = lax.dot_general(
        group_cls.astype(F32), group_dlog, (((0,), (0,)), ((), ())), precision=PRECISE, preferred_element_type=F32
    )[None]
    totals = jnp.sum(square[:6], axis=1)
    root_squares = jnp.sqrt(totals[:5] / (totals[5] * width))
    return (
        layer_rows,
        logits,
        grad_input.reshape(rows, seq, width),
        own_merge,
        own_qkv,
        own_vecs[6],
        own_vecs[7],
        own_out,
        own_vecs[0],
        own_vecs[1],
        own_vecs[2],
        own_up,
        own_up_bias,
        own_down,
        own_vecs[3],
        own_vecs[4],
        own_vecs[5],
        grad_head,
        root_squares,
    )


def solution(mesh):
    three = P(BOTH, None, None)
    two = P(BOTH, None)
    one = P(BOTH)
    placed = (
        three, one, two, P("table"), one, two, two, one, one, two, one, one, one, two, one, two, one, one, one, three,
        three, two,
    )
    results = (
        three, two, three, two, two, one, one, two, one, one, one, two, one, two, one, one, one, three, P(),
    )
    return jax.shard_map(body, mesh=mesh, in_specs=placed, out_specs=results, check_vma=False)
```
